32 devices in a mesh: gx: 4 (over x, core), gy: 8 (over z, y).
Axes of the slice: x: 2, y: 2, z: 4, core: 2. Of those that a mesh axis runs over, the one named last changes fastest.
Arguments:
- text_in: bfloat16 [16384, 768], P(('gx', 'gy')), may hold values from -6 to 6
- layout_in: bfloat16 [16384, 192], P(('gx', 'gy')), may hold values from -6 to 6
- lengths: int32 [32], P(('gx', 'gy')), may hold values from 64 to 512, as said below
- dup_rows: int32 [16384], P(('gx', 'gy')), may hold values from 0 to 1, as said below
- text_attention: float32 [3072, 768], P(('gx', 'gy')), may hold values from -3 to 3
- text_up: float32 [768, 3072], P(None, ('gx', 'gy')), may hold values from -0.21875 to 0.21875
- text_down: float32 [3072, 768], P(('gx', 'gy')), may hold values from -0.109375 to 0.109375
- text_vector: float32 [9216], P(('gx', 'gy')), may hold values from -2 to 2
- layout_attention: float32 [768, 192], P(('gx', 'gy')), may hold values from -3 to 3
- layout_up: float32 [192, 768], P(None, ('gx', 'gy')), may hold values from -0.4375 to 0.4375
- layout_down: float32 [768, 192], P(('gx', 'gy')), may hold values from -0.21875 to 0.21875
- layout_vector: float32 [2304], P(('gx', 'gy')), may hold values from -2 to 2
- text_cotangent: bfloat16 [16384, 768], P(('gx', 'gy')), may hold values from -6 to 6
- layout_cotangent: bfloat16 [16384, 192], P(('gx', 'gy')), may hold values from -6 to 6
Outputs:
- text_out: bfloat16 [16384, 768], P(('gx', 'gy'))
- layout_out: bfloat16 [16384, 192], P(('gx', 'gy'))
- text_in_grad: bfloat16 [16384, 768], P(('gx', 'gy'))
- layout_in_grad: bfloat16 [16384, 192], P(('gx', 'gy'))
- text_attention_grad: float32 [3072, 768], P(('gx', 'gy'))
- text_up_grad: float32 [768, 3072], P(None, ('gx', 'gy'))
- text_down_grad: float32 [3072, 768], P(('gx', 'gy'))
- text_vector_grad: float32 [9216], P(('gx', 'gy'))
- layout_attention_grad: float32 [768, 192], P(('gx', 'gy'))
- layout_up_grad: float32 [192, 768], P(None, ('gx', 'gy'))
- layout_down_grad: float32 [768, 192], P(('gx', 'gy'))
- layout_vector_grad: float32 [2304], P(('gx', 'gy'))
The draws below stay inside these ranges and needn't reach their ends.
Inputs may be any that keep to these rules, and one draw needn't show every extreme that they name: `lengths`: each stretch has at least 64 live tokens; some stretch is full. `dup_rows`: within a stretch the ones form a prefix of at most 128 rows.
All inputs are finite; a program needn't handle non-finite values.
Results may differ from the reference program's by a relative error of at most 0.013.
The reference program's roundings to bfloat16 on the way count: a program that leaves them out, or rounds other values in their place, can miss the bound.
Values may be sent and summed in bfloat16 or wider, within the bound.
No kernel may reach another device: no remote copies, remote signals or barrier semaphores. Data moves between devices by JAX's collectives and lax.ppermute only.
A program may use at most 256 MiB of HBM per device.

```python
import math
import jax
import jax.numpy as jnp
from jax import lax

D = 768
FF = 3072
DL = 192
FFL = 768
HEADS = 12
HD = 64
HDL = 16
STRETCH = 512
MINLEN = 64
INTERSECTION = 128
SLOTS = 32
TOKENS = 16384


def attention_stack(key, width):
    total = 4 * width
    base = jax.random.truncated_normal(key, -3.0, 3.0, (total, width), jnp.float32)
    block = jnp.arange(total) // width
    factor = jnp.where(block == 3, 6.0, 1.0).astype(jnp.float32)
    return base * factor[:, None] / math.sqrt(width)


def vector_draw(key, width, hidden):
    total = 8 * width + hidden
    base = jax.random.truncated_normal(key, -4.0, 4.0, (total,), jnp.float32)
    block = jnp.arange(total) // width
    is_gain = (block == 3) | (block == 6)
    return jnp.where(is_gain, 1.0 + 0.15 * base, 0.3 * base)


def draw_text_attention(key, part):
    return attention_stack(jax.random.fold_in(key, 11), D)


def draw_layout_attention(key, part):
    return attention_stack(jax.random.fold_in(key, 12), DL)


def draw_text_vector(key, part):
    return vector_draw(jax.random.fold_in(key, 13), D, FF)


def draw_layout_vector(key, part):
    return vector_draw(jax.random.fold_in(key, 14), DL, FFL)


def draw_lengths(key, part):
    first = jax.random.fold_in(key, 21)
    second = jax.random.fold_in(key, 22)
    values = jax.random.randint(first, (SLOTS,), MINLEN, STRETCH + 1)
    chosen = jax.random.randint(second, (), 0, SLOTS)
    return values.at[chosen].set(STRETCH).astype(jnp.int32)


def draw_dup_rows(key, part):
    first = jax.random.fold_in(key, 31)
    second = jax.random.fold_in(key, 32)
    counts = jax.random.randint(first, (SLOTS,), 0, INTERSECTION + 1)
    chosen = jax.random.randint(second, (), 0, SLOTS)
    counts = counts.at[chosen].set(INTERSECTION)
    flags = jnp.arange(STRETCH)[None, :] < counts[:, None]
    return flags.reshape(TOKENS).astype(jnp.int32)


def block_scale(own_key, dims, split, least, high):
    loudness, own = 1.0, jax.random.fold_in(own_key, 6)
    for axis_at, blocks in split:
        steps = jnp.exp(jax.random.uniform(jax.random.fold_in(own, axis_at), (blocks,), jnp.float32, least / len(split), high / len(split)))
        loudness = loudness * jnp.repeat(steps, dims[axis_at] // blocks).reshape([-1 if axis == axis_at else 1 for axis in range(len(dims))])
    return loudness


def centred(key, shape, scale, bound, cuts=(), kind=jnp.bfloat16):
    factor_of = block_scale(key, shape, cuts, -0.22, 0.18) if cuts else 1.0
    entries = jax.random.normal(key, shape, jnp.float32) * scale * factor_of
    return jnp.minimum(jnp.maximum(entries, -bound), bound).astype(kind)


def setup_inputs(seed: int = 0) -> dict:
    key_of = jax.random.split(jax.random.key(seed), 15)
    text_in = centred(key_of[0], (TOKENS, D), 1.0, 6.0, ((0, 32),))
    layout_in = centred(key_of[1], (TOKENS, DL), 1.0, 6.0, ((0, 32),))
    lengths = draw_lengths(jax.random.fold_in(key_of[14], 71), 0)
    dup_rows = draw_dup_rows(jax.random.fold_in(key_of[14], 71), 0)
    text_attention = draw_text_attention(jax.random.fold_in(key_of[14], 71), 0)
    text_up = centred(key_of[5], (D, FF), D ** -0.5, 0.21875, ((1, 32),), jnp.float32)
    text_down = centred(key_of[6], (FF, D), FF ** -0.5, 0.109375, ((0, 32),), jnp.float32)
    text_vector = draw_text_vector(jax.random.fold_in(key_of[14], 71), 0)
    layout_attention = draw_layout_attention(jax.random.fold_in(key_of[14], 71), 0)
    layout_up = centred(key_of[9], (DL, FFL), DL ** -0.5, 0.4375, ((1, 32),), jnp.float32)
    layout_down = centred(key_of[10], (FFL, DL), FFL ** -0.5, 0.21875, ((0, 32),), jnp.float32)
    layout_vector = draw_layout_vector(jax.random.fold_in(key_of[14], 71), 0)
    text_cotangent = centred(key_of[12], (TOKENS, D), 1.0, 6.0, ((0, 32),))
    layout_cotangent = centred(key_of[13], (TOKENS, DL), 1.0, 6.0, ((0, 32),))
    return {"text_in": text_in, "layout_in": layout_in, "lengths": lengths, "dup_rows": dup_rows, "text_attention": text_attention, "text_up": text_up, "text_down": text_down, "text_vector": text_vector, "layout_attention": layout_attention, "layout_up": layout_up, "layout_down": layout_down, "layout_vector": layout_vector, "text_cotangent": text_cotangent, "layout_cotangent": layout_cotangent}


EPS = 1e-05
NEG = -1e+30
HIGHEST = lax.Precision.HIGHEST

@jax.custom_vjp
def low(v):
    return lax.optimization_barrier(v.astype(jnp.bfloat16)).astype(jnp.float32)

@jax.custom_vjp
def low_back(v):
    return v

def low_keep(v):
    return (low(v), None)

def low_pass(kept, grad):
    return (grad,)

def back_keep(v):
    return (v, None)

def back_low(kept, grad):
    return (low(grad),)
low.defvjp(low_keep, low_pass)
low_back.defvjp(back_keep, back_low)

def matmul(inputs, weight):
    return jnp.einsum('bsd,de->bse', inputs, weight, precision=HIGHEST)

def normalize(resid, gain, shift):
    center = resid - lax.optimization_barrier(jnp.mean(resid, -1, keepdims=True))
    varian = lax.optimization_barrier(jnp.mean(center * center, -1, keepdims=True))
    return center * lax.rsqrt(varian + EPS) * gain + shift

def vector_parts(vector, width):
    return [vector[index * width:(index + 1) * width] for index in range(8)] + [vector[8 * width:]]

def stream_open(inputs, attention_w, vector, width):
    parts = vector_parts(vector, width)
    query = low(low_back(matmul(inputs, attention_w[:width]) + parts[0]))
    keys = low(low_back(matmul(inputs, attention_w[width:2 * width])))
    values = low(low_back(matmul(inputs, attention_w[2 * width:3 * width]) + parts[1]))
    return (query, keys, values)

def stream_close(inputs, attended, attention_w, up_w, down_w, vector, width):
    parts = vector_parts(vector, width)
    after = low_back(matmul(attended, attention_w[3 * width:]) + parts[2])
    first = normalize(inputs + after, parts[3], parts[4])
    upper = low_back(matmul(low(first), up_w) + parts[8])
    hidden_act = low(jax.nn.gelu(upper, approximate=False))
    branch = low_back(matmul(hidden_act, down_w) + parts[5])
    return normalize(first + branch, parts[6], parts[7])

def split_heads(array):
    return array.reshape(array.shape[0], array.shape[1], HEADS, -1)

def head_product(query, keys):
    return jnp.einsum('bqhd,bkhd->bhqk', split_heads(query), split_heads(keys), precision=HIGHEST)

def branch_probs(text_part, layout_part, visible):
    scores = low_back(text_part * (1.0 / math.sqrt(HD)) + layout_part * (1.0 / math.sqrt(HDL)))
    scores = jnp.where(visible[:, None, None, :], scores, NEG)
    return low(jax.nn.softmax(scores, axis=-1))

def group_layer(weights, fixed, pieces):
    text_x, layout_x, lens, text_fixed = pieces
    t_attention, t_up, t_down, t_vector, l_attention, l_up, l_down, l_vector = weights
    fixed_attention, fixed_vector = fixed
    text_query, text_keys, text_values = stream_open(text_x, t_attention, t_vector, D)
    layout_query, layout_keys, layout_values = stream_open(layout_x, l_attention, l_vector, DL)
    fixed_query, fixed_keys, unused = stream_open(text_fixed, fixed_attention, fixed_vector, D)
    batch = text_x.shape[0]
    rows = text_x.shape[1]
    visible = jnp.arange(rows)[None, :] < lens[:, None]
    text_part = head_product(text_query, text_keys)
    layout_part = head_product(layout_query, layout_keys)
    fixed_part = head_product(fixed_query, fixed_keys)
    text_probs = branch_probs(text_part, layout_part, visible)
    layout_probs = branch_probs(fixed_part, layout_part, visible)
    text_att = jnp.einsum('bhqk,bkhd->bqhd', text_probs, split_heads(text_values), precision=HIGHEST)
    layout_att = jnp.einsum('bhqk,bkhd->bqhd', layout_probs, split_heads(layout_values), precision=HIGHEST)
    text_att = low(low_back(text_att.reshape(batch, rows, D)))
    layout_att = low(low_back(layout_att.reshape(batch, rows, DL)))
    text_final = stream_close(text_x, text_att, t_attention, t_up, t_down, t_vector, D)
    layout_final = stream_close(layout_x, layout_att, l_attention, l_up, l_down, l_vector, DL)
    return (text_final, layout_final)

def reference(text_in, layout_in, lengths, dup_rows, text_attention, text_up, text_down, text_vector, layout_attention, layout_up, layout_down, layout_vector, text_cotangent, layout_cotangent):
    group = math.gcd(SLOTS, 8)
    count = SLOTS // group
    length_groups = lengths.reshape(count, group)
    text_fixed = text_in.astype(jnp.float32).reshape(count, group, STRETCH, D)
    fixed = (low(text_attention), low(text_vector))

    def forward(weights, text_x, layout_x):
        lowered = tuple((low(weight) for weight in weights))
        text_groups = text_x.reshape(count, group, STRETCH, D)
        layout_groups = layout_x.reshape(count, group, STRETCH, DL)
        results = lax.map(lambda pieces: jax.checkpoint(group_layer)(lowered, fixed, pieces), (text_groups, layout_groups, length_groups, text_fixed))
        return (results[0].reshape(TOKENS, D), results[1].reshape(TOKENS, DL))
    weights = (text_attention, text_up, text_down, text_vector, layout_attention, layout_up, layout_down, layout_vector)
    outputs, pull = jax.vjp(forward, weights, text_in.astype(jnp.float32), layout_in.astype(jnp.float32))
    position = jnp.arange(STRETCH)
    keep = (position[None, :] < lengths[:, None]) & (dup_rows.reshape(SLOTS, STRETCH) == 0)
    keep = keep.reshape(TOKENS, 1).astype(jnp.float32)
    weight_grads, text_grad, layout_grad = pull((text_cotangent.astype(jnp.float32) * keep, layout_cotangent.astype(jnp.float32) * keep))
    return (outputs[0].astype(jnp.bfloat16), outputs[1].astype(jnp.bfloat16), text_grad.astype(jnp.bfloat16), layout_grad.astype(jnp.bfloat16), weight_grads[0], weight_grads[1], weight_grads[2], weight_grads[3], weight_grads[4], weight_grads[5], weight_grads[6], weight_grads[7])
```

```python
import functools
import math

import jax
import jax.numpy as jnp
from jax import lax
from jax.sharding import PartitionSpec as P


AXES = ("gx", "gy")


def exchange_dims(shape):
    gx, gy = shape["gx"], shape["gy"]
    outer = {8: 4, 32: 4}.get(gy, gy)
    inner = gy // outer
    core = 2 if gx % 2 == 0 else 1
    core_dim = (gy, core)
    x_dim = (gy * core, gx // core)
    if inner <= outer:
        z_dim, y_dim = (inner, outer), (1, inner)
    else:
        z_dim, y_dim = (1, inner), (inner, outer)
    return x_dim, core_dim, z_dim, y_dim


def orders(shape):
    x_dim, core_dim, z_dim, y_dim = exchange_dims(shape)
    return ((z_dim, y_dim, x_dim, core_dim), (z_dim, x_dim, y_dim, core_dim))


def offsets(order):
    table = [0]
    for stride, size in order:
        table = [offset ^ (stride * step) for step in range(size) for offset in table]
    return table


def swap(array, offset, count):
    return lax.ppermute(array, AXES, [(device, device ^ offset) for device in range(count)])


def gather_part(part, order, count):
    held = part[None]
    for stride, size in order:
        pieces = [held] + [swap(held, stride * step, count) for step in range(1, size)]
        held = jnp.concatenate(pieces, 0)
    return held


def scatter_part(parts, order, count):
    held = parts
    for stride, size in reversed(order):
        held = held.reshape((size, held.shape[0] // size) + held.shape[1:])
        total = held[0].astype(jnp.float32)
        for step in range(1, size):
            total = total + swap(held[step], stride * step, count).astype(jnp.float32)
        last = (stride, size) == order[0]
        held = total if last else total.astype(jnp.bfloat16)
    return held[0]


def flat_index(gy):
    return lax.axis_index("gx") * gy + lax.axis_index("gy")


def positions(order, count):
    table = offsets(order)
    inverse = [0] * count
    for position, offset in enumerate(table):
        inverse[offset] = position
    return jnp.array(table, jnp.int32), jnp.array(inverse, jnp.int32)


def gather_rows(shard, shape, me):
    count = shape["gx"] * shape["gy"]
    half = shard.shape[0] // 2
    pieces = []
    for index, order in enumerate(orders(shape)):
        held = gather_part(shard[index * half : (index + 1) * half], order, count)
        inverse = positions(order, count)[1]
        pieces.append(jnp.take(held, inverse[jnp.arange(count) ^ me], axis=0))
    return jnp.concatenate(pieces, 1)


def scatter_rows(grads, shape, me):
    count = shape["gx"] * shape["gy"]
    half = grads.shape[1] // 2
    pieces = []
    for index, order in enumerate(orders(shape)):
        table = positions(order, count)[0]
        parts = jnp.take(grads[:, index * half : (index + 1) * half], me ^ table, axis=0)
        pieces.append(scatter_part(parts, order, count))
    return jnp.concatenate(pieces, 0)


def pad_cols(array, width):
    return jnp.pad(array, ((0, 0),) * (array.ndim - 1) + ((0, width - array.shape[-1]),))


def pack_rows(text_rows, layout_rows, vectors):
    side = D // 3
    layouts = jnp.concatenate([pad_cols(rows, side) for rows in layout_rows], -1)
    packed = jnp.concatenate([text_rows, layouts, pad_cols(vectors, D)[..., None, :]], -2)
    rows = packed.shape[-2]
    extra = -rows % 16
    return jnp.pad(packed, ((0, 0),) * (packed.ndim - 2) + ((0, extra), (0, 0)))


def unpack_rows(packed, text_rows, layout_rows, text_vec, layout_vec):
    side = D // 3
    text = packed[..., :text_rows, :]
    block = packed[..., text_rows : text_rows + layout_rows, :]
    layouts = [block[..., side * index : side * index + DL] for index in range(3)]
    vectors = packed[..., text_rows + layout_rows, :]
    return text, layouts, vectors[..., :text_vec], vectors[..., text_vec : text_vec + layout_vec]

D = 768
DL = 192
HEADS = 12


EPS = 1e-05
NEG = -1e30


def matmul(left, right):
    return jnp.dot(left, right, preferred_element_type=jnp.float32)


def contract_rows(left, right):
    return lax.dot_general(
        left, right, (((0,), (0,)), ((), ())), preferred_element_type=jnp.float32
    )


def contract_cols(left, right):
    return lax.dot_general(
        left, right, (((1,), (1,)), ((), ())), preferred_element_type=jnp.float32
    )


def vector_parts(vector, width):
    values = vector.astype(jnp.float32)
    return [values[index * width : (index + 1) * width] for index in range(8)] + [
        values[8 * width :]
    ]


def normalize(resid, gain, shift):
    center = resid - jnp.mean(resid, -1, keepdims=True)
    varian = jnp.mean(center * center, -1, keepdims=True)
    inverse = lax.rsqrt(varian + EPS)
    scaled = center * inverse
    return (scaled * gain + shift, scaled, inverse)


def norm_back(grad, scaled, inverse, gain):
    weighted = grad * gain
    inner = jnp.mean(weighted, -1, keepdims=True)
    across = jnp.mean(weighted * scaled, -1, keepdims=True)
    return inverse * (weighted - inner - scaled * across)


def exact_gelu(value):
    return jax.nn.gelu(value, approximate=False)


def open_stream(inputs, weights, width):
    parts = vector_parts(weights[3], width)
    stacked = weights[0][: 3 * width].reshape(3, width, width)
    projected = jnp.einsum("nd,jde->jne", inputs, stacked, preferred_element_type=jnp.float32)
    query = (projected[0] + parts[0]).astype(jnp.bfloat16)
    keys = projected[1].astype(jnp.bfloat16)
    values = (projected[2] + parts[1]).astype(jnp.bfloat16)
    return (query, keys, values)


def heads_view(array):
    return array.reshape(array.shape[0], HEADS, array.shape[1] // HEADS)


def head_scale(array):
    return 1.0 / math.sqrt(array.shape[1] // HEADS)


def joint_scores(text_query, text_keys, layout_query, layout_keys, length):
    rows = text_query.shape[0]
    text_part = jnp.einsum(
        "qhd,khd->hqk",
        heads_view(text_query),
        heads_view(text_keys),
        preferred_element_type=jnp.float32,
    )
    layout_part = jnp.einsum(
        "qhd,khd->hqk",
        heads_view(layout_query),
        heads_view(layout_keys),
        preferred_element_type=jnp.float32,
    )
    scores = text_part * head_scale(text_query) + layout_part * head_scale(layout_query)
    visible = jnp.arange(rows) < length
    return jnp.where(visible[None, None, :], scores, NEG)


def weigh_values(probs, values):
    mixed = jnp.einsum(
        "hqk,khd->qhd", probs, heads_view(values), preferred_element_type=jnp.float32
    )
    return mixed.reshape(values.shape[0], values.shape[1])


def attend_forward(pieces):
    text_query, text_keys, text_values, layout_query, layout_keys, layout_values, length = pieces
    scores = joint_scores(text_query, text_keys, layout_query, layout_keys, length)
    top = jnp.max(scores, -1, keepdims=True)
    expo = jnp.exp(scores - top)
    total = jnp.sum(expo, -1, keepdims=True)
    probs = (expo / total).astype(jnp.bfloat16)
    text_att = weigh_values(probs, text_values).astype(jnp.bfloat16)
    layout_att = weigh_values(probs, layout_values).astype(jnp.bfloat16)
    return (text_att, layout_att, (top + jnp.log(total))[:, :, 0])


def values_grad(probs_low, grad_out):
    moved = jnp.einsum(
        "hqk,qhd->khd", probs_low, heads_view(grad_out), preferred_element_type=jnp.float32
    )
    return moved.reshape(grad_out.shape[0], grad_out.shape[1]).astype(jnp.bfloat16)


def query_keys_grad(score_grads, query, keys):
    scale = head_scale(query)
    rows, width = query.shape
    query_grad = jnp.zeros((rows, HEADS, width // HEADS), jnp.float32)
    keys_grad = jnp.zeros((rows, HEADS, width // HEADS), jnp.float32)
    for score_grad in score_grads:
        query_grad = query_grad + jnp.einsum(
            "hqk,khd->qhd", score_grad, heads_view(keys), preferred_element_type=jnp.float32
        )
        keys_grad = keys_grad + jnp.einsum(
            "hqk,qhd->khd", score_grad, heads_view(query), preferred_element_type=jnp.float32
        )
    query_grad = query_grad * scale
    keys_grad = keys_grad * scale
    return (
        query_grad.reshape(rows, width).astype(jnp.bfloat16),
        keys_grad.reshape(rows, width).astype(jnp.bfloat16),
    )


def softmax_back(probs, mixed):
    return (probs * (mixed - jnp.sum(probs * mixed, -1, keepdims=True))).astype(jnp.bfloat16)


def attend_backward(pieces):
    (
        text_query,
        text_keys,
        text_values,
        layout_query,
        layout_keys,
        layout_values,
        length,
        log_total,
        text_grad,
        layout_grad,
    ) = pieces
    scores = joint_scores(text_query, text_keys, layout_query, layout_keys, length)
    probs = jnp.exp(scores - log_total[:, :, None])
    probs_low = probs.astype(jnp.bfloat16)
    text_values_grad = values_grad(probs_low, text_grad)
    layout_values_grad = values_grad(probs_low, layout_grad)
    text_mixed = jnp.einsum(
        "qhd,khd->hqk",
        heads_view(text_grad),
        heads_view(text_values),
        preferred_element_type=jnp.float32,
    )
    layout_mixed = jnp.einsum(
        "qhd,khd->hqk",
        heads_view(layout_grad),
        heads_view(layout_values),
        preferred_element_type=jnp.float32,
    )
    text_score_grad = softmax_back(probs, text_mixed)
    layout_score_grad = softmax_back(probs, layout_mixed)
    text_query_grad, text_keys_grad = query_keys_grad((text_score_grad,), text_query, text_keys)
    layout_query_grad, layout_keys_grad = query_keys_grad(
        (text_score_grad, layout_score_grad), layout_query, layout_keys
    )
    return (
        text_query_grad,
        text_keys_grad,
        text_values_grad,
        layout_query_grad,
        layout_keys_grad,
        layout_values_grad,
    )


def close_stream(inputs, attended, weights, width):
    attention_w, up_w, down_w, vector = weights
    parts = vector_parts(vector, width)
    after = matmul(attended, attention_w[3 * width :]) + parts[2]
    first, scaled_one, inverse_one = normalize(
        inputs.astype(jnp.float32) + after, parts[3], parts[4]
    )
    first_low = first.astype(jnp.bfloat16)
    upper = contract_cols(first_low, up_w) + parts[8]
    hidden_act = exact_gelu(upper).astype(jnp.bfloat16)
    final, scaled_two, inverse_two = normalize(
        first + matmul(hidden_act, down_w) + parts[5], parts[6], parts[7]
    )
    return (final, (scaled_one, inverse_one, first_low, upper, hidden_act, scaled_two, inverse_two))


def close_back(cotan, attended, saved, weights, width):
    scaled_one, inverse_one, first_low, upper, hidden_act, scaled_two, inverse_two = saved
    attention_w, up_w, down_w, vector = weights
    parts = vector_parts(vector, width)
    gain_two_grad = jnp.sum(cotan * scaled_two, 0)
    shift_two_grad = jnp.sum(cotan, 0)
    second_grad = norm_back(cotan, scaled_two, inverse_two, parts[6])
    branch_low = second_grad.astype(jnp.bfloat16)
    down_grad = contract_rows(hidden_act, branch_low)
    bias_down_grad = jnp.sum(branch_low.astype(jnp.float32), 0)
    act_grad = contract_cols(branch_low, down_w)
    gelu_back = jax.vjp(exact_gelu, upper)[1]
    upper_low = gelu_back(act_grad)[0].astype(jnp.bfloat16)
    up_grad_flipped = contract_rows(upper_low, first_low)
    bias_up_grad = jnp.sum(upper_low.astype(jnp.float32), 0)
    first_grad = second_grad + matmul(upper_low, up_w)
    gain_one_grad = jnp.sum(first_grad * scaled_one, 0)
    shift_one_grad = jnp.sum(first_grad, 0)
    resid_grad = norm_back(first_grad, scaled_one, inverse_one, parts[3])
    after_low = resid_grad.astype(jnp.bfloat16)
    out_weight_grad = contract_rows(attended, after_low)
    bias_out_grad = jnp.sum(after_low.astype(jnp.float32), 0)
    attended_grad = contract_cols(after_low, attention_w[3 * width :]).astype(jnp.bfloat16)
    tail = (
        bias_out_grad,
        gain_one_grad,
        shift_one_grad,
        bias_down_grad,
        gain_two_grad,
        shift_two_grad,
        bias_up_grad,
    )
    return (resid_grad, attended_grad, out_weight_grad, tail, up_grad_flipped, down_grad)


def open_back(
    inputs,
    resid_grad,
    query_grad,
    keys_grad,
    values_grad,
    out_weight_grad,
    tail,
    attention_w,
    width,
):
    stacked_grad = jnp.stack([query_grad, keys_grad, values_grad])
    weight_grad = jnp.einsum(
        "nd,jne->jde", inputs, stacked_grad, preferred_element_type=jnp.float32
    ).reshape(3 * width, width)
    input_grad = resid_grad + jnp.einsum(
        "jne,jde->nd",
        stacked_grad,
        attention_w[: 3 * width].reshape(3, width, width),
        preferred_element_type=jnp.float32,
    )
    bias_query_grad = jnp.sum(query_grad.astype(jnp.float32), 0)
    bias_value_grad = jnp.sum(values_grad.astype(jnp.float32), 0)
    (
        bias_out_grad,
        gain_one_grad,
        shift_one_grad,
        bias_down_grad,
        gain_two_grad,
        shift_two_grad,
        bias_up_grad,
    ) = tail
    vector_grad = jnp.concatenate(
        [
            bias_query_grad,
            bias_value_grad,
            bias_out_grad,
            gain_one_grad,
            shift_one_grad,
            bias_down_grad,
            gain_two_grad,
            shift_two_grad,
            bias_up_grad,
        ]
    )
    attention_grad = jnp.concatenate([weight_grad, out_weight_grad], 0)
    return (input_grad, attention_grad, vector_grad)


def by_stretch(array, stretches):
    return array.reshape((stretches, array.shape[0] // stretches) + array.shape[1:])


def shards(
    MESH_SHAPE,
    text_in,
    layout_in,
    lengths,
    dup_rows,
    text_attention,
    text_up,
    text_down,
    text_vector,
    layout_attention,
    layout_up,
    layout_down,
    layout_vector,
    text_cotangent,
    layout_cotangent,
):
    shape = MESH_SHAPE
    count = shape["gx"] * shape["gy"]
    me = flat_index(shape["gy"])
    text_rows, layout_rows = text_attention.shape[0], layout_attention.shape[0]
    text_vec, layout_vec = text_vector.shape[0], layout_vector.shape[0]
    packed = pack_rows(
        text_attention,
        [layout_attention, layout_up.T, layout_down],
        jnp.concatenate([text_vector, layout_vector]),
    ).astype(jnp.bfloat16)
    gathered = gather_rows(packed, shape, me)
    up_all = gather_rows(text_up.T.astype(jnp.bfloat16), shape, me).reshape(-1, D)
    down_all = gather_rows(text_down.astype(jnp.bfloat16), shape, me).reshape(-1, D)
    text_all, layouts_all, text_vec_all, layout_vec_all = unpack_rows(
        gathered, text_rows, layout_rows, text_vec, layout_vec
    )
    text_weights = (text_all.reshape(-1, D), up_all, down_all, text_vec_all.reshape(-1))
    layout_weights = tuple(rows.reshape(-1, DL) for rows in layouts_all) + (
        layout_vec_all.reshape(-1),
    )
    stretches = lengths.shape[0]
    text_query, text_keys, text_values = open_stream(text_in, text_weights, D)
    layout_query, layout_keys, layout_values = open_stream(layout_in, layout_weights, DL)
    opened = (text_query, text_keys, text_values, layout_query, layout_keys, layout_values)
    opened_stretches = tuple((by_stretch(array, stretches) for array in opened))
    text_att, layout_att, log_total = lax.map(attend_forward, opened_stretches + (lengths,))
    text_att = text_att.reshape(-1, D)
    layout_att = layout_att.reshape(-1, DL)
    text_final, text_saved = close_stream(text_in, text_att, text_weights, D)
    layout_final, layout_saved = close_stream(layout_in, layout_att, layout_weights, DL)
    text_back, layout_back = text_weights, layout_weights
    span = text_in.shape[0] // stretches
    position = jnp.arange(span)
    keep = (position[None, :] < lengths[:, None]) & (dup_rows.reshape(stretches, span) == 0)
    keep = keep.reshape(-1, 1).astype(jnp.float32)
    text_cot = text_cotangent.astype(jnp.float32) * keep
    layout_cot = layout_cotangent.astype(jnp.float32) * keep
    text_resid, text_att_grad, text_out_w, text_tail, text_up_flipped, text_down_grad = close_back(
        text_cot, text_att, text_saved, text_back, D
    )
    (
        layout_resid,
        layout_att_grad,
        layout_out_w,
        layout_tail,
        layout_up_flipped,
        layout_down_grad,
    ) = close_back(layout_cot, layout_att, layout_saved, layout_back, DL)
    back_pieces = opened_stretches + (
        lengths,
        log_total,
        by_stretch(text_att_grad, stretches),
        by_stretch(layout_att_grad, stretches),
    )
    grads = lax.map(attend_backward, back_pieces)
    (
        text_query_grad,
        text_keys_grad,
        text_values_grad,
        layout_query_grad,
        layout_keys_grad,
        layout_values_grad,
    ) = tuple((array.reshape(-1, array.shape[-1]) for array in grads))
    text_input_grad, text_attention_grad, text_vector_grad = open_back(
        text_in,
        text_resid,
        text_query_grad,
        text_keys_grad,
        text_values_grad,
        text_out_w,
        text_tail,
        text_back[0],
        D,
    )
    layout_input_grad, layout_attention_grad, layout_vector_grad = open_back(
        layout_in,
        layout_resid,
        layout_query_grad,
        layout_keys_grad,
        layout_values_grad,
        layout_out_w,
        layout_tail,
        layout_back[0],
        DL,
    )
    def by_owner(array):
        return array.reshape((count, array.shape[0] // count) + array.shape[1:])

    attention_sum = scatter_rows(
        pack_rows(
            by_owner(text_attention_grad),
            [by_owner(g) for g in (layout_attention_grad, layout_up_flipped, layout_down_grad)],
            jnp.concatenate([by_owner(text_vector_grad), by_owner(layout_vector_grad)], -1),
        ).astype(jnp.bfloat16),
        shape,
        me,
    )
    up_sum = scatter_rows(by_owner(text_up_flipped).astype(jnp.bfloat16), shape, me)
    down_sum = scatter_rows(by_owner(text_down_grad).astype(jnp.bfloat16), shape, me)
    text_attention_sum, layout_sums, text_vec_sum, layout_vec_sum = unpack_rows(
        attention_sum, text_rows, layout_rows, text_vec, layout_vec
    )
    return (
        text_final.astype(jnp.bfloat16),
        layout_final.astype(jnp.bfloat16),
        text_input_grad.astype(jnp.bfloat16),
        layout_input_grad.astype(jnp.bfloat16),
        text_attention_sum,
        up_sum.T,
        down_sum,
        text_vec_sum,
        layout_sums[0],
        layout_sums[1].T,
        layout_sums[2],
        layout_vec_sum,
    )


def solution(mesh):
    placed = (
        P(("gx", "gy"), None),
        P(("gx", "gy"), None),
        P(("gx", "gy")),
        P(("gx", "gy")),
        P(("gx", "gy"), None),
        P(None, ("gx", "gy")),
        P(("gx", "gy"), None),
        P(("gx", "gy")),
        P(("gx", "gy"), None),
        P(None, ("gx", "gy")),
        P(("gx", "gy"), None),
        P(("gx", "gy")),
        P(("gx", "gy"), None),
        P(("gx", "gy"), None),
    )
    return jax.shard_map(
        functools.partial(shards, dict(mesh.shape)),
        mesh=mesh,
        in_specs=placed,
        out_specs=(
            P(("gx", "gy"), None),
            P(("gx", "gy"), None),
            P(("gx", "gy"), None),
            P(("gx", "gy"), None),
            P(("gx", "gy"), None),
            P(None, ("gx", "gy")),
            P(("gx", "gy"), None),
            P(("gx", "gy")),
            P(("gx", "gy"), None),
            P(None, ("gx", "gy")),
            P(("gx", "gy"), None),
            P(("gx", "gy")),
        ),
        check_vma=False,
    )
```

```python
import functools
import math

import jax
import jax.numpy as jnp
from jax import lax
from jax.experimental import pallas as pl
from jax.experimental.pallas import tpu as pltpu
from jax.sharding import PartitionSpec as P


AXES = ("gx", "gy")


def exchange_dims(shape):
    gx, gy = shape["gx"], shape["gy"]
    outer = {8: 4, 32: 4}.get(gy, gy)
    inner = gy // outer
    core = 2 if gx % 2 == 0 else 1
    core_dim = (gy, core)
    x_dim = (gy * core, gx // core)
    if inner <= outer:
        z_dim, y_dim = (inner, outer), (1, inner)
    else:
        z_dim, y_dim = (1, inner), (inner, outer)
    return x_dim, core_dim, z_dim, y_dim


def orders(shape):
    x_dim, core_dim, z_dim, y_dim = exchange_dims(shape)
    return ((z_dim, y_dim, x_dim, core_dim), (z_dim, x_dim, y_dim, core_dim))


def offsets(order):
    table = [0]
    for stride, size in order:
        table = [offset ^ (stride * step) for step in range(size) for offset in table]
    return table


def swap(array, offset, count):
    return lax.ppermute(array, AXES, [(device, device ^ offset) for device in range(count)])


def gather_part(part, order, count):
    held = part[None]
    for stride, size in order:
        pieces = [held] + [swap(held, stride * step, count) for step in range(1, size)]
        held = jnp.concatenate(pieces, 0)
    return held


def scatter_part(parts, order, count):
    held = parts
    for stride, size in reversed(order):
        held = held.reshape((size, held.shape[0] // size) + held.shape[1:])
        total = held[0].astype(jnp.float32)
        for step in range(1, size):
            total = total + swap(held[step], stride * step, count).astype(jnp.float32)
        last = (stride, size) == order[0]
        held = total if last else total.astype(jnp.bfloat16)
    return held[0]


def flat_index(gy):
    return lax.axis_index("gx") * gy + lax.axis_index("gy")


def positions(order, count):
    table = offsets(order)
    inverse = [0] * count
    for position, offset in enumerate(table):
        inverse[offset] = position
    return jnp.array(table, jnp.int32), jnp.array(inverse, jnp.int32)


def gather_rows(shard, shape, me):
    count = shape["gx"] * shape["gy"]
    half = shard.shape[0] // 2
    pieces = []
    for index, order in enumerate(orders(shape)):
        held = gather_part(shard[index * half : (index + 1) * half], order, count)
        inverse = positions(order, count)[1]
        pieces.append(jnp.take(held, inverse[jnp.arange(count) ^ me], axis=0))
    return jnp.concatenate(pieces, 1)


def scatter_rows(grads, shape, me):
    count = shape["gx"] * shape["gy"]
    half = grads.shape[1] // 2
    pieces = []
    for index, order in enumerate(orders(shape)):
        table = positions(order, count)[0]
        parts = jnp.take(grads[:, index * half : (index + 1) * half], me ^ table, axis=0)
        pieces.append(scatter_part(parts, order, count))
    return jnp.concatenate(pieces, 0)


def pad_cols(array, width):
    return jnp.pad(array, ((0, 0),) * (array.ndim - 1) + ((0, width - array.shape[-1]),))


def pack_rows(text_rows, layout_rows, vectors):
    side = D // 3
    layouts = jnp.concatenate([pad_cols(rows, side) for rows in layout_rows], -1)
    packed = jnp.concatenate([text_rows, layouts, pad_cols(vectors, D)[..., None, :]], -2)
    rows = packed.shape[-2]
    extra = -rows % 16
    return jnp.pad(packed, ((0, 0),) * (packed.ndim - 2) + ((0, extra), (0, 0)))


def unpack_rows(packed, text_rows, layout_rows, text_vec, layout_vec):
    side = D // 3
    text = packed[..., :text_rows, :]
    block = packed[..., text_rows : text_rows + layout_rows, :]
    layouts = [block[..., side * index : side * index + DL] for index in range(3)]
    vectors = packed[..., text_rows + layout_rows, :]
    return text, layouts, vectors[..., :text_vec], vectors[..., text_vec : text_vec + layout_vec]

D = 768
DL = 192
HEADS = 12
FF = 4 * D
FFL = 4 * DL


EPS = 1e-05
NEG = -1e30


def matmul(left, right):
    return jnp.dot(left, right, preferred_element_type=jnp.float32)


def contract_rows(left, right):
    return lax.dot_general(
        left, right, (((0,), (0,)), ((), ())), preferred_element_type=jnp.float32
    )


def contract_cols(left, right):
    return lax.dot_general(
        left, right, (((1,), (1,)), ((), ())), preferred_element_type=jnp.float32
    )


def vector_parts(vector, width):
    values = vector.astype(jnp.float32)
    return [values[index * width : (index + 1) * width] for index in range(8)] + [
        values[8 * width :]
    ]


def normalize(resid, gain, shift):
    center = resid - jnp.mean(resid, -1, keepdims=True)
    varian = jnp.mean(center * center, -1, keepdims=True)
    inverse = lax.rsqrt(varian + EPS)
    scaled = center * inverse
    return (scaled * gain + shift, scaled, inverse)


def norm_back(grad, scaled, inverse, gain):
    weighted = grad * gain
    inner = jnp.mean(weighted, -1, keepdims=True)
    across = jnp.mean(weighted * scaled, -1, keepdims=True)
    return inverse * (weighted - inner - scaled * across)


def exact_gelu(value):
    return jax.nn.gelu(value, approximate=False)


def open_stream(inputs, weights, width):
    parts = vector_parts(weights[3], width)
    stacked = weights[0][: 3 * width].reshape(3, width, width)
    projected = jnp.einsum("nd,jde->jne", inputs, stacked, preferred_element_type=jnp.float32)
    query = (projected[0] + parts[0]).astype(jnp.bfloat16)
    keys = projected[1].astype(jnp.bfloat16)
    values = (projected[2] + parts[1]).astype(jnp.bfloat16)
    return (query, keys, values)


def heads_view(array):
    return array.reshape(array.shape[0], HEADS, array.shape[1] // HEADS)


def head_scale(array):
    return 1.0 / math.sqrt(array.shape[1] // HEADS)


def joint_scores(text_query, text_keys, layout_query, layout_keys, length):
    rows = text_query.shape[0]
    text_part = jnp.einsum(
        "qhd,khd->hqk",
        heads_view(text_query),
        heads_view(text_keys),
        preferred_element_type=jnp.float32,
    )
    layout_part = jnp.einsum(
        "qhd,khd->hqk",
        heads_view(layout_query),
        heads_view(layout_keys),
        preferred_element_type=jnp.float32,
    )
    scores = text_part * head_scale(text_query) + layout_part * head_scale(layout_query)
    visible = jnp.arange(rows) < length
    return jnp.where(visible[None, None, :], scores, NEG)


def weigh_values(probs, values):
    mixed = jnp.einsum(
        "hqk,khd->qhd", probs, heads_view(values), preferred_element_type=jnp.float32
    )
    return mixed.reshape(values.shape[0], values.shape[1])


def attend_forward(pieces):
    text_query, text_keys, text_values, layout_query, layout_keys, layout_values, length = pieces
    scores = joint_scores(text_query, text_keys, layout_query, layout_keys, length)
    top = jnp.max(scores, -1, keepdims=True)
    expo = jnp.exp(scores - top)
    total = jnp.sum(expo, -1, keepdims=True)
    probs = (expo / total).astype(jnp.bfloat16)
    text_att = weigh_values(probs, text_values).astype(jnp.bfloat16)
    layout_att = weigh_values(probs, layout_values).astype(jnp.bfloat16)
    return (text_att, layout_att, (top + jnp.log(total))[:, :, 0])


def values_grad(probs_low, grad_out):
    moved = jnp.einsum(
        "hqk,qhd->khd", probs_low, heads_view(grad_out), preferred_element_type=jnp.float32
    )
    return moved.reshape(grad_out.shape[0], grad_out.shape[1]).astype(jnp.bfloat16)


def query_keys_grad(score_grads, query, keys):
    scale = head_scale(query)
    rows, width = query.shape
    query_grad = jnp.zeros((rows, HEADS, width // HEADS), jnp.float32)
    keys_grad = jnp.zeros((rows, HEADS, width // HEADS), jnp.float32)
    for score_grad in score_grads:
        query_grad = query_grad + jnp.einsum(
            "hqk,khd->qhd", score_grad, heads_view(keys), preferred_element_type=jnp.float32
        )
        keys_grad = keys_grad + jnp.einsum(
            "hqk,qhd->khd", score_grad, heads_view(query), preferred_element_type=jnp.float32
        )
    query_grad = query_grad * scale
    keys_grad = keys_grad * scale
    return (
        query_grad.reshape(rows, width).astype(jnp.bfloat16),
        keys_grad.reshape(rows, width).astype(jnp.bfloat16),
    )


def softmax_back(probs, mixed):
    return (probs * (mixed - jnp.sum(probs * mixed, -1, keepdims=True))).astype(jnp.bfloat16)


def attend_backward(pieces):
    (
        text_query,
        text_keys,
        text_values,
        layout_query,
        layout_keys,
        layout_values,
        length,
        log_total,
        text_grad,
        layout_grad,
    ) = pieces
    scores = joint_scores(text_query, text_keys, layout_query, layout_keys, length)
    probs = jnp.exp(scores - log_total[:, :, None])
    probs_low = probs.astype(jnp.bfloat16)
    text_values_grad = values_grad(probs_low, text_grad)
    layout_values_grad = values_grad(probs_low, layout_grad)
    text_mixed = jnp.einsum(
        "qhd,khd->hqk",
        heads_view(text_grad),
        heads_view(text_values),
        preferred_element_type=jnp.float32,
    )
    layout_mixed = jnp.einsum(
        "qhd,khd->hqk",
        heads_view(layout_grad),
        heads_view(layout_values),
        preferred_element_type=jnp.float32,
    )
    text_score_grad = softmax_back(probs, text_mixed)
    layout_score_grad = softmax_back(probs, layout_mixed)
    text_query_grad, text_keys_grad = query_keys_grad((text_score_grad,), text_query, text_keys)
    layout_query_grad, layout_keys_grad = query_keys_grad(
        (text_score_grad, layout_score_grad), layout_query, layout_keys
    )
    return (
        text_query_grad,
        text_keys_grad,
        text_values_grad,
        layout_query_grad,
        layout_keys_grad,
        layout_values_grad,
    )


def close_stream(inputs, attended, weights, width):
    attention_w, up_w, down_w, vector = weights
    parts = vector_parts(vector, width)
    after = matmul(attended, attention_w[3 * width :]) + parts[2]
    first, scaled_one, inverse_one = normalize(
        inputs.astype(jnp.float32) + after, parts[3], parts[4]
    )
    first_low = first.astype(jnp.bfloat16)
    upper = contract_cols(first_low, up_w) + parts[8]
    hidden_act = exact_gelu(upper).astype(jnp.bfloat16)
    final, scaled_two, inverse_two = normalize(
        first + matmul(hidden_act, down_w) + parts[5], parts[6], parts[7]
    )
    return (final, (scaled_one, inverse_one, first_low, upper, hidden_act, scaled_two, inverse_two))


def close_back(cotan, attended, saved, weights, width):
    scaled_one, inverse_one, first_low, upper, hidden_act, scaled_two, inverse_two = saved
    attention_w, up_w, down_w, vector = weights
    parts = vector_parts(vector, width)
    gain_two_grad = jnp.sum(cotan * scaled_two, 0)
    shift_two_grad = jnp.sum(cotan, 0)
    second_grad = norm_back(cotan, scaled_two, inverse_two, parts[6])
    branch_low = second_grad.astype(jnp.bfloat16)
    down_grad = contract_rows(hidden_act, branch_low)
    bias_down_grad = jnp.sum(branch_low.astype(jnp.float32), 0)
    act_grad = contract_cols(branch_low, down_w)
    gelu_back = jax.vjp(exact_gelu, upper)[1]
    upper_low = gelu_back(act_grad)[0].astype(jnp.bfloat16)
    up_grad_flipped = contract_rows(upper_low, first_low)
    bias_up_grad = jnp.sum(upper_low.astype(jnp.float32), 0)
    first_grad = second_grad + matmul(upper_low, up_w)
    gain_one_grad = jnp.sum(first_grad * scaled_one, 0)
    shift_one_grad = jnp.sum(first_grad, 0)
    resid_grad = norm_back(first_grad, scaled_one, inverse_one, parts[3])
    after_low = resid_grad.astype(jnp.bfloat16)
    out_weight_grad = contract_rows(attended, after_low)
    bias_out_grad = jnp.sum(after_low.astype(jnp.float32), 0)
    attended_grad = contract_cols(after_low, attention_w[3 * width :]).astype(jnp.bfloat16)
    tail = (
        bias_out_grad,
        gain_one_grad,
        shift_one_grad,
        bias_down_grad,
        gain_two_grad,
        shift_two_grad,
        bias_up_grad,
    )
    return (resid_grad, attended_grad, out_weight_grad, tail, up_grad_flipped, down_grad)


def open_back(
    inputs,
    resid_grad,
    query_grad,
    keys_grad,
    values_grad,
    out_weight_grad,
    tail,
    attention_w,
    width,
):
    stacked_grad = jnp.stack([query_grad, keys_grad, values_grad])
    weight_grad = jnp.einsum(
        "nd,jne->jde", inputs, stacked_grad, preferred_element_type=jnp.float32
    ).reshape(3 * width, width)
    input_grad = resid_grad + jnp.einsum(
        "jne,jde->nd",
        stacked_grad,
        attention_w[: 3 * width].reshape(3, width, width),
        preferred_element_type=jnp.float32,
    )
    bias_query_grad = jnp.sum(query_grad.astype(jnp.float32), 0)
    bias_value_grad = jnp.sum(values_grad.astype(jnp.float32), 0)
    (
        bias_out_grad,
        gain_one_grad,
        shift_one_grad,
        bias_down_grad,
        gain_two_grad,
        shift_two_grad,
        bias_up_grad,
    ) = tail
    vector_grad = jnp.concatenate(
        [
            bias_query_grad,
            bias_value_grad,
            bias_out_grad,
            gain_one_grad,
            shift_one_grad,
            bias_down_grad,
            gain_two_grad,
            shift_two_grad,
            bias_up_grad,
        ]
    )
    attention_grad = jnp.concatenate([weight_grad, out_weight_grad], 0)
    return (input_grad, attention_grad, vector_grad)


def by_stretch(array, stretches):
    return array.reshape((stretches, array.shape[0] // stretches) + array.shape[1:])


def shards(
    shape,
    text_in,
    layout_in,
    lengths,
    dup_rows,
    text_attention,
    text_up,
    text_down,
    text_vector,
    layout_attention,
    layout_up,
    layout_down,
    layout_vector,
    text_cotangent,
    layout_cotangent,
):
    count = shape["gx"] * shape["gy"]
    me = flat_index(shape["gy"])
    text_rows, layout_rows = text_attention.shape[0], layout_attention.shape[0]
    text_vec, layout_vec = text_vector.shape[0], layout_vector.shape[0]
    packed = pack_rows(
        text_attention,
        [layout_attention, layout_up.T, layout_down],
        jnp.concatenate([text_vector, layout_vector]),
    ).astype(jnp.bfloat16)
    gathered = gather_rows(packed, shape, me)
    up_all = gather_rows(text_up.T.astype(jnp.bfloat16), shape, me).reshape(-1, D)
    down_all = gather_rows(text_down.astype(jnp.bfloat16), shape, me).reshape(-1, D)
    text_all, layouts_all, text_vec_all, layout_vec_all = unpack_rows(
        gathered, text_rows, layout_rows, text_vec, layout_vec
    )
    text_weights = (text_all.reshape(-1, D), up_all, down_all, text_vec_all.reshape(-1))
    layout_weights = tuple(rows.reshape(-1, DL) for rows in layouts_all) + (
        layout_vec_all.reshape(-1),
    )
    stretches = lengths.shape[0]
    text_query, text_keys, text_values = open_stream(text_in, text_weights, D)
    layout_query, layout_keys, layout_values = open_stream(layout_in, layout_weights, DL)
    opened = (text_query, text_keys, text_values, layout_query, layout_keys, layout_values)
    opened_stretches = tuple((by_stretch(array, stretches) for array in opened))
    text_att, layout_att, log_total = lax.map(attend_forward, opened_stretches + (lengths,))
    text_att = text_att.reshape(-1, D)
    layout_att = layout_att.reshape(-1, DL)
    text_final, text_saved = close_stream(text_in, text_att, text_weights, D)
    layout_final, layout_saved = close_stream(layout_in, layout_att, layout_weights, DL)
    text_back, layout_back = text_weights, layout_weights
    span = text_in.shape[0] // stretches
    position = jnp.arange(span)
    keep = (position[None, :] < lengths[:, None]) & (dup_rows.reshape(stretches, span) == 0)
    keep = keep.reshape(-1, 1).astype(jnp.float32)
    text_cot = text_cotangent.astype(jnp.float32) * keep
    layout_cot = layout_cotangent.astype(jnp.float32) * keep
    text_resid, text_att_grad, text_out_w, text_tail, text_up_flipped, text_down_grad = close_back(
        text_cot, text_att, text_saved, text_back, D
    )
    (
        layout_resid,
        layout_att_grad,
        layout_out_w,
        layout_tail,
        layout_up_flipped,
        layout_down_grad,
    ) = close_back(layout_cot, layout_att, layout_saved, layout_back, DL)
    back_pieces = opened_stretches + (
        lengths,
        log_total,
        by_stretch(text_att_grad, stretches),
        by_stretch(layout_att_grad, stretches),
    )
    grads = lax.map(attend_backward, back_pieces)
    (
        text_query_grad,
        text_keys_grad,
        text_values_grad,
        layout_query_grad,
        layout_keys_grad,
        layout_values_grad,
    ) = tuple((array.reshape(-1, array.shape[-1]) for array in grads))
    text_input_grad, text_attention_grad, text_vector_grad = open_back(
        text_in,
        text_resid,
        text_query_grad,
        text_keys_grad,
        text_values_grad,
        text_out_w,
        text_tail,
        text_back[0],
        D,
    )
    layout_input_grad, layout_attention_grad, layout_vector_grad = open_back(
        layout_in,
        layout_resid,
        layout_query_grad,
        layout_keys_grad,
        layout_values_grad,
        layout_out_w,
        layout_tail,
        layout_back[0],
        DL,
    )
    def by_owner(array):
        return array.reshape((count, array.shape[0] // count) + array.shape[1:])

    attention_sum = scatter_rows(
        pack_rows(
            by_owner(text_attention_grad),
            [by_owner(g) for g in (layout_attention_grad, layout_up_flipped, layout_down_grad)],
            jnp.concatenate([by_owner(text_vector_grad), by_owner(layout_vector_grad)], -1),
        ).astype(jnp.bfloat16),
        shape,
        me,
    )
    up_sum = scatter_rows(by_owner(text_up_flipped).astype(jnp.bfloat16), shape, me)
    down_sum = scatter_rows(by_owner(text_down_grad).astype(jnp.bfloat16), shape, me)
    text_attention_sum, layout_sums, text_vec_sum, layout_vec_sum = unpack_rows(
        attention_sum, text_rows, layout_rows, text_vec, layout_vec
    )
    return (
        text_final.astype(jnp.bfloat16),
        layout_final.astype(jnp.bfloat16),
        text_input_grad.astype(jnp.bfloat16),
        layout_input_grad.astype(jnp.bfloat16),
        text_attention_sum,
        up_sum.T,
        down_sum,
        text_vec_sum,
        layout_sums[0],
        layout_sums[1].T,
        layout_sums[2],
        layout_vec_sum,
    )


BF = jnp.bfloat16
F32 = jnp.float32
CAT = 128
TEXT_LANES = D // HEADS
LAYOUT_LANES = DL // HEADS
MASK_LANE = TEXT_LANES + LAYOUT_LANES
VMEM_SPEC = pl.BlockSpec(memory_space=pltpu.VMEM)
SMEM_SPEC = pl.BlockSpec(memory_space=pltpu.SMEM)
ANY_SPEC = pl.BlockSpec(memory_space=pl.ANY)


def nn(left, right):
    return lax.dot_general(left, right, (((1,), (0,)), ((), ())), preferred_element_type=F32)


def nt(left, right):
    return lax.dot_general(left, right, (((1,), (1,)), ((), ())), preferred_element_type=F32)


def tn(left, right):
    return lax.dot_general(left, right, (((0,), (0,)), ((), ())), preferred_element_type=F32)


def row_mean(array):
    return jnp.sum(array, -1, keepdims=True) * (1.0 / array.shape[-1])


def col_sum(array):
    return jnp.sum(array, 0, keepdims=True)


def norm(resid):
    center = resid - row_mean(resid)
    inverse = lax.rsqrt(row_mean(center * center) + EPS)
    return center * inverse, inverse


def norm_grad(grad, scaled, inverse, gain):
    weighted = grad * gain
    return inverse * (weighted - row_mean(weighted) - scaled * row_mean(weighted * scaled))


def kernel_call(body, name, outs, ins, scratch=()):
    return pl.pallas_call(
        body,
        out_shape=[jax.ShapeDtypeStruct(shape, kind) for shape, kind, _ in outs],
        in_specs=[spec for _, spec in ins],
        out_specs=[spec for _, _, spec in outs],
        scratch_shapes=list(scratch),
        name=name,
        compiler_params=pltpu.CompilerParams(vmem_limit_bytes=60 * 2**20),
    )(*[array for array, _ in ins])


def stack_parts(blocks, cut):
    count, (_, rows, width) = len(blocks), blocks[0].shape

    def body(*refs):
        sems = refs[-1]
        first, second = refs[count], refs[count + 1]
        copies = []
        for index in range(count):
            source = refs[index].at[0]
            copies.append(
                pltpu.make_async_copy(source.at[0:cut], first.at[index], sems.at[2 * index])
            )
            copies.append(
                pltpu.make_async_copy(
                    source.at[cut:rows], second.at[index], sems.at[2 * index + 1]
                )
            )
        for copy in copies:
            copy.start()
        for copy in copies:
            copy.wait()

    return kernel_call(
        body,
        "stack_parts",
        [((count, cut, width), BF, ANY_SPEC), ((count, rows - cut, width), BF, ANY_SPEC)],
        [(block, ANY_SPEC) for block in blocks],
        [pltpu.SemaphoreType.DMA((2 * count,))],
    )


def gather_pieces(shard, cut, shape):
    count = shape["gx"] * shape["gy"]
    (x, nx), (core, ncore), (z, nz), (y, ny) = exchange_dims(shape)
    blocks = [shard[None]]
    blocks += [swap(blocks[0], z * step, count) for step in range(1, nz)]
    parts = []
    for held, (first, second) in zip(stack_parts(blocks, cut), ((y, x), (x, y))):
        near = swap(held, first, count)
        pieces = [(held, 0), (near, first), (swap(held, second, count), second)]
        pieces.append((swap(near, second, count), first ^ second))
        pieces += [(swap(array, core, count), offset ^ core) for array, offset in pieces]
        parts.append(pieces)
    return parts


def fetch_blocks(me, pieces, refs, z_stride, place, sems, base):
    copies = []
    for (array, offset), ref in zip(pieces, refs):
        for index in range(array.shape[0]):
            device = me ^ (offset ^ (z_stride * index))
            for source, target in place(ref.at[index], device):
                copies.append(pltpu.make_async_copy(source, target, sems.at[base + len(copies)]))
    return copies


def send_blocks(me, dims, swapped, source, keep, send, sems, base):
    (x, _), (core, _), (z, nz), (y, _) = dims
    top, low = (y, x) if swapped else (x, y)
    count = 4 * nz
    waits = []
    for device in range(2 * count):
        away = me ^ device
        slot = (away // top % 2) * 2 * nz + (away // low % 2) * nz + away // z % nz
        far = away // core % 2
        sem = sems.at[base + device]

        @pl.when(far == 0)
        def _():
            pltpu.make_async_copy(source(device), keep.at[slot], sem).start()

        @pl.when(far == 1)
        def _():
            pltpu.make_async_copy(source(device), send.at[slot], sem).start()

        waits.append(pltpu.make_async_copy(source(device), keep.at[slot], sem))
    return waits


def reduce_part(keep, send, dims, swapped, count):
    (x, _), (core, _), (z, nz), (y, _) = dims
    top, low = (y, x) if swapped else (x, y)
    total = keep.astype(F32) + swap(send, core, count).astype(F32)
    for stride in (top, low):
        half = total.shape[0] // 2
        total = total[:half] + swap(total[half:].astype(BF), stride, count).astype(F32)
    result = total[0]
    for step in range(1, nz):
        result = result + swap(total[step].astype(BF), z * step, count).astype(F32)
    return result


def vector_rows(read, width, segment, count):
    rows = []
    for row in range(segment * count // width):
        at, stop, parts = row * width, (row + 1) * width, []
        while at < stop:
            device, start = at // segment, at % segment
            take = min(segment - start, stop - at)
            parts.append(read(device, start, start + take))
            at += take
        rows.append(parts[0] if len(parts) == 1 else jnp.concatenate(parts, 1))
    return rows


def project(me, length, text_in, layout_in, parts, sizes, z_stride):
    count, text_rows, layout_rows, text_vec, layout_vec, cut = sizes
    rows = text_in.shape[0]
    pieces = parts[0] + parts[1]
    copies_of = count * 3

    def body(*refs):
        me_ref, length_ref, x_ref, xl_ref = refs[:4]
        piece_refs = refs[4 : 4 + len(pieces)]
        (
            q_ref,
            k_ref,
            v_ref,
            weight_out,
            layout_ref,
            up_ref,
            down_ref,
            text_vec_ref,
            layout_vec_ref,
            weight,
            tail,
            sems,
            out_sem,
        ) = refs[4 + len(pieces) :]
        mine = me_ref[0]

        def place_one(source, device):
            base = pl.multiple_of(device * text_rows, 16)
            return [(source, weight.at[pl.ds(base, cut)])]

        def place_two(source, device):
            base = pl.multiple_of(device * text_rows + cut, 16)
            return [
                (source.at[0 : text_rows - cut], weight.at[pl.ds(base, text_rows - cut)]),
                (source.at[text_rows - cut :], tail.at[device]),
            ]

        split = len(parts[0])
        copies = fetch_blocks(mine, parts[0], piece_refs[:split], z_stride, place_one, sems, 0)
        copies += fetch_blocks(
            mine, parts[1], piece_refs[split:], z_stride, place_two, sems, len(copies)
        )
        for copy in copies:
            copy.start()
        for copy in copies:
            copy.wait()
        out_copy = pltpu.make_async_copy(weight, weight_out, out_sem)
        out_copy.start()
        side = D // 3
        for device in range(count):
            block = pl.ds(device * layout_rows, layout_rows)
            for index, ref in enumerate((layout_ref, up_ref, down_ref)):
                ref[block, :] = tail[device, 0:layout_rows, side * index : side * index + DL]

        def read_text(device, start, stop):
            return tail[device, layout_rows : layout_rows + 1, start:stop].astype(F32)

        def read_layout(device, start, stop):
            return read_text(device, text_vec + start, text_vec + stop)

        for index, row in enumerate(vector_rows(read_text, D, text_vec, count)):
            text_vec_ref[index] = row
        for index, row in enumerate(vector_rows(read_layout, DL, layout_vec, count)):
            layout_vec_ref[index] = row
        x, xl = x_ref[...], xl_ref[...]
        seen = lax.broadcasted_iota(jnp.int32, (rows, CAT - MASK_LANE), 0) < length_ref[0]
        lane = lax.broadcasted_iota(jnp.int32, (rows, CAT - MASK_LANE), 1)
        ones = jnp.where(lane == 0, 1.0, 0.0).astype(BF)
        hidden = jnp.where((lane == 0) & jnp.logical_not(seen), NEG, 0.0).astype(BF)
        nothing = jnp.zeros((rows, CAT - MASK_LANE), BF)
        for index, (ref, extra) in enumerate(((q_ref, ones), (k_ref, hidden), (v_ref, nothing))):
            text = nn(x, weight[index * D : (index + 1) * D, :])
            layout = nn(xl, layout_ref[index * DL : (index + 1) * DL, :])
            if index != 1:
                text = text + text_vec_ref[index // 2]
                layout = layout + layout_vec_ref[index // 2]
            text, layout = text.astype(BF), layout.astype(BF)
            if index == 0:
                text = text * (1.0 / math.sqrt(TEXT_LANES))
                layout = layout * (1.0 / math.sqrt(LAYOUT_LANES))
            for head in range(HEADS):
                ref[head] = jnp.concatenate(
                    [
                        text[:, TEXT_LANES * head : TEXT_LANES * (head + 1)],
                        layout[:, LAYOUT_LANES * head : LAYOUT_LANES * (head + 1)],
                        extra,
                    ],
                    1,
                )
        out_copy.wait()

    cat = ((HEADS, rows, CAT), BF, VMEM_SPEC)
    return kernel_call(
        body,
        "project",
        [
            cat,
            cat,
            cat,
            ((4 * D, D), BF, ANY_SPEC),
            ((4 * DL, DL), BF, VMEM_SPEC),
            ((FFL, DL), BF, VMEM_SPEC),
            ((FFL, DL), BF, VMEM_SPEC),
            ((12, 1, D), F32, VMEM_SPEC),
            ((12, 1, DL), F32, VMEM_SPEC),
        ],
        [(me, SMEM_SPEC), (length, SMEM_SPEC), (text_in, VMEM_SPEC), (layout_in, VMEM_SPEC)]
        + [(array, ANY_SPEC) for array, _ in pieces],
        [
            pltpu.VMEM((4 * D, D), BF),
            pltpu.VMEM((count, parts[0][0][0].shape[1] + parts[1][0][0].shape[1] - text_rows, D), BF),
            pltpu.SemaphoreType.DMA((copies_of,)),
            pltpu.SemaphoreType.DMA,
        ],
    )


def heads_out(ref):
    text = jnp.concatenate([ref[head, :, 0:TEXT_LANES] for head in range(HEADS)], 1)
    layout = jnp.concatenate([ref[head, :, TEXT_LANES:MASK_LANE] for head in range(HEADS)], 1)
    return text, layout


def attend(text_in, layout_in, query, keys, values, weight, layout_w, text_vec, layout_vec):
    rows = text_in.shape[0]

    def body(
        x_ref,
        xl_ref,
        q_ref,
        k_ref,
        v_ref,
        weight_any,
        layout_ref,
        tv_ref,
        lv_ref,
        out_t,
        out_l,
        lse_ref,
        norm_t,
        inv_t,
        norm_l,
        inv_l,
        mixed,
        weight,
        sem,
    ):
        fetch = pltpu.make_async_copy(weight_any.at[3 * D : 4 * D], weight, sem)
        fetch.start()

        def head_step(head, carry):
            scores = nt(k_ref[head], q_ref[head])
            top = jnp.max(scores, 0, keepdims=True)
            expo = jnp.exp(scores - top)
            total = col_sum(expo)
            probs = (expo * (1.0 / total)).astype(BF)
            mixed[head] = tn(v_ref[head], probs).T.astype(BF)
            lse_ref[head] = top + jnp.log(total)
            return carry

        lax.fori_loop(0, HEADS, head_step, 0)
        text, layout = heads_out(mixed)
        out_t[...] = text
        out_l[...] = layout
        fetch.wait()
        after = nn(text, weight[...]) + tv_ref[2]
        norm_t[...], inv_t[...] = norm(x_ref[...].astype(F32) + after)
        after = nn(layout, layout_ref[3 * DL : 4 * DL, :]) + lv_ref[2]
        norm_l[...], inv_l[...] = norm(xl_ref[...].astype(F32) + after)

    return kernel_call(
        body,
        "attend",
        [
            ((rows, D), BF, VMEM_SPEC),
            ((rows, DL), BF, VMEM_SPEC),
            ((HEADS, 1, rows), F32, VMEM_SPEC),
            ((rows, D), F32, VMEM_SPEC),
            ((rows, 1), F32, VMEM_SPEC),
            ((rows, DL), F32, VMEM_SPEC),
            ((rows, 1), F32, VMEM_SPEC),
        ],
        [
            (text_in, VMEM_SPEC),
            (layout_in, VMEM_SPEC),
            (query, VMEM_SPEC),
            (keys, VMEM_SPEC),
            (values, VMEM_SPEC),
            (weight, ANY_SPEC),
            (layout_w, VMEM_SPEC),
            (text_vec, VMEM_SPEC),
            (layout_vec, VMEM_SPEC),
        ],
        [pltpu.VMEM((HEADS, rows, CAT), BF), pltpu.VMEM((D, D), BF), pltpu.SemaphoreType.DMA],
    )


def erf_of(value):
    value = jnp.clip(value, -4.0, 4.0)
    square = value * value
    top = jnp.full_like(square, -2.72614225801306e-10)
    for factor in (
        2.77068142495902e-08,
        -2.10102402082508e-06,
        -5.69250639462346e-05,
        -7.34990630326855e-04,
        -2.95459980854025e-03,
        -1.60960333262415e-02,
    ):
        top = top * square + factor
    low = jnp.full_like(square, -1.45660718464996e-05)
    for factor in (
        -2.13374055278905e-04,
        -1.68282697438203e-03,
        -7.37332916720468e-03,
        -1.42647390514189e-02,
    ):
        low = low * square + factor
    return value * top / low


def gelu_both(value):
    below = 0.5 * (1.0 + erf_of(value * math.sqrt(0.5)))
    density = jnp.exp(value * value * -0.5) * (1.0 / math.sqrt(2.0 * math.pi))
    return value * below, below + value * density


def feed_stream(norm_ref, vec_ref, cot_ref, keep, up, down, hidden, slope, blocks, write, outs):
    out_ref, grad_ref, vec_out = outs
    first = norm_ref[...] * vec_ref[3] + vec_ref[4]
    low = first.astype(BF)

    def forward(block, total):
        upper = nt(low, up(block)) + vec_ref[8 + block]
        act, rise = gelu_both(upper)
        act = act.astype(BF)
        hidden[block] = act
        slope[block] = rise
        return total + nn(act, down(block))

    branch = lax.fori_loop(0, blocks, forward, jnp.zeros_like(first))
    scaled, inverse = norm(first + branch + vec_ref[5])
    out_ref[...] = (scaled * vec_ref[6] + vec_ref[7]).astype(BF)
    cotan = cot_ref[...].astype(F32) * keep
    vec_out[1] = col_sum(cotan * scaled)
    vec_out[2] = col_sum(cotan)
    second = norm_grad(cotan, scaled, inverse, vec_ref[6])
    branch_low = second.astype(BF)
    vec_out[0] = col_sum(branch_low.astype(F32))

    def backward(block, total):
        act_grad = nt(branch_low, down(block))
        upper_low = (act_grad * slope[block]).astype(BF)
        vec_out[3 + block] = col_sum(upper_low.astype(F32))
        write(block, tn(upper_low, low), tn(hidden[block], branch_low))
        return total + nn(upper_low, up(block))

    grad_ref[...] = lax.fori_loop(0, blocks, backward, second)


def feed(me, keep_rows, norm_t, norm_l, tv, lv, cot_t, cot_l, parts, lu, ld, dims, text_rows):
    rows = norm_t.shape[0]
    pieces = parts[0] + parts[1]
    nz, z_stride = dims[2][1], dims[2][0]
    count = 8 * nz
    blocks = FF // D

    def body(*refs):
        me_ref, keep_ref, nt_ref, nl_ref, tv_ref, lv_ref, ct_ref, cl_ref, lu_ref, ld_ref = refs[:10]
        piece_refs = refs[10 : 10 + len(pieces)]
        (
            out_t,
            out_l,
            grad_t,
            grad_l,
            vec_t,
            vec_l,
            lu_grad,
            ld_grad,
            up_keep,
            up_send,
            down_keep,
            down_send,
            up,
            down,
            hidden,
            slope,
            hidden_l,
            slope_l,
            up_grad,
            down_grad,
            sems,
        ) = refs[10 + len(pieces) :]
        mine = me_ref[0]

        def place(target):
            def at(source, device):
                return [(source, target.at[pl.ds(pl.multiple_of(device * text_rows, 16), text_rows)])]

            return at

        split = len(parts[0])
        copies = fetch_blocks(mine, parts[0], piece_refs[:split], z_stride, place(up), sems, 0)
        copies += fetch_blocks(
            mine, parts[1], piece_refs[split:], z_stride, place(down), sems, count
        )
        for copy in copies:
            copy.start()
        keep = keep_ref[...]

        def rows_of(ref, size):
            return lambda block: ref[pl.ds(pl.multiple_of(block * size, 8), size), :]

        def write_l(block, one, two):
            at = pl.ds(pl.multiple_of(block * DL, 8), DL)
            lu_grad[at, :] = one.astype(BF)
            ld_grad[at, :] = two.astype(BF)

        feed_stream(
            nl_ref,
            lv_ref,
            cl_ref,
            keep,
            rows_of(lu_ref, DL),
            rows_of(ld_ref, DL),
            hidden_l,
            slope_l,
            FFL // DL,
            write_l,
            (out_l, grad_l, vec_l),
        )
        for copy in copies:
            copy.wait()

        def write_t(block, one, two):
            at = pl.ds(pl.multiple_of(block * D, 16), D)
            up_grad[at, :] = one.astype(BF)
            down_grad[at, :] = two.astype(BF)

        feed_stream(
            nt_ref,
            tv_ref,
            ct_ref,
            keep,
            rows_of(up, D),
            rows_of(down, D),
            hidden,
            slope,
            blocks,
            write_t,
            (out_t, grad_t, vec_t),
        )
        waits = send_blocks(
            mine,
            dims,
            False,
            lambda device: up_grad.at[device * text_rows : (device + 1) * text_rows],
            up_keep,
            up_send,
            sems,
            0,
        )
        waits += send_blocks(
            mine,
            dims,
            True,
            lambda device: down_grad.at[device * text_rows : (device + 1) * text_rows],
            down_keep,
            down_send,
            sems,
            count,
        )
        for wait in waits:
            wait.wait()

    part = ((count // 2, text_rows, D), BF, ANY_SPEC)
    return kernel_call(
        body,
        "feed",
        [
            ((rows, D), BF, VMEM_SPEC),
            ((rows, DL), BF, VMEM_SPEC),
            ((rows, D), F32, VMEM_SPEC),
            ((rows, DL), F32, VMEM_SPEC),
            ((3 + blocks, 1, D), F32, VMEM_SPEC),
            ((3 + blocks, 1, DL), F32, VMEM_SPEC),
            ((FFL, DL), BF, VMEM_SPEC),
            ((FFL, DL), BF, VMEM_SPEC),
            part,
            part,
            part,
            part,
        ],
        [
            (me, SMEM_SPEC),
            (keep_rows, VMEM_SPEC),
            (norm_t, VMEM_SPEC),
            (norm_l, VMEM_SPEC),
            (tv, VMEM_SPEC),
            (lv, VMEM_SPEC),
            (cot_t, VMEM_SPEC),
            (cot_l, VMEM_SPEC),
            (lu, VMEM_SPEC),
            (ld, VMEM_SPEC),
        ]
        + [(array, ANY_SPEC) for array, _ in pieces],
        [
            pltpu.VMEM((FF, D), BF),
            pltpu.VMEM((FF, D), BF),
            pltpu.VMEM((blocks, rows, D), BF),
            pltpu.VMEM((blocks, rows, D), F32),
            pltpu.VMEM((FFL // DL, rows, DL), BF),
            pltpu.VMEM((FFL // DL, rows, DL), F32),
            pltpu.VMEM((FF, D), BF),
            pltpu.VMEM((FF, D), BF),
            pltpu.SemaphoreType.DMA((2 * count,)),
        ],
    )


def attend_back(grad_t, grad_l, norms, outs, weight, layout_w, tv, lv, query, keys, values, lse):
    rows = grad_t.shape[0]
    norm_t, inv_t, norm_l, inv_l = norms
    out_t, out_l = outs

    def body(
        gt_ref,
        gl_ref,
        nt_ref,
        it_ref,
        nl_ref,
        il_ref,
        ot_ref,
        ol_ref,
        weight_any,
        layout_ref,
        tv_ref,
        lv_ref,
        q_ref,
        k_ref,
        v_ref,
        lse_ref,
        resid_t,
        resid_l,
        out_wt,
        out_wl,
        vec_t,
        vec_l,
        dqt,
        dql,
        dkt,
        dkl,
        dvt,
        dvl,
        dout,
        dq,
        dk,
        dv,
        weight,
        sem,
    ):
        fetch = pltpu.make_async_copy(weight_any.at[3 * D : 4 * D], weight, sem)
        fetch.start()

        def close(grad, scaled, inverse, vec, mixed, vec_out, resid_ref, wide):
            vec_out[1] = col_sum(grad * scaled)
            vec_out[2] = col_sum(grad)
            resid = norm_grad(grad, scaled, inverse, vec[3])
            resid_ref[...] = resid
            after = resid.astype(BF)
            vec_out[0] = col_sum(after.astype(F32))
            return after, tn(mixed, after).astype(BF), nt(after, wide()).astype(BF)

        def wide_l():
            return layout_ref[3 * DL : 4 * DL, :]

        def wide_t():
            fetch.wait()
            return weight[...]

        _, out_wl[...], att_l = close(
            gl_ref[...], nl_ref[...], il_ref[...], lv_ref, ol_ref[...], vec_l, resid_l, wide_l
        )
        _, out_wt[...], att_t = close(
            gt_ref[...], nt_ref[...], it_ref[...], tv_ref, ot_ref[...], vec_t, resid_t, wide_t
        )
        nothing = jnp.zeros((rows, CAT - MASK_LANE), BF)
        for head in range(HEADS):
            dout[head] = jnp.concatenate(
                [
                    att_t[:, TEXT_LANES * head : TEXT_LANES * (head + 1)],
                    att_l[:, LAYOUT_LANES * head : LAYOUT_LANES * (head + 1)],
                    nothing,
                ],
                1,
            )
        is_text = lax.broadcasted_iota(jnp.int32, (rows, CAT), 1) < TEXT_LANES
        text_row = lax.broadcasted_iota(jnp.int32, (CAT, rows), 0) < TEXT_LANES

        def head_step(head, carry):
            q, k, v, do = q_ref[head], k_ref[head], v_ref[head], dout[head]
            probs = jnp.exp(nt(k, q) - lse_ref[head])
            dv[head] = nn(probs.astype(BF), do).astype(BF)
            none = jnp.zeros_like(v)
            mixed = nt(jnp.where(is_text, v, none), do)
            score_t = (probs * (mixed - col_sum(probs * mixed))).astype(BF)
            mixed = nt(jnp.where(is_text, none, v), do)
            score_l = (probs * (mixed - col_sum(probs * mixed))).astype(BF)
            dk_t = nn(score_t, q)
            dk_l = nn(score_l, q)
            dk[head] = jnp.where(is_text, dk_t, dk_t + dk_l).astype(BF)
            dq_t = tn(k, score_t)
            dq_l = tn(k, score_l)
            scaled = jnp.where(
                text_row,
                dq_t * (1.0 / math.sqrt(TEXT_LANES)),
                (dq_t + dq_l) * (1.0 / math.sqrt(LAYOUT_LANES)),
            )
            dq[head] = scaled.T.astype(BF)
            return carry

        lax.fori_loop(0, HEADS, head_step, 0)
        dqt[...], dql[...] = heads_out(dq)
        dkt[...], dkl[...] = heads_out(dk)
        dvt[...], dvl[...] = heads_out(dv)

    text, layout = ((rows, D), BF, VMEM_SPEC), ((rows, DL), BF, VMEM_SPEC)
    cat = pltpu.VMEM((HEADS, rows, CAT), BF)
    return kernel_call(
        body,
        "attend_back",
        [
            ((rows, D), F32, VMEM_SPEC),
            ((rows, DL), F32, VMEM_SPEC),
            ((D, D), BF, VMEM_SPEC),
            ((DL, DL), BF, VMEM_SPEC),
            ((3, 1, D), F32, VMEM_SPEC),
            ((3, 1, DL), F32, VMEM_SPEC),
            text,
            layout,
            text,
            layout,
            text,
            layout,
        ],
        [
            (grad_t, VMEM_SPEC),
            (grad_l, VMEM_SPEC),
            (norm_t, VMEM_SPEC),
            (inv_t, VMEM_SPEC),
            (norm_l, VMEM_SPEC),
            (inv_l, VMEM_SPEC),
            (out_t, VMEM_SPEC),
            (out_l, VMEM_SPEC),
            (weight, ANY_SPEC),
            (layout_w, VMEM_SPEC),
            (tv, VMEM_SPEC),
            (lv, VMEM_SPEC),
            (query, VMEM_SPEC),
            (keys, VMEM_SPEC),
            (values, VMEM_SPEC),
            (lse, VMEM_SPEC),
        ],
        [cat, cat, cat, cat, pltpu.VMEM((D, D), BF), pltpu.SemaphoreType.DMA],
    )


def project_back(
    me, text_in, layout_in, back, resids, weight, layout_w, out_w, ffn_l, vecs, dims, sizes
):
    count, text_rows, layout_rows, text_vec, layout_vec, cut = sizes
    rows = text_in.shape[0]
    packed = text_rows + layout_rows + 8

    def body(
        me_ref,
        x_ref,
        xl_ref,
        dqt,
        dql,
        dkt,
        dkl,
        dvt,
        dvl,
        resid_t,
        resid_l,
        weight_any,
        layout_ref,
        out_wt,
        out_wl,
        lu_grad,
        ld_grad,
        close_t,
        close_l,
        feed_t,
        feed_l,
        grad_t,
        grad_l,
        keep_one,
        send_one,
        keep_two,
        send_two,
        weight,
        pack,
        att_l,
        sems,
        sem,
    ):
        fetch = pltpu.make_async_copy(weight_any.at[0 : 3 * D], weight, sem)
        fetch.start()
        mine = me_ref[0]
        x, xl = x_ref[...], xl_ref[...]
        side = D // 3
        for device in range(count):
            pack[device, text_rows : text_rows + layout_rows, :] = jnp.zeros((layout_rows, D), BF)
        per_block = D // text_rows
        for index, ref in enumerate((dqt, dkt, dvt)):
            grad = tn(x, ref[...]).astype(BF)
            for part in range(per_block):
                pack[index * per_block + part, 0:text_rows, :] = grad[
                    part * text_rows : (part + 1) * text_rows
                ]
        for part in range(per_block):
            pack[3 * per_block + part, 0:text_rows, :] = out_wt[
                part * text_rows : (part + 1) * text_rows, :
            ]
        for index, ref in enumerate((dql, dkl, dvl)):
            att_l[index * DL : (index + 1) * DL, :] = tn(xl, ref[...]).astype(BF)
        att_l[3 * DL : 4 * DL, :] = out_wl[...]
        for device in range(count):
            block = pl.ds(device * layout_rows, layout_rows)
            for index, ref in enumerate((att_l, lu_grad, ld_grad)):
                pack[
                    device,
                    text_rows : text_rows + layout_rows,
                    side * index : side * index + DL,
                ] = ref[block, :]

        def vector(query, values, close, feeds):
            rows_of = [col_sum(query[...].astype(F32)), col_sum(values[...].astype(F32))]
            rows_of += [close[0], close[1], close[2], feeds[0], feeds[1], feeds[2]]
            return rows_of + [feeds[3 + block] for block in range(FF // D)]

        text_rows_of = vector(dqt, dvt, close_t, feed_t)
        layout_rows_of = vector(dql, dvl, close_l, feed_l)

        def segment(all_rows, width, start, size):
            parts, stop = [], start + size
            while start < stop:
                row, at = start // width, start % width
                take = min(width - at, stop - start)
                parts.append(all_rows[row][:, at : at + take])
                start += take
            return parts

        row = lax.broadcasted_iota(jnp.int32, (8, D), 0)
        for device in range(count):
            parts = segment(text_rows_of, D, device * text_vec, text_vec)
            parts += segment(layout_rows_of, DL, device * layout_vec, layout_vec)
            parts.append(jnp.zeros((1, D - text_vec - layout_vec), F32))
            line = jnp.concatenate(parts, 1)
            pack[device, text_rows + layout_rows :, :] = jnp.where(
                row == 0, jnp.broadcast_to(line, (8, D)), 0.0
            ).astype(BF)
        waits = send_blocks(
            mine, dims, False, lambda device: pack.at[device, 0:cut], keep_one, send_one, sems, 0
        )
        waits += send_blocks(
            mine,
            dims,
            True,
            lambda device: pack.at[device, cut:packed],
            keep_two,
            send_two,
            sems,
            count,
        )
        total = resid_l[...]
        for index, ref in enumerate((dql, dkl, dvl)):
            total = total + nt(ref[...], layout_ref[index * DL : (index + 1) * DL, :])
        grad_l[...] = total.astype(BF)
        fetch.wait()
        total = resid_t[...]
        for index, ref in enumerate((dqt, dkt, dvt)):
            total = total + nt(ref[...], weight[index * D : (index + 1) * D, :])
        grad_t[...] = total.astype(BF)
        for wait in waits:
            wait.wait()

    one = ((count // 2, cut, D), BF, ANY_SPEC)
    two = ((count // 2, packed - cut, D), BF, ANY_SPEC)
    arrays = [text_in, layout_in, *back, *resids]
    return kernel_call(
        body,
        "project_back",
        [((rows, D), BF, VMEM_SPEC), ((rows, DL), BF, VMEM_SPEC), one, one, two, two],
        [(me, SMEM_SPEC)]
        + [(array, VMEM_SPEC) for array in arrays]
        + [(weight, ANY_SPEC), (layout_w, VMEM_SPEC)]
        + [(array, VMEM_SPEC) for array in (*out_w, *ffn_l, *vecs)],
        [
            pltpu.VMEM((3 * D, D), BF),
            pltpu.VMEM((count, packed, D), BF),
            pltpu.VMEM((4 * DL, DL), BF),
            pltpu.SemaphoreType.DMA((2 * count,)),
            pltpu.SemaphoreType.DMA,
        ],
    )


def shards_fast(
    shape,
    text_in,
    layout_in,
    lengths,
    dup_rows,
    text_attention,
    text_up,
    text_down,
    text_vector,
    layout_attention,
    layout_up,
    layout_down,
    layout_vector,
    text_cotangent,
    layout_cotangent,
):
    count = shape["gx"] * shape["gy"]
    dims = exchange_dims(shape)
    z_stride = dims[2][0]
    me = flat_index(shape["gy"]).reshape(1).astype(jnp.int32)
    text_rows, layout_rows = text_attention.shape[0], layout_attention.shape[0]
    text_vec, layout_vec = text_vector.shape[0], layout_vector.shape[0]
    packed = pack_rows(
        text_attention,
        [layout_attention, layout_up.T, layout_down],
        jnp.concatenate([text_vector, layout_vector]),
    ).astype(BF)
    cut = packed.shape[0] // 2
    sizes = (count, text_rows, layout_rows, text_vec, layout_vec, cut)
    parts = gather_pieces(packed, cut, shape)
    feed_shard = jnp.concatenate([text_up.T, text_down], 0).astype(BF)
    feed_parts = gather_pieces(feed_shard, text_rows, shape)
    q, k, v, weight, layout_w, lu, ld, tv, lv = project(
        me, lengths, text_in, layout_in, parts, sizes, z_stride
    )
    out_t, out_l, lse, norm_t, inv_t, norm_l, inv_l = attend(
        text_in, layout_in, q, k, v, weight, layout_w, tv, lv
    )
    span = text_in.shape[0]
    keep = (jnp.arange(span) < lengths[0]) & (dup_rows == 0)
    keep = keep.astype(F32)[:, None]
    (
        text_final,
        layout_final,
        grad_t,
        grad_l,
        feed_vt,
        feed_vl,
        lu_grad,
        ld_grad,
        up_keep,
        up_send,
        down_keep,
        down_send,
    ) = feed(
        me,
        keep,
        norm_t,
        norm_l,
        tv,
        lv,
        text_cotangent,
        layout_cotangent,
        feed_parts,
        lu,
        ld,
        dims,
        text_rows,
    )
    resid_t, resid_l, out_wt, out_wl, close_t, close_l, *back = attend_back(
        grad_t,
        grad_l,
        (norm_t, inv_t, norm_l, inv_l),
        (out_t, out_l),
        weight,
        layout_w,
        tv,
        lv,
        q,
        k,
        v,
        lse,
    )
    text_input_grad, layout_input_grad, keep_one, send_one, keep_two, send_two = project_back(
        me,
        text_in,
        layout_in,
        back,
        (resid_t, resid_l),
        weight,
        layout_w,
        (out_wt, out_wl),
        (lu_grad, ld_grad),
        (close_t, close_l, feed_vt, feed_vl),
        dims,
        sizes,
    )
    up_sum = reduce_part(up_keep, up_send, dims, False, count)
    down_sum = reduce_part(down_keep, down_send, dims, True, count)
    packed_sum = jnp.concatenate(
        [
            reduce_part(keep_one, send_one, dims, False, count),
            reduce_part(keep_two, send_two, dims, True, count),
        ],
        0,
    )
    text_sum, layout_sums, text_vec_sum, layout_vec_sum = unpack_rows(
        packed_sum, text_rows, layout_rows, text_vec, layout_vec
    )
    return (
        text_final,
        layout_final,
        text_input_grad,
        layout_input_grad,
        text_sum,
        up_sum.T,
        down_sum,
        text_vec_sum,
        layout_sums[0],
        layout_sums[1].T,
        layout_sums[2],
        layout_vec_sum,
    )


def fits(shape, text_in, lengths, text_attention, layout_attention):
    (_, nx), (_, ncore), (_, nz), (_, ny) = exchange_dims(shape)
    return (
        (nx, ncore, ny) == (2, 2, 2)
        and lengths.shape[0] == 1
        and text_attention.shape[0] % 16 == 0
        and layout_attention.shape[0] % 8 == 0
        and D % text_attention.shape[0] == 0
    )


def layer(shape, text_in, layout_in, lengths, dup_rows, *rest):
    chosen = shards_fast if fits(shape, text_in, lengths, rest[0], rest[4]) else shards
    return chosen(shape, text_in, layout_in, lengths, dup_rows, *rest)


def solution(mesh):
    placed = (
        P(("gx", "gy"), None),
        P(("gx", "gy"), None),
        P(("gx", "gy")),
        P(("gx", "gy")),
        P(("gx", "gy"), None),
        P(None, ("gx", "gy")),
        P(("gx", "gy"), None),
        P(("gx", "gy")),
        P(("gx", "gy"), None),
        P(None, ("gx", "gy")),
        P(("gx", "gy"), None),
        P(("gx", "gy")),
        P(("gx", "gy"), None),
        P(("gx", "gy"), None),
    )
    return jax.shard_map(
        functools.partial(layer, dict(mesh.shape)),
        mesh=mesh,
        in_specs=placed,
        out_specs=(
            P(("gx", "gy"), None),
            P(("gx", "gy"), None),
            P(("gx", "gy"), None),
            P(("gx", "gy"), None),
            P(("gx", "gy"), None),
            P(None, ("gx", "gy")),
            P(("gx", "gy"), None),
            P(("gx", "gy")),
            P(("gx", "gy"), None),
            P(None, ("gx", "gy")),
            P(("gx", "gy"), None),
            P(("gx", "gy")),
        ),
        check_vma=False,
    )
```

```python
import functools
import math

import jax
import jax.numpy as jnp
from jax import lax
from jax.experimental import pallas as pl
from jax.experimental.pallas import tpu as pltpu
from jax.sharding import PartitionSpec as P


AXES = ("gx", "gy")


def exchange_dims(shape):
    gx, gy = shape["gx"], shape["gy"]
    outer = {8: 4, 32: 4}.get(gy, gy)
    inner = gy // outer
    core = 2 if gx % 2 == 0 else 1
    core_dim = (gy, core)
    x_dim = (gy * core, gx // core)
    if inner <= outer:
        z_dim, y_dim = (inner, outer), (1, inner)
    else:
        z_dim, y_dim = (1, inner), (inner, outer)
    return x_dim, core_dim, z_dim, y_dim


def orders(shape):
    x_dim, core_dim, z_dim, y_dim = exchange_dims(shape)
    return ((z_dim, y_dim, x_dim, core_dim), (z_dim, x_dim, y_dim, core_dim))


def offsets(order):
    table = [0]
    for stride, size in order:
        table = [offset ^ (stride * step) for step in range(size) for offset in table]
    return table


def swap(array, offset, count):
    return lax.ppermute(array, AXES, [(device, device ^ offset) for device in range(count)])


def gather_part(part, order, count):
    held = part[None]
    for stride, size in order:
        pieces = [held] + [swap(held, stride * step, count) for step in range(1, size)]
        held = jnp.concatenate(pieces, 0)
    return held


def scatter_part(parts, order, count):
    held = parts
    for stride, size in reversed(order):
        held = held.reshape((size, held.shape[0] // size) + held.shape[1:])
        total = held[0].astype(jnp.float32)
        for step in range(1, size):
            total = total + swap(held[step], stride * step, count).astype(jnp.float32)
        last = (stride, size) == order[0]
        held = total if last else total.astype(jnp.bfloat16)
    return held[0]


def flat_index(gy):
    return lax.axis_index("gx") * gy + lax.axis_index("gy")


def positions(order, count):
    table = offsets(order)
    inverse = [0] * count
    for position, offset in enumerate(table):
        inverse[offset] = position
    return jnp.array(table, jnp.int32), jnp.array(inverse, jnp.int32)


def gather_rows(shard, shape, me):
    count = shape["gx"] * shape["gy"]
    half = shard.shape[0] // 2
    pieces = []
    for index, order in enumerate(orders(shape)):
        held = gather_part(shard[index * half : (index + 1) * half], order, count)
        inverse = positions(order, count)[1]
        pieces.append(jnp.take(held, inverse[jnp.arange(count) ^ me], axis=0))
    return jnp.concatenate(pieces, 1)


def scatter_rows(grads, shape, me):
    count = shape["gx"] * shape["gy"]
    half = grads.shape[1] // 2
    pieces = []
    for index, order in enumerate(orders(shape)):
        table = positions(order, count)[0]
        parts = jnp.take(grads[:, index * half : (index + 1) * half], me ^ table, axis=0)
        pieces.append(scatter_part(parts, order, count))
    return jnp.concatenate(pieces, 0)


def pad_cols(array, width):
    return jnp.pad(array, ((0, 0),) * (array.ndim - 1) + ((0, width - array.shape[-1]),))


def pack_rows(text_rows, layout_rows, vectors):
    side = D // 3
    layouts = jnp.concatenate([pad_cols(rows, side) for rows in layout_rows], -1)
    packed = jnp.concatenate([text_rows, layouts, pad_cols(vectors, D)[..., None, :]], -2)
    rows = packed.shape[-2]
    extra = -rows % 16
    return jnp.pad(packed, ((0, 0),) * (packed.ndim - 2) + ((0, extra), (0, 0)))


def unpack_rows(packed, text_rows, layout_rows, text_vec, layout_vec):
    side = D // 3
    text = packed[..., :text_rows, :]
    block = packed[..., text_rows : text_rows + layout_rows, :]
    layouts = [block[..., side * index : side * index + DL] for index in range(3)]
    vectors = packed[..., text_rows + layout_rows, :]
    return text, layouts, vectors[..., :text_vec], vectors[..., text_vec : text_vec + layout_vec]


D = 768
DL = 192
HEADS = 12
FF = 4 * D
FFL = 4 * DL


EPS = 1e-05
NEG = -1e30


def matmul(left, right):
    return jnp.dot(left, right, preferred_element_type=jnp.float32)


def contract_rows(left, right):
    return lax.dot_general(
        left, right, (((0,), (0,)), ((), ())), preferred_element_type=jnp.float32
    )


def contract_cols(left, right):
    return lax.dot_general(
        left, right, (((1,), (1,)), ((), ())), preferred_element_type=jnp.float32
    )


def vector_parts(vector, width):
    values = vector.astype(jnp.float32)
    return [values[index * width : (index + 1) * width] for index in range(8)] + [
        values[8 * width :]
    ]


def normalize(resid, gain, shift):
    center = resid - jnp.mean(resid, -1, keepdims=True)
    varian = jnp.mean(center * center, -1, keepdims=True)
    inverse = lax.rsqrt(varian + EPS)
    scaled = center * inverse
    return (scaled * gain + shift, scaled, inverse)


def norm_back(grad, scaled, inverse, gain):
    weighted = grad * gain
    inner = jnp.mean(weighted, -1, keepdims=True)
    across = jnp.mean(weighted * scaled, -1, keepdims=True)
    return inverse * (weighted - inner - scaled * across)


def exact_gelu(value):
    return jax.nn.gelu(value, approximate=False)


def open_stream(inputs, weights, width):
    parts = vector_parts(weights[3], width)
    stacked = weights[0][: 3 * width].reshape(3, width, width)
    projected = jnp.einsum("nd,jde->jne", inputs, stacked, preferred_element_type=jnp.float32)
    query = (projected[0] + parts[0]).astype(jnp.bfloat16)
    keys = projected[1].astype(jnp.bfloat16)
    values = (projected[2] + parts[1]).astype(jnp.bfloat16)
    return (query, keys, values)


def heads_view(array):
    return array.reshape(array.shape[0], HEADS, array.shape[1] // HEADS)


def head_scale(array):
    return 1.0 / math.sqrt(array.shape[1] // HEADS)


def joint_scores(text_query, text_keys, layout_query, layout_keys, length):
    rows = text_query.shape[0]
    text_part = jnp.einsum(
        "qhd,khd->hqk",
        heads_view(text_query),
        heads_view(text_keys),
        preferred_element_type=jnp.float32,
    )
    layout_part = jnp.einsum(
        "qhd,khd->hqk",
        heads_view(layout_query),
        heads_view(layout_keys),
        preferred_element_type=jnp.float32,
    )
    scores = text_part * head_scale(text_query) + layout_part * head_scale(layout_query)
    visible = jnp.arange(rows) < length
    return jnp.where(visible[None, None, :], scores, NEG)


def weigh_values(probs, values):
    mixed = jnp.einsum(
        "hqk,khd->qhd", probs, heads_view(values), preferred_element_type=jnp.float32
    )
    return mixed.reshape(values.shape[0], values.shape[1])


def attend_forward(pieces):
    text_query, text_keys, text_values, layout_query, layout_keys, layout_values, length = pieces
    scores = joint_scores(text_query, text_keys, layout_query, layout_keys, length)
    top = jnp.max(scores, -1, keepdims=True)
    expo = jnp.exp(scores - top)
    total = jnp.sum(expo, -1, keepdims=True)
    probs = (expo / total).astype(jnp.bfloat16)
    text_att = weigh_values(probs, text_values).astype(jnp.bfloat16)
    layout_att = weigh_values(probs, layout_values).astype(jnp.bfloat16)
    return (text_att, layout_att, (top + jnp.log(total))[:, :, 0])


def values_grad(probs_low, grad_out):
    moved = jnp.einsum(
        "hqk,qhd->khd", probs_low, heads_view(grad_out), preferred_element_type=jnp.float32
    )
    return moved.reshape(grad_out.shape[0], grad_out.shape[1]).astype(jnp.bfloat16)


def query_keys_grad(score_grads, query, keys):
    scale = head_scale(query)
    rows, width = query.shape
    query_grad = jnp.zeros((rows, HEADS, width // HEADS), jnp.float32)
    keys_grad = jnp.zeros((rows, HEADS, width // HEADS), jnp.float32)
    for score_grad in score_grads:
        query_grad = query_grad + jnp.einsum(
            "hqk,khd->qhd", score_grad, heads_view(keys), preferred_element_type=jnp.float32
        )
        keys_grad = keys_grad + jnp.einsum(
            "hqk,qhd->khd", score_grad, heads_view(query), preferred_element_type=jnp.float32
        )
    query_grad = query_grad * scale
    keys_grad = keys_grad * scale
    return (
        query_grad.reshape(rows, width).astype(jnp.bfloat16),
        keys_grad.reshape(rows, width).astype(jnp.bfloat16),
    )


def softmax_back(probs, mixed):
    return (probs * (mixed - jnp.sum(probs * mixed, -1, keepdims=True))).astype(jnp.bfloat16)


def attend_backward(pieces):
    (
        text_query,
        text_keys,
        text_values,
        layout_query,
        layout_keys,
        layout_values,
        length,
        log_total,
        text_grad,
        layout_grad,
    ) = pieces
    scores = joint_scores(text_query, text_keys, layout_query, layout_keys, length)
    probs = jnp.exp(scores - log_total[:, :, None])
    probs_low = probs.astype(jnp.bfloat16)
    text_values_grad = values_grad(probs_low, text_grad)
    layout_values_grad = values_grad(probs_low, layout_grad)
    text_mixed = jnp.einsum(
        "qhd,khd->hqk",
        heads_view(text_grad),
        heads_view(text_values),
        preferred_element_type=jnp.float32,
    )
    layout_mixed = jnp.einsum(
        "qhd,khd->hqk",
        heads_view(layout_grad),
        heads_view(layout_values),
        preferred_element_type=jnp.float32,
    )
    text_score_grad = softmax_back(probs, text_mixed)
    layout_score_grad = softmax_back(probs, layout_mixed)
    text_query_grad, text_keys_grad = query_keys_grad((text_score_grad,), text_query, text_keys)
    layout_query_grad, layout_keys_grad = query_keys_grad(
        (text_score_grad, layout_score_grad), layout_query, layout_keys
    )
    return (
        text_query_grad,
        text_keys_grad,
        text_values_grad,
        layout_query_grad,
        layout_keys_grad,
        layout_values_grad,
    )


def close_stream(inputs, attended, weights, width):
    attention_w, up_w, down_w, vector = weights
    parts = vector_parts(vector, width)
    after = matmul(attended, attention_w[3 * width :]) + parts[2]
    first, scaled_one, inverse_one = normalize(
        inputs.astype(jnp.float32) + after, parts[3], parts[4]
    )
    first_low = first.astype(jnp.bfloat16)
    upper = contract_cols(first_low, up_w) + parts[8]
    hidden_act = exact_gelu(upper).astype(jnp.bfloat16)
    final, scaled_two, inverse_two = normalize(
        first + matmul(hidden_act, down_w) + parts[5], parts[6], parts[7]
    )
    return (final, (scaled_one, inverse_one, first_low, upper, hidden_act, scaled_two, inverse_two))


def close_back(cotan, attended, saved, weights, width):
    scaled_one, inverse_one, first_low, upper, hidden_act, scaled_two, inverse_two = saved
    attention_w, up_w, down_w, vector = weights
    parts = vector_parts(vector, width)
    gain_two_grad = jnp.sum(cotan * scaled_two, 0)
    shift_two_grad = jnp.sum(cotan, 0)
    second_grad = norm_back(cotan, scaled_two, inverse_two, parts[6])
    branch_low = second_grad.astype(jnp.bfloat16)
    down_grad = contract_rows(hidden_act, branch_low)
    bias_down_grad = jnp.sum(branch_low.astype(jnp.float32), 0)
    act_grad = contract_cols(branch_low, down_w)
    gelu_back = jax.vjp(exact_gelu, upper)[1]
    upper_low = gelu_back(act_grad)[0].astype(jnp.bfloat16)
    up_grad_flipped = contract_rows(upper_low, first_low)
    bias_up_grad = jnp.sum(upper_low.astype(jnp.float32), 0)
    first_grad = second_grad + matmul(upper_low, up_w)
    gain_one_grad = jnp.sum(first_grad * scaled_one, 0)
    shift_one_grad = jnp.sum(first_grad, 0)
    resid_grad = norm_back(first_grad, scaled_one, inverse_one, parts[3])
    after_low = resid_grad.astype(jnp.bfloat16)
    out_weight_grad = contract_rows(attended, after_low)
    bias_out_grad = jnp.sum(after_low.astype(jnp.float32), 0)
    attended_grad = contract_cols(after_low, attention_w[3 * width :]).astype(jnp.bfloat16)
    tail = (
        bias_out_grad,
        gain_one_grad,
        shift_one_grad,
        bias_down_grad,
        gain_two_grad,
        shift_two_grad,
        bias_up_grad,
    )
    return (resid_grad, attended_grad, out_weight_grad, tail, up_grad_flipped, down_grad)


def open_back(
    inputs,
    resid_grad,
    query_grad,
    keys_grad,
    values_grad,
    out_weight_grad,
    tail,
    attention_w,
    width,
):
    stacked_grad = jnp.stack([query_grad, keys_grad, values_grad])
    weight_grad = jnp.einsum(
        "nd,jne->jde", inputs, stacked_grad, preferred_element_type=jnp.float32
    ).reshape(3 * width, width)
    input_grad = resid_grad + jnp.einsum(
        "jne,jde->nd",
        stacked_grad,
        attention_w[: 3 * width].reshape(3, width, width),
        preferred_element_type=jnp.float32,
    )
    bias_query_grad = jnp.sum(query_grad.astype(jnp.float32), 0)
    bias_value_grad = jnp.sum(values_grad.astype(jnp.float32), 0)
    (
        bias_out_grad,
        gain_one_grad,
        shift_one_grad,
        bias_down_grad,
        gain_two_grad,
        shift_two_grad,
        bias_up_grad,
    ) = tail
    vector_grad = jnp.concatenate(
        [
            bias_query_grad,
            bias_value_grad,
            bias_out_grad,
            gain_one_grad,
            shift_one_grad,
            bias_down_grad,
            gain_two_grad,
            shift_two_grad,
            bias_up_grad,
        ]
    )
    attention_grad = jnp.concatenate([weight_grad, out_weight_grad], 0)
    return (input_grad, attention_grad, vector_grad)


def by_stretch(array, stretches):
    return array.reshape((stretches, array.shape[0] // stretches) + array.shape[1:])


def shards(
    shape,
    text_in,
    layout_in,
    lengths,
    dup_rows,
    text_attention,
    text_up,
    text_down,
    text_vector,
    layout_attention,
    layout_up,
    layout_down,
    layout_vector,
    text_cotangent,
    layout_cotangent,
):
    count = shape["gx"] * shape["gy"]
    me = flat_index(shape["gy"])
    text_rows, layout_rows = text_attention.shape[0], layout_attention.shape[0]
    text_vec, layout_vec = text_vector.shape[0], layout_vector.shape[0]
    packed = pack_rows(
        text_attention,
        [layout_attention, layout_up.T, layout_down],
        jnp.concatenate([text_vector, layout_vector]),
    ).astype(jnp.bfloat16)
    gathered = gather_rows(packed, shape, me)
    up_all = gather_rows(text_up.T.astype(jnp.bfloat16), shape, me).reshape(-1, D)
    down_all = gather_rows(text_down.astype(jnp.bfloat16), shape, me).reshape(-1, D)
    text_all, layouts_all, text_vec_all, layout_vec_all = unpack_rows(
        gathered, text_rows, layout_rows, text_vec, layout_vec
    )
    text_weights = (text_all.reshape(-1, D), up_all, down_all, text_vec_all.reshape(-1))
    layout_weights = tuple(rows.reshape(-1, DL) for rows in layouts_all) + (
        layout_vec_all.reshape(-1),
    )
    stretches = lengths.shape[0]
    text_query, text_keys, text_values = open_stream(text_in, text_weights, D)
    layout_query, layout_keys, layout_values = open_stream(layout_in, layout_weights, DL)
    opened = (text_query, text_keys, text_values, layout_query, layout_keys, layout_values)
    opened_stretches = tuple((by_stretch(array, stretches) for array in opened))
    text_att, layout_att, log_total = lax.map(attend_forward, opened_stretches + (lengths,))
    text_att = text_att.reshape(-1, D)
    layout_att = layout_att.reshape(-1, DL)
    text_final, text_saved = close_stream(text_in, text_att, text_weights, D)
    layout_final, layout_saved = close_stream(layout_in, layout_att, layout_weights, DL)
    text_back, layout_back = text_weights, layout_weights
    span = text_in.shape[0] // stretches
    position = jnp.arange(span)
    keep = (position[None, :] < lengths[:, None]) & (dup_rows.reshape(stretches, span) == 0)
    keep = keep.reshape(-1, 1).astype(jnp.float32)
    text_cot = text_cotangent.astype(jnp.float32) * keep
    layout_cot = layout_cotangent.astype(jnp.float32) * keep
    text_resid, text_att_grad, text_out_w, text_tail, text_up_flipped, text_down_grad = close_back(
        text_cot, text_att, text_saved, text_back, D
    )
    (
        layout_resid,
        layout_att_grad,
        layout_out_w,
        layout_tail,
        layout_up_flipped,
        layout_down_grad,
    ) = close_back(layout_cot, layout_att, layout_saved, layout_back, DL)
    back_pieces = opened_stretches + (
        lengths,
        log_total,
        by_stretch(text_att_grad, stretches),
        by_stretch(layout_att_grad, stretches),
    )
    grads = lax.map(attend_backward, back_pieces)
    (
        text_query_grad,
        text_keys_grad,
        text_values_grad,
        layout_query_grad,
        layout_keys_grad,
        layout_values_grad,
    ) = tuple((array.reshape(-1, array.shape[-1]) for array in grads))
    text_input_grad, text_attention_grad, text_vector_grad = open_back(
        text_in,
        text_resid,
        text_query_grad,
        text_keys_grad,
        text_values_grad,
        text_out_w,
        text_tail,
        text_back[0],
        D,
    )
    layout_input_grad, layout_attention_grad, layout_vector_grad = open_back(
        layout_in,
        layout_resid,
        layout_query_grad,
        layout_keys_grad,
        layout_values_grad,
        layout_out_w,
        layout_tail,
        layout_back[0],
        DL,
    )

    def by_owner(array):
        return array.reshape((count, array.shape[0] // count) + array.shape[1:])

    attention_sum = scatter_rows(
        pack_rows(
            by_owner(text_attention_grad),
            [by_owner(g) for g in (layout_attention_grad, layout_up_flipped, layout_down_grad)],
            jnp.concatenate([by_owner(text_vector_grad), by_owner(layout_vector_grad)], -1),
        ).astype(jnp.bfloat16),
        shape,
        me,
    )
    up_sum = scatter_rows(by_owner(text_up_flipped).astype(jnp.bfloat16), shape, me)
    down_sum = scatter_rows(by_owner(text_down_grad).astype(jnp.bfloat16), shape, me)
    text_attention_sum, layout_sums, text_vec_sum, layout_vec_sum = unpack_rows(
        attention_sum, text_rows, layout_rows, text_vec, layout_vec
    )
    return (
        text_final.astype(jnp.bfloat16),
        layout_final.astype(jnp.bfloat16),
        text_input_grad.astype(jnp.bfloat16),
        layout_input_grad.astype(jnp.bfloat16),
        text_attention_sum,
        up_sum.T,
        down_sum,
        text_vec_sum,
        layout_sums[0],
        layout_sums[1].T,
        layout_sums[2],
        layout_vec_sum,
    )


BF = jnp.bfloat16
F32 = jnp.float32
CAT = 128
TEXT_LANES = D // HEADS
LAYOUT_LANES = DL // HEADS
MASK_LANE = TEXT_LANES + LAYOUT_LANES
VMEM_SPEC = pl.BlockSpec(memory_space=pltpu.VMEM)
SMEM_SPEC = pl.BlockSpec(memory_space=pltpu.SMEM)
ANY_SPEC = pl.BlockSpec(memory_space=pl.ANY)


def nn(left, right):
    return lax.dot_general(left, right, (((1,), (0,)), ((), ())), preferred_element_type=F32)


def nt(left, right):
    return lax.dot_general(left, right, (((1,), (1,)), ((), ())), preferred_element_type=F32)


def tn(left, right):
    return lax.dot_general(left, right, (((0,), (0,)), ((), ())), preferred_element_type=F32)


def row_mean(array):
    return jnp.sum(array, -1, keepdims=True) * (1.0 / array.shape[-1])


def col_sum(array):
    return jnp.sum(array, 0, keepdims=True)


def norm(resid):
    center = resid - row_mean(resid)
    inverse = lax.rsqrt(row_mean(center * center) + EPS)
    return center * inverse, inverse


def norm_grad(grad, scaled, inverse, gain):
    weighted = grad * gain
    return inverse * (weighted - row_mean(weighted) - scaled * row_mean(weighted * scaled))


def kernel_call(body, outs, ins, scratch=()):
    return pl.pallas_call(
        body,
        out_shape=[jax.ShapeDtypeStruct(shape, kind) for shape, kind, _ in outs],
        in_specs=[spec for _, spec in ins],
        out_specs=[spec for _, _, spec in outs],
        scratch_shapes=list(scratch),
        compiler_params=pltpu.CompilerParams(vmem_limit_bytes=60 * 2**20),
    )(*[array for array, _ in ins])


def stack_blocks(blocks):
    count, (_, rows, width) = len(blocks), blocks[0].shape

    def body(*refs):
        out, sems = refs[count], refs[count + 1]
        copies = [
            pltpu.make_async_copy(refs[index].at[0], out.at[index], sems.at[index])
            for index in range(count)
        ]
        for copy in copies:
            copy.start()
        for copy in copies:
            copy.wait()

    return kernel_call(
        body,
        [((count, rows, width), BF, ANY_SPEC)],
        [(block, VMEM_SPEC) for block in blocks],
        [pltpu.SemaphoreType.DMA((count,))],
    )[0]


def turn(dims, core_bit):
    (x, _), _, _, (y, _) = dims
    return (x, y) if core_bit else (y, x)


def swap_turn(array, dims, which, count):
    core = dims[1][0]
    return lax.ppermute(
        array,
        AXES,
        [(device, device ^ turn(dims, device // core % 2)[which]) for device in range(count)],
    )


def gather_pieces(shard, shape):
    count = shape["gx"] * shape["gy"]
    dims = exchange_dims(shape)
    _, (core, _), (z, nz), _ = dims

    blocks = [shard[None]]
    for step in range(1, nz):
        blocks.append(swap(blocks[0], z * step, count))
    held = stack_blocks(blocks)
    near = swap_turn(held, dims, 0, count)
    second = swap_turn(held, dims, 1, count)
    far = swap_turn(near, dims, 1, count)
    pieces = [held, near, second, far]
    for index in range(4):
        pieces.append(swap(pieces[index], core, count))
    return pieces


def offsets_of(me, dims):
    (x, _), (core, _), _, (y, _) = dims
    odd = me // core % 2
    first = jnp.where(odd == 1, x, y)
    second = jnp.where(odd == 1, y, x)
    return [0, first, second, x ^ y, core, core ^ second, core ^ first, core ^ x ^ y]


def fetch_blocks(me, dims, refs, place, sems):
    z, nz = dims[2]
    copies = []
    for offset, ref in zip(offsets_of(me, dims), refs):
        for index in range(nz):
            device = me ^ (offset ^ (z * index))
            for source, target in place(ref.at[index], device):
                copies.append(pltpu.make_async_copy(source, target, sems.at[len(copies)]))
    return copies


def send_blocks(me, dims, source, keep, send, sems, base):
    _, (core, _), (z, nz), _ = dims
    count = 4 * nz
    waits = []
    for device in range(2 * count):
        top, low = turn(dims, device // core % 2)
        away = me ^ device
        slot = (away // top % 2) * 2 * nz + (away // low % 2) * nz + away // z % nz
        far = away // core % 2
        sem = sems.at[base + device]

        @pl.when(far == 0)
        def _():
            pltpu.make_async_copy(source(device), keep.at[slot], sem).start()

        @pl.when(far == 1)
        def _():
            pltpu.make_async_copy(source(device), send.at[slot], sem).start()

        waits.append(pltpu.make_async_copy(source(device), keep.at[slot], sem))
    return waits


def added(terms, start, stop):
    total = terms[0][start:stop].astype(F32)
    for term in terms[1:]:
        total = total + term[start:stop].astype(F32)
    return total


def reduce_part(keep, send, dims, count):
    _, (core, _), (z, nz), _ = dims

    terms = [keep, swap(send, core, count)]
    for which in range(2):
        half = terms[0].shape[0] // 2 if which == 0 else nz
        got = swap_turn(added(terms, half, 2 * half).astype(BF), dims, which, count)
        terms.append(got)
        terms = [term[:half] for term in terms]
    result = added(terms, 0, 1)[0]
    for step in range(1, nz):
        got = swap(added(terms, step, step + 1)[0].astype(BF), z * step, count)
        result = result + got.astype(F32)
    return result


def vector_rows(read, width, segment, count):
    rows = []
    for row in range(segment * count // width):
        at, stop, parts = row * width, (row + 1) * width, []
        while at < stop:
            device, start = at // segment, at % segment
            take = min(segment - start, stop - at)
            parts.append(read(device, start, start + take))
            at += take
        rows.append(parts[0] if len(parts) == 1 else jnp.concatenate(parts, 1))
    return rows


def project(me, length, text_in, layout_in, pieces, sizes, dims):
    count, text_rows, layout_rows, text_vec, layout_vec = sizes
    rows = text_in.shape[0]
    packed = pieces[0].shape[1]

    def body(*refs):
        me_ref, length_ref, x_ref, xl_ref = refs[:4]
        piece_refs = refs[4 : 4 + len(pieces)]
        (
            q_ref,
            k_ref,
            v_ref,
            weight_out,
            layout_ref,
            up_ref,
            down_ref,
            text_vec_ref,
            layout_vec_ref,
            weight,
            tail,
            sems,
            out_sem,
        ) = refs[4 + len(pieces) :]
        mine = me_ref[0]

        def place(source, device):
            base = pl.multiple_of(device * text_rows, 16)
            return [
                (source.at[0:text_rows], weight.at[pl.ds(base, text_rows)]),
                (source.at[text_rows:packed], tail.at[device]),
            ]

        copies = fetch_blocks(mine, dims, piece_refs, place, sems)
        for copy in copies:
            copy.start()
        for copy in copies:
            copy.wait()
        out_copy = pltpu.make_async_copy(weight, weight_out, out_sem)
        out_copy.start()
        side = D // 3
        for device in range(count):
            block = pl.ds(device * layout_rows, layout_rows)
            for index, ref in enumerate((layout_ref, up_ref, down_ref)):
                ref[block, :] = tail[device, 0:layout_rows, side * index : side * index + DL]

        def read_text(device, start, stop):
            return tail[device, layout_rows : layout_rows + 1, start:stop].astype(F32)

        def read_layout(device, start, stop):
            return read_text(device, text_vec + start, text_vec + stop)

        for index, row in enumerate(vector_rows(read_text, D, text_vec, count)):
            text_vec_ref[index] = row
        for index, row in enumerate(vector_rows(read_layout, DL, layout_vec, count)):
            layout_vec_ref[index] = row
        x, xl = x_ref[...], xl_ref[...]
        seen = lax.broadcasted_iota(jnp.int32, (rows, CAT - MASK_LANE), 0) < length_ref[0]
        lane = lax.broadcasted_iota(jnp.int32, (rows, CAT - MASK_LANE), 1)
        ones = jnp.where(lane == 0, 1.0, 0.0).astype(BF)
        hidden = jnp.where((lane == 0) & jnp.logical_not(seen), NEG, 0.0).astype(BF)
        nothing = jnp.zeros((rows, CAT - MASK_LANE), BF)
        for index, (ref, extra) in enumerate(((q_ref, ones), (k_ref, hidden), (v_ref, nothing))):
            text = nn(x, weight[index * D : (index + 1) * D, :])
            layout = nn(xl, layout_ref[index * DL : (index + 1) * DL, :])
            if index != 1:
                text = text + text_vec_ref[index // 2]
                layout = layout + layout_vec_ref[index // 2]
            text, layout = text.astype(BF), layout.astype(BF)
            if index == 0:
                text = text * (1.0 / math.sqrt(TEXT_LANES))
                layout = layout * (1.0 / math.sqrt(LAYOUT_LANES))
            for head in range(HEADS):
                ref[head] = jnp.concatenate(
                    [
                        text[:, TEXT_LANES * head : TEXT_LANES * (head + 1)],
                        layout[:, LAYOUT_LANES * head : LAYOUT_LANES * (head + 1)],
                        extra,
                    ],
                    1,
                )
        out_copy.wait()

    cat = ((HEADS, rows, CAT), BF, VMEM_SPEC)
    return kernel_call(
        body,
        [
            cat,
            cat,
            cat,
            ((4 * D, D), BF, ANY_SPEC),
            ((4 * DL, DL), BF, VMEM_SPEC),
            ((FFL, DL), BF, VMEM_SPEC),
            ((FFL, DL), BF, VMEM_SPEC),
            ((12, 1, D), F32, VMEM_SPEC),
            ((12, 1, DL), F32, VMEM_SPEC),
        ],
        [(me, SMEM_SPEC), (length, SMEM_SPEC), (text_in, VMEM_SPEC), (layout_in, VMEM_SPEC)]
        + [(array, ANY_SPEC) for array in pieces],
        [
            pltpu.VMEM((4 * D, D), BF),
            pltpu.VMEM((count, packed - text_rows, D), BF),
            pltpu.SemaphoreType.DMA((2 * count,)),
            pltpu.SemaphoreType.DMA,
        ],
    )


def heads_out(ref):
    heads = range(ref.shape[0])
    text = jnp.concatenate([ref[head, :, 0:TEXT_LANES] for head in heads], 1)
    layout = jnp.concatenate([ref[head, :, TEXT_LANES:MASK_LANE] for head in heads], 1)
    return text, layout


def attend(text_in, layout_in, query, keys, values, weight, layout_w, text_vec, layout_vec):
    rows = text_in.shape[0]

    def body(
        x_ref,
        xl_ref,
        q_ref,
        k_ref,
        v_ref,
        weight_any,
        layout_ref,
        tv_ref,
        lv_ref,
        out_t,
        out_l,
        lse_ref,
        norm_t,
        inv_t,
        norm_l,
        inv_l,
        mixed,
        weight,
        sem,
    ):
        fetch = pltpu.make_async_copy(weight_any.at[3 * D : 4 * D], weight, sem)
        fetch.start()

        def head_step(head, carry):
            scores = nt(k_ref[head], q_ref[head])
            top = jnp.max(scores, 0, keepdims=True)
            expo = jnp.exp(scores - top)
            total = col_sum(expo)
            probs = (expo * (1.0 / total)).astype(BF)
            mixed[head] = tn(v_ref[head], probs).T.astype(BF)
            lse_ref[head] = top + jnp.log(total)
            return carry

        lax.fori_loop(0, HEADS, head_step, 0)
        text, layout = heads_out(mixed)
        out_t[...] = text
        out_l[...] = layout
        fetch.wait()
        after = nn(text, weight[...]) + tv_ref[2]
        norm_t[...], inv_t[...] = norm(x_ref[...].astype(F32) + after)
        after = nn(layout, layout_ref[3 * DL : 4 * DL, :]) + lv_ref[2]
        norm_l[...], inv_l[...] = norm(xl_ref[...].astype(F32) + after)

    return kernel_call(
        body,
        [
            ((rows, D), BF, VMEM_SPEC),
            ((rows, DL), BF, VMEM_SPEC),
            ((HEADS, 1, rows), F32, VMEM_SPEC),
            ((rows, D), F32, VMEM_SPEC),
            ((rows, 1), F32, VMEM_SPEC),
            ((rows, DL), F32, VMEM_SPEC),
            ((rows, 1), F32, VMEM_SPEC),
        ],
        [
            (text_in, VMEM_SPEC),
            (layout_in, VMEM_SPEC),
            (query, VMEM_SPEC),
            (keys, VMEM_SPEC),
            (values, VMEM_SPEC),
            (weight, ANY_SPEC),
            (layout_w, VMEM_SPEC),
            (text_vec, VMEM_SPEC),
            (layout_vec, VMEM_SPEC),
        ],
        [pltpu.VMEM((HEADS, rows, CAT), BF), pltpu.VMEM((D, D), BF), pltpu.SemaphoreType.DMA],
    )


def erf_of(value):
    value = jnp.clip(value, -4.0, 4.0)
    square = value * value
    top = jnp.full_like(square, -2.72614225801306e-10)
    for factor in (
        2.77068142495902e-08,
        -2.10102402082508e-06,
        -5.69250639462346e-05,
        -7.34990630326855e-04,
        -2.95459980854025e-03,
        -1.60960333262415e-02,
    ):
        top = top * square + factor
    low = jnp.full_like(square, -1.45660718464996e-05)
    for factor in (
        -2.13374055278905e-04,
        -1.68282697438203e-03,
        -7.37332916720468e-03,
        -1.42647390514189e-02,
    ):
        low = low * square + factor
    return value * top / low


def gelu_both(value):
    below = 0.5 * (1.0 + erf_of(value * math.sqrt(0.5)))
    density = jnp.exp(value * value * -0.5) * (1.0 / math.sqrt(2.0 * math.pi))
    return value * below, below + value * density


def feed_stream(norm_ref, vec_ref, cot_ref, keep, up, down, hidden, slope, blocks, write, outs):
    out_ref, grad_ref, vec_out = outs
    first = norm_ref[...] * vec_ref[3] + vec_ref[4]
    low = first.astype(BF)

    def forward(block, total):
        upper = nt(low, up(block)) + vec_ref[8 + block]
        act, rise = gelu_both(upper)
        act = act.astype(BF)
        hidden[block] = act
        slope[block] = rise
        return total + nn(act, down(block))

    branch = lax.fori_loop(0, blocks, forward, jnp.zeros_like(first))
    scaled, inverse = norm(first + branch + vec_ref[5])
    out_ref[...] = (scaled * vec_ref[6] + vec_ref[7]).astype(BF)
    cotan = cot_ref[...].astype(F32) * keep
    vec_out[1] = col_sum(cotan * scaled)
    vec_out[2] = col_sum(cotan)
    second = norm_grad(cotan, scaled, inverse, vec_ref[6])
    branch_low = second.astype(BF)
    vec_out[0] = col_sum(branch_low.astype(F32))

    def backward(block, total):
        act_grad = nt(branch_low, down(block))
        upper_low = (act_grad * slope[block]).astype(BF)
        vec_out[3 + block] = col_sum(upper_low.astype(F32))
        write(block, tn(upper_low, low), tn(hidden[block], branch_low))
        return total + nn(upper_low, up(block))

    grad_ref[...] = lax.fori_loop(0, blocks, backward, second)


def feed(me, keep_rows, norm_t, norm_l, tv, lv, cot_t, cot_l, pieces, lu, ld, dims, text_rows):
    rows = norm_t.shape[0]
    count = 8 * dims[2][1]
    blocks = FF // D

    def body(*refs):
        me_ref, keep_ref, nt_ref, nl_ref, tv_ref, lv_ref, ct_ref, cl_ref, lu_ref, ld_ref = refs[:10]
        piece_refs = refs[10 : 10 + len(pieces)]
        (
            out_t,
            out_l,
            grad_t,
            grad_l,
            vec_t,
            vec_l,
            lu_grad,
            ld_grad,
            both_keep,
            both_send,
            up,
            down,
            hidden,
            slope,
            hidden_l,
            slope_l,
            grads,
            sems,
        ) = refs[10 + len(pieces) :]
        mine = me_ref[0]

        def place(source, device):
            at = pl.ds(pl.multiple_of(device * text_rows, 16), text_rows)
            return [
                (source.at[0:text_rows], up.at[at]),
                (source.at[text_rows : 2 * text_rows], down.at[at]),
            ]

        copies = fetch_blocks(mine, dims, piece_refs, place, sems)
        for copy in copies:
            copy.start()
        keep = keep_ref[...]

        def rows_of(ref, size):
            return lambda block: ref[pl.ds(pl.multiple_of(block * size, 8), size), :]

        def write_l(block, one, two):
            at = pl.ds(pl.multiple_of(block * DL, 8), DL)
            lu_grad[at, :] = one.astype(BF)
            ld_grad[at, :] = two.astype(BF)

        feed_stream(
            nl_ref,
            lv_ref,
            cl_ref,
            keep,
            rows_of(lu_ref, DL),
            rows_of(ld_ref, DL),
            hidden_l,
            slope_l,
            FFL // DL,
            write_l,
            (out_l, grad_l, vec_l),
        )
        for copy in copies:
            copy.wait()

        per_block = D // text_rows

        def write_t(block, one, two):
            for part in range(per_block):
                at = slice(part * text_rows, (part + 1) * text_rows)
                grads[block * per_block + part, 0:text_rows] = one[at].astype(BF)
                grads[block * per_block + part, text_rows:] = two[at].astype(BF)

        feed_stream(
            nt_ref,
            tv_ref,
            ct_ref,
            keep,
            rows_of(up, D),
            rows_of(down, D),
            hidden,
            slope,
            blocks,
            write_t,
            (out_t, grad_t, vec_t),
        )
        waits = send_blocks(
            mine, dims, lambda device: grads.at[device], both_keep, both_send, sems, 0
        )
        for wait in waits:
            wait.wait()

    part = ((count // 2, 2 * text_rows, D), BF, ANY_SPEC)
    return kernel_call(
        body,
        [
            ((rows, D), BF, VMEM_SPEC),
            ((rows, DL), BF, VMEM_SPEC),
            ((rows, D), F32, VMEM_SPEC),
            ((rows, DL), F32, VMEM_SPEC),
            ((3 + blocks, 1, D), F32, VMEM_SPEC),
            ((3 + blocks, 1, DL), F32, VMEM_SPEC),
            ((FFL, DL), BF, VMEM_SPEC),
            ((FFL, DL), BF, VMEM_SPEC),
            part,
            part,
        ],
        [
            (me, SMEM_SPEC),
            (keep_rows, VMEM_SPEC),
            (norm_t, VMEM_SPEC),
            (norm_l, VMEM_SPEC),
            (tv, VMEM_SPEC),
            (lv, VMEM_SPEC),
            (cot_t, VMEM_SPEC),
            (cot_l, VMEM_SPEC),
            (lu, VMEM_SPEC),
            (ld, VMEM_SPEC),
        ]
        + [(array, ANY_SPEC) for array in pieces],
        [
            pltpu.VMEM((FF, D), BF),
            pltpu.VMEM((FF, D), BF),
            pltpu.VMEM((blocks, rows, D), BF),
            pltpu.VMEM((blocks, rows, D), F32),
            pltpu.VMEM((FFL // DL, rows, DL), BF),
            pltpu.VMEM((FFL // DL, rows, DL), F32),
            pltpu.VMEM((count, 2 * text_rows, D), BF),
            pltpu.SemaphoreType.DMA((2 * count,)),
        ],
    )


def close_back_pair(grad_t, grad_l, norms, outs, weight, layout_w, tv, lv):
    rows = grad_t.shape[0]
    norm_t, inv_t, norm_l, inv_l = norms
    out_t, out_l = outs

    def body(
        gt_ref,
        gl_ref,
        nt_ref,
        it_ref,
        nl_ref,
        il_ref,
        ot_ref,
        ol_ref,
        weight_any,
        layout_ref,
        tv_ref,
        lv_ref,
        resid_t,
        resid_l,
        out_wt,
        out_wl,
        vec_t,
        vec_l,
        dout,
        weight,
        sem,
    ):
        fetch = pltpu.make_async_copy(weight_any.at[3 * D : 4 * D], weight, sem)
        fetch.start()

        def close(grad, scaled, inverse, vec, mixed, vec_out, resid_ref, wide):
            vec_out[1] = col_sum(grad * scaled)
            vec_out[2] = col_sum(grad)
            resid = norm_grad(grad, scaled, inverse, vec[3])
            resid_ref[...] = resid
            after = resid.astype(BF)
            vec_out[0] = col_sum(after.astype(F32))
            return after, tn(mixed, after).astype(BF), nt(after, wide()).astype(BF)

        def wide_l():
            return layout_ref[3 * DL : 4 * DL, :]

        def wide_t():
            fetch.wait()
            return weight[...]

        _, out_wl[...], att_l = close(
            gl_ref[...], nl_ref[...], il_ref[...], lv_ref, ol_ref[...], vec_l, resid_l, wide_l
        )
        _, out_wt[...], att_t = close(
            gt_ref[...], nt_ref[...], it_ref[...], tv_ref, ot_ref[...], vec_t, resid_t, wide_t
        )
        nothing = jnp.zeros((rows, CAT - MASK_LANE), BF)
        for head in range(HEADS):
            dout[head] = jnp.concatenate(
                [
                    att_t[:, TEXT_LANES * head : TEXT_LANES * (head + 1)],
                    att_l[:, LAYOUT_LANES * head : LAYOUT_LANES * (head + 1)],
                    nothing,
                ],
                1,
            )

    return kernel_call(
        body,
        [
            ((rows, D), F32, VMEM_SPEC),
            ((rows, DL), F32, VMEM_SPEC),
            ((D, D), BF, VMEM_SPEC),
            ((DL, DL), BF, VMEM_SPEC),
            ((3, 1, D), F32, VMEM_SPEC),
            ((3, 1, DL), F32, VMEM_SPEC),
            ((HEADS, rows, CAT), BF, VMEM_SPEC),
        ],
        [
            (grad_t, VMEM_SPEC),
            (grad_l, VMEM_SPEC),
            (norm_t, VMEM_SPEC),
            (inv_t, VMEM_SPEC),
            (norm_l, VMEM_SPEC),
            (inv_l, VMEM_SPEC),
            (out_t, VMEM_SPEC),
            (out_l, VMEM_SPEC),
            (weight, ANY_SPEC),
            (layout_w, VMEM_SPEC),
            (tv, VMEM_SPEC),
            (lv, VMEM_SPEC),
        ],
        [pltpu.VMEM((D, D), BF), pltpu.SemaphoreType.DMA],
    )


def heads_back(query, keys, values, lse, dout, start, stop):
    rows = query.shape[1]
    size = stop - start

    def body(q_any, k_any, v_any, lse_any, do_any, dq, dk, dv, q_ref, k_ref, v_ref, do_ref, lse_ref, sems):
        copies = [
            pltpu.make_async_copy(source.at[start:stop], target, sems.at[index])
            for index, (source, target) in enumerate(
                (
                    (q_any, q_ref),
                    (k_any, k_ref),
                    (v_any, v_ref),
                    (do_any, do_ref),
                    (lse_any, lse_ref),
                )
            )
        ]
        for copy in copies:
            copy.start()
        for copy in copies:
            copy.wait()
        is_text = lax.broadcasted_iota(jnp.int32, (rows, CAT), 1) < TEXT_LANES
        text_row = lax.broadcasted_iota(jnp.int32, (CAT, rows), 0) < TEXT_LANES

        def head_step(head, carry):
            q, k, v, do = q_ref[head], k_ref[head], v_ref[head], do_ref[head]
            probs = jnp.exp(nt(k, q) - lse_ref[head])
            dv[head] = nn(probs.astype(BF), do).astype(BF)
            none = jnp.zeros_like(v)
            mixed = nt(jnp.where(is_text, v, none), do)
            score_t = (probs * (mixed - col_sum(probs * mixed))).astype(BF)
            mixed = nt(jnp.where(is_text, none, v), do)
            score_l = (probs * (mixed - col_sum(probs * mixed))).astype(BF)
            dk_t = nn(score_t, q)
            dk_l = nn(score_l, q)
            dk[head] = jnp.where(is_text, dk_t, dk_t + dk_l).astype(BF)
            dq_t = tn(k, score_t)
            dq_l = tn(k, score_l)
            scaled = jnp.where(
                text_row,
                dq_t * (1.0 / math.sqrt(TEXT_LANES)),
                (dq_t + dq_l) * (1.0 / math.sqrt(LAYOUT_LANES)),
            )
            dq[head] = scaled.T.astype(BF)
            return carry

        lax.fori_loop(0, size, head_step, 0)

    cat = pltpu.VMEM((size, rows, CAT), BF)
    part = ((size, rows, CAT), BF, VMEM_SPEC)
    return kernel_call(
        body,
        [part, part, part],
        [(array, ANY_SPEC) for array in (query, keys, values, lse, dout)],
        [cat, cat, cat, cat, pltpu.VMEM((size, 1, rows), F32), pltpu.SemaphoreType.DMA((5,))],
    )


def weight_grads(me, text_in, layout_in, backs, out_w, ffn_l, vecs, dims, sizes):
    count, text_rows, layout_rows, text_vec, layout_vec = sizes
    rows = text_in.shape[0]
    packed = text_rows + layout_rows + 8
    groups = len(backs)

    def body(*refs):
        me_ref, x_ref, xl_ref = refs[:3]
        back_refs = refs[3 : 3 + 3 * groups]
        (
            out_wt,
            out_wl,
            lu_grad,
            ld_grad,
            close_t,
            close_l,
            feed_t,
            feed_l,
            joined_t,
            joined_l,
            keep,
            send,
            pack,
            att_l,
            sems,
        ) = refs[3 + 3 * groups :]
        mine = me_ref[0]
        x, xl = x_ref[...], xl_ref[...]
        side = D // 3
        for device in range(count):
            pack[device, text_rows : text_rows + layout_rows, :] = jnp.zeros((layout_rows, D), BF)
        per_block = D // text_rows
        for index in range(3):
            pieces = [heads_out(back_refs[3 * group + index]) for group in range(groups)]
            joined_t[index] = jnp.concatenate([text for text, _ in pieces], 1)
            joined_l[index] = jnp.concatenate([layout for _, layout in pieces], 1)
            grad = tn(x, joined_t[index]).astype(BF)
            for part in range(per_block):
                pack[index * per_block + part, 0:text_rows, :] = grad[
                    part * text_rows : (part + 1) * text_rows
                ]
            att_l[index * DL : (index + 1) * DL, :] = tn(xl, joined_l[index]).astype(BF)
        for part in range(per_block):
            pack[3 * per_block + part, 0:text_rows, :] = out_wt[
                part * text_rows : (part + 1) * text_rows, :
            ]
        att_l[3 * DL : 4 * DL, :] = out_wl[...]
        for device in range(count):
            block = pl.ds(device * layout_rows, layout_rows)
            for index, ref in enumerate((att_l, lu_grad, ld_grad)):
                pack[
                    device,
                    text_rows : text_rows + layout_rows,
                    side * index : side * index + DL,
                ] = ref[block, :]

        def vector(joined, close, feeds):
            rows_of = [col_sum(joined[0].astype(F32)), col_sum(joined[2].astype(F32))]
            rows_of += [close[0], close[1], close[2], feeds[0], feeds[1], feeds[2]]
            return rows_of + [feeds[3 + block] for block in range(FF // D)]

        text_rows_of = vector(joined_t, close_t, feed_t)
        layout_rows_of = vector(joined_l, close_l, feed_l)

        def segment(all_rows, width, start, size):
            parts, stop = [], start + size
            while start < stop:
                row, at = start // width, start % width
                take = min(width - at, stop - start)
                parts.append(all_rows[row][:, at : at + take])
                start += take
            return parts

        row = lax.broadcasted_iota(jnp.int32, (8, D), 0)
        for device in range(count):
            parts = segment(text_rows_of, D, device * text_vec, text_vec)
            parts += segment(layout_rows_of, DL, device * layout_vec, layout_vec)
            parts.append(jnp.zeros((1, D - text_vec - layout_vec), F32))
            line = jnp.concatenate(parts, 1)
            pack[device, text_rows + layout_rows :, :] = jnp.where(
                row == 0, jnp.broadcast_to(line, (8, D)), 0.0
            ).astype(BF)
        waits = send_blocks(mine, dims, lambda device: pack.at[device], keep, send, sems, 0)
        for wait in waits:
            wait.wait()

    part = ((count // 2, packed, D), BF, ANY_SPEC)
    arrays = [text_in, layout_in]
    for back in backs:
        arrays += list(back)
    arrays += [*out_w, *ffn_l, *vecs]
    return kernel_call(
        body,
        [((3, rows, D), BF, VMEM_SPEC), ((3, rows, DL), BF, VMEM_SPEC), part, part],
        [(me, SMEM_SPEC)] + [(array, VMEM_SPEC) for array in arrays],
        [
            pltpu.VMEM((count, packed, D), BF),
            pltpu.VMEM((4 * DL, DL), BF),
            pltpu.SemaphoreType.DMA((count,)),
        ],
    )


def input_grads(joined_t, joined_l, resid_t, resid_l, weight, layout_w):
    rows = resid_t.shape[0]

    def body(jt, jl, rt, rl, weight_any, layout_ref, grad_t, grad_l, weight, sem):
        fetch = pltpu.make_async_copy(weight_any.at[0 : 3 * D], weight, sem)
        fetch.start()
        total = rl[...]
        for index in range(3):
            total = total + nt(jl[index], layout_ref[index * DL : (index + 1) * DL, :])
        grad_l[...] = total.astype(BF)
        fetch.wait()
        total = rt[...]
        for index in range(3):
            total = total + nt(jt[index], weight[index * D : (index + 1) * D, :])
        grad_t[...] = total.astype(BF)

    return kernel_call(
        body,
        [((rows, D), BF, VMEM_SPEC), ((rows, DL), BF, VMEM_SPEC)],
        [(array, VMEM_SPEC) for array in (joined_t, joined_l, resid_t, resid_l)]
        + [(weight, ANY_SPEC), (layout_w, VMEM_SPEC)],
        [pltpu.VMEM((3 * D, D), BF), pltpu.SemaphoreType.DMA],
    )


def shards_fast(
    shape,
    text_in,
    layout_in,
    lengths,
    dup_rows,
    text_attention,
    text_up,
    text_down,
    text_vector,
    layout_attention,
    layout_up,
    layout_down,
    layout_vector,
    text_cotangent,
    layout_cotangent,
):
    count = shape["gx"] * shape["gy"]
    dims = exchange_dims(shape)
    me = flat_index(shape["gy"]).reshape(1).astype(jnp.int32)
    text_rows, layout_rows = text_attention.shape[0], layout_attention.shape[0]
    text_vec, layout_vec = text_vector.shape[0], layout_vector.shape[0]
    packed = pack_rows(
        text_attention,
        [layout_attention, layout_up.T, layout_down],
        jnp.concatenate([text_vector, layout_vector]),
    ).astype(BF)
    sizes = (count, text_rows, layout_rows, text_vec, layout_vec)
    parts = gather_pieces(packed, shape)
    feed_shard = jnp.concatenate([text_up.T, text_down], 0).astype(BF)
    feed_parts = gather_pieces(feed_shard, shape)
    q, k, v, weight, layout_w, lu, ld, tv, lv = project(
        me, lengths, text_in, layout_in, parts, sizes, dims
    )
    out_t, out_l, lse, norm_t, inv_t, norm_l, inv_l = attend(
        text_in, layout_in, q, k, v, weight, layout_w, tv, lv
    )
    span = text_in.shape[0]
    keep = (jnp.arange(span) < lengths[0]) & (dup_rows == 0)
    keep = keep.astype(F32)[:, None]
    (
        text_final,
        layout_final,
        grad_t,
        grad_l,
        feed_vt,
        feed_vl,
        lu_grad,
        ld_grad,
        both_keep,
        both_send,
    ) = feed(
        me,
        keep,
        norm_t,
        norm_l,
        tv,
        lv,
        text_cotangent,
        layout_cotangent,
        feed_parts,
        lu,
        ld,
        dims,
        text_rows,
    )
    resid_t, resid_l, out_wt, out_wl, close_t, close_l, dout = close_back_pair(
        grad_t, grad_l, (norm_t, inv_t, norm_l, inv_l), (out_t, out_l), weight, layout_w, tv, lv
    )
    middle = HEADS // 2
    backs = [
        heads_back(q, k, v, lse, dout, 0, middle), heads_back(q, k, v, lse, dout, middle, HEADS)
    ]
    joined_t, joined_l, keep_packed, send_packed = weight_grads(
        me,
        text_in,
        layout_in,
        backs,
        (out_wt, out_wl),
        (lu_grad, ld_grad),
        (close_t, close_l, feed_vt, feed_vl),
        dims,
        sizes,
    )
    text_input_grad, layout_input_grad = input_grads(
        joined_t, joined_l, resid_t, resid_l, weight, layout_w
    )
    both_sum = reduce_part(both_keep, both_send, dims, count)
    up_sum, down_sum = both_sum[:text_rows], both_sum[text_rows:]
    packed_sum = reduce_part(keep_packed, send_packed, dims, count)
    text_sum, layout_sums, text_vec_sum, layout_vec_sum = unpack_rows(
        packed_sum, text_rows, layout_rows, text_vec, layout_vec
    )
    return (
        text_final,
        layout_final,
        text_input_grad,
        layout_input_grad,
        text_sum,
        up_sum.T,
        down_sum,
        text_vec_sum,
        layout_sums[0],
        layout_sums[1].T,
        layout_sums[2],
        layout_vec_sum,
    )


def fits(shape):
    (_, nx), (_, ncore), (_, nz), (_, ny) = exchange_dims(shape)
    count = shape["gx"] * shape["gy"]
    return (
        (nx, ncore, ny) == (2, 2, 2)
        and (4 * D) % (16 * count) == 0
        and (4 * DL) % (8 * count) == 0
        and D % (4 * D // count) == 0
    )


def layer(fast, shape, *arrays):
    if not fast or arrays[2].shape[0] != 1:
        return shards(shape, *arrays)
    return shards_fast(shape, *arrays)


def solution(mesh):
    placed = (
        P(("gx", "gy"), None),
        P(("gx", "gy"), None),
        P(("gx", "gy")),
        P(("gx", "gy")),
        P(("gx", "gy"), None),
        P(None, ("gx", "gy")),
        P(("gx", "gy"), None),
        P(("gx", "gy")),
        P(("gx", "gy"), None),
        P(None, ("gx", "gy")),
        P(("gx", "gy"), None),
        P(("gx", "gy")),
        P(("gx", "gy"), None),
        P(("gx", "gy"), None),
    )
    shape = dict(mesh.shape)
    fast = fits(shape)
    return jax.shard_map(
        functools.partial(layer, fast, shape),
        mesh=mesh,
        in_specs=placed,
        out_specs=(
            P(("gx", "gy"), None),
            P(("gx", "gy"), None),
            P(("gx", "gy"), None),
            P(("gx", "gy"), None),
            P(("gx", "gy"), None),
            P(None, ("gx", "gy")),
            P(("gx", "gy"), None),
            P(("gx", "gy")),
            P(("gx", "gy"), None),
            P(None, ("gx", "gy")),
            P(("gx", "gy"), None),
            P(("gx", "gy")),
        ),
        check_vma=False,
    )
```

```python
import functools
import math

import jax
import jax.numpy as jnp
from jax import lax
from jax.experimental import pallas as pl
from jax.experimental.pallas import tpu as pltpu
from jax.sharding import PartitionSpec as P


AXES = ("gx", "gy")


def exchange_dims(shape):
    gx, gy = shape["gx"], shape["gy"]
    outer = {8: 4, 32: 4}.get(gy, gy)
    inner = gy // outer
    core = 2 if gx % 2 == 0 else 1
    core_dim = (gy, core)
    x_dim = (gy * core, gx // core)
    if inner <= outer:
        z_dim, y_dim = (inner, outer), (1, inner)
    else:
        z_dim, y_dim = (1, inner), (inner, outer)
    return x_dim, core_dim, z_dim, y_dim


def orders(shape):
    x_dim, core_dim, z_dim, y_dim = exchange_dims(shape)
    return ((z_dim, y_dim, x_dim, core_dim), (z_dim, x_dim, y_dim, core_dim))


def offsets(order):
    table = [0]
    for stride, size in order:
        table = [offset ^ (stride * step) for step in range(size) for offset in table]
    return table


def swap(array, offset, count):
    return lax.ppermute(array, AXES, [(device, device ^ offset) for device in range(count)])


def gather_part(part, order, count):
    held = part[None]
    for stride, size in order:
        pieces = [held] + [swap(held, stride * step, count) for step in range(1, size)]
        held = jnp.concatenate(pieces, 0)
    return held


def scatter_part(parts, order, count):
    held = parts
    for stride, size in reversed(order):
        held = held.reshape((size, held.shape[0] // size) + held.shape[1:])
        total = held[0].astype(jnp.float32)
        for step in range(1, size):
            total = total + swap(held[step], stride * step, count).astype(jnp.float32)
        last = (stride, size) == order[0]
        held = total if last else total.astype(jnp.bfloat16)
    return held[0]


def flat_index(gy):
    return lax.axis_index("gx") * gy + lax.axis_index("gy")


def positions(order, count):
    table = offsets(order)
    inverse = [0] * count
    for position, offset in enumerate(table):
        inverse[offset] = position
    return jnp.array(table, jnp.int32), jnp.array(inverse, jnp.int32)


def gather_rows(shard, shape, me):
    count = shape["gx"] * shape["gy"]
    half = shard.shape[0] // 2
    pieces = []
    for index, order in enumerate(orders(shape)):
        held = gather_part(shard[index * half : (index + 1) * half], order, count)
        inverse = positions(order, count)[1]
        pieces.append(jnp.take(held, inverse[jnp.arange(count) ^ me], axis=0))
    return jnp.concatenate(pieces, 1)


def scatter_rows(grads, shape, me):
    count = shape["gx"] * shape["gy"]
    half = grads.shape[1] // 2
    pieces = []
    for index, order in enumerate(orders(shape)):
        table = positions(order, count)[0]
        parts = jnp.take(grads[:, index * half : (index + 1) * half], me ^ table, axis=0)
        pieces.append(scatter_part(parts, order, count))
    return jnp.concatenate(pieces, 0)


def pad_cols(array, width):
    return jnp.pad(array, ((0, 0),) * (array.ndim - 1) + ((0, width - array.shape[-1]),))


def pack_rows(text_rows, layout_rows, vectors):
    side = D // 3
    layouts = jnp.concatenate([pad_cols(rows, side) for rows in layout_rows], -1)
    packed = jnp.concatenate([text_rows, layouts, pad_cols(vectors, D)[..., None, :]], -2)
    rows = packed.shape[-2]
    extra = -rows % 16
    return jnp.pad(packed, ((0, 0),) * (packed.ndim - 2) + ((0, extra), (0, 0)))


def unpack_rows(packed, text_rows, layout_rows, text_vec, layout_vec):
    side = D // 3
    text = packed[..., :text_rows, :]
    block = packed[..., text_rows : text_rows + layout_rows, :]
    layouts = [block[..., side * index : side * index + DL] for index in range(3)]
    vectors = packed[..., text_rows + layout_rows, :]
    return text, layouts, vectors[..., :text_vec], vectors[..., text_vec : text_vec + layout_vec]


D = 768
DL = 192
HEADS = 12
FF = 4 * D
FFL = 4 * DL


EPS = 1e-05
NEG = -1e30


def matmul(left, right):
    return jnp.dot(left, right, preferred_element_type=jnp.float32)


def contract_rows(left, right):
    return lax.dot_general(
        left, right, (((0,), (0,)), ((), ())), preferred_element_type=jnp.float32
    )


def contract_cols(left, right):
    return lax.dot_general(
        left, right, (((1,), (1,)), ((), ())), preferred_element_type=jnp.float32
    )


def vector_parts(vector, width):
    values = vector.astype(jnp.float32)
    return [values[index * width : (index + 1) * width] for index in range(8)] + [
        values[8 * width :]
    ]


def normalize(resid, gain, shift):
    center = resid - jnp.mean(resid, -1, keepdims=True)
    varian = jnp.mean(center * center, -1, keepdims=True)
    inverse = lax.rsqrt(varian + EPS)
    scaled = center * inverse
    return (scaled * gain + shift, scaled, inverse)


def norm_back(grad, scaled, inverse, gain):
    weighted = grad * gain
    inner = jnp.mean(weighted, -1, keepdims=True)
    across = jnp.mean(weighted * scaled, -1, keepdims=True)
    return inverse * (weighted - inner - scaled * across)


def exact_gelu(value):
    return jax.nn.gelu(value, approximate=False)


def open_stream(inputs, weights, width):
    parts = vector_parts(weights[3], width)
    stacked = weights[0][: 3 * width].reshape(3, width, width)
    projected = jnp.einsum("nd,jde->jne", inputs, stacked, preferred_element_type=jnp.float32)
    query = (projected[0] + parts[0]).astype(jnp.bfloat16)
    keys = projected[1].astype(jnp.bfloat16)
    values = (projected[2] + parts[1]).astype(jnp.bfloat16)
    return (query, keys, values)


def heads_view(array):
    return array.reshape(array.shape[0], HEADS, array.shape[1] // HEADS)


def head_scale(array):
    return 1.0 / math.sqrt(array.shape[1] // HEADS)


def joint_scores(text_query, text_keys, layout_query, layout_keys, length):
    rows = text_query.shape[0]
    text_part = jnp.einsum(
        "qhd,khd->hqk",
        heads_view(text_query),
        heads_view(text_keys),
        preferred_element_type=jnp.float32,
    )
    layout_part = jnp.einsum(
        "qhd,khd->hqk",
        heads_view(layout_query),
        heads_view(layout_keys),
        preferred_element_type=jnp.float32,
    )
    scores = text_part * head_scale(text_query) + layout_part * head_scale(layout_query)
    visible = jnp.arange(rows) < length
    return jnp.where(visible[None, None, :], scores, NEG)


def weigh_values(probs, values):
    mixed = jnp.einsum(
        "hqk,khd->qhd", probs, heads_view(values), preferred_element_type=jnp.float32
    )
    return mixed.reshape(values.shape[0], values.shape[1])


def attend_forward(pieces):
    text_query, text_keys, text_values, layout_query, layout_keys, layout_values, length = pieces
    scores = joint_scores(text_query, text_keys, layout_query, layout_keys, length)
    top = jnp.max(scores, -1, keepdims=True)
    expo = jnp.exp(scores - top)
    total = jnp.sum(expo, -1, keepdims=True)
    probs = (expo / total).astype(jnp.bfloat16)
    text_att = weigh_values(probs, text_values).astype(jnp.bfloat16)
    layout_att = weigh_values(probs, layout_values).astype(jnp.bfloat16)
    return (text_att, layout_att, (top + jnp.log(total))[:, :, 0])


def values_grad(probs_low, grad_out):
    moved = jnp.einsum(
        "hqk,qhd->khd", probs_low, heads_view(grad_out), preferred_element_type=jnp.float32
    )
    return moved.reshape(grad_out.shape[0], grad_out.shape[1]).astype(jnp.bfloat16)


def query_keys_grad(score_grads, query, keys):
    scale = head_scale(query)
    rows, width = query.shape
    query_grad = jnp.zeros((rows, HEADS, width // HEADS), jnp.float32)
    keys_grad = jnp.zeros((rows, HEADS, width // HEADS), jnp.float32)
    for score_grad in score_grads:
        query_grad = query_grad + jnp.einsum(
            "hqk,khd->qhd", score_grad, heads_view(keys), preferred_element_type=jnp.float32
        )
        keys_grad = keys_grad + jnp.einsum(
            "hqk,qhd->khd", score_grad, heads_view(query), preferred_element_type=jnp.float32
        )
    query_grad = query_grad * scale
    keys_grad = keys_grad * scale
    return (
        query_grad.reshape(rows, width).astype(jnp.bfloat16),
        keys_grad.reshape(rows, width).astype(jnp.bfloat16),
    )


def softmax_back(probs, mixed):
    return (probs * (mixed - jnp.sum(probs * mixed, -1, keepdims=True))).astype(jnp.bfloat16)


def attend_backward(pieces):
    (
        text_query,
        text_keys,
        text_values,
        layout_query,
        layout_keys,
        layout_values,
        length,
        log_total,
        text_grad,
        layout_grad,
    ) = pieces
    scores = joint_scores(text_query, text_keys, layout_query, layout_keys, length)
    probs = jnp.exp(scores - log_total[:, :, None])
    probs_low = probs.astype(jnp.bfloat16)
    text_values_grad = values_grad(probs_low, text_grad)
    layout_values_grad = values_grad(probs_low, layout_grad)
    text_mixed = jnp.einsum(
        "qhd,khd->hqk",
        heads_view(text_grad),
        heads_view(text_values),
        preferred_element_type=jnp.float32,
    )
    layout_mixed = jnp.einsum(
        "qhd,khd->hqk",
        heads_view(layout_grad),
        heads_view(layout_values),
        preferred_element_type=jnp.float32,
    )
    text_score_grad = softmax_back(probs, text_mixed)
    layout_score_grad = softmax_back(probs, layout_mixed)
    text_query_grad, text_keys_grad = query_keys_grad((text_score_grad,), text_query, text_keys)
    layout_query_grad, layout_keys_grad = query_keys_grad(
        (text_score_grad, layout_score_grad), layout_query, layout_keys
    )
    return (
        text_query_grad,
        text_keys_grad,
        text_values_grad,
        layout_query_grad,
        layout_keys_grad,
        layout_values_grad,
    )


def close_stream(inputs, attended, weights, width):
    attention_w, up_w, down_w, vector = weights
    parts = vector_parts(vector, width)
    after = matmul(attended, attention_w[3 * width :]) + parts[2]
    first, scaled_one, inverse_one = normalize(
        inputs.astype(jnp.float32) + after, parts[3], parts[4]
    )
    first_low = first.astype(jnp.bfloat16)
    upper = contract_cols(first_low, up_w) + parts[8]
    hidden_act = exact_gelu(upper).astype(jnp.bfloat16)
    final, scaled_two, inverse_two = normalize(
        first + matmul(hidden_act, down_w) + parts[5], parts[6], parts[7]
    )
    return (final, (scaled_one, inverse_one, first_low, upper, hidden_act, scaled_two, inverse_two))


def close_back(cotan, attended, saved, weights, width):
    scaled_one, inverse_one, first_low, upper, hidden_act, scaled_two, inverse_two = saved
    attention_w, up_w, down_w, vector = weights
    parts = vector_parts(vector, width)
    gain_two_grad = jnp.sum(cotan * scaled_two, 0)
    shift_two_grad = jnp.sum(cotan, 0)
    second_grad = norm_back(cotan, scaled_two, inverse_two, parts[6])
    branch_low = second_grad.astype(jnp.bfloat16)
    down_grad = contract_rows(hidden_act, branch_low)
    bias_down_grad = jnp.sum(branch_low.astype(jnp.float32), 0)
    act_grad = contract_cols(branch_low, down_w)
    gelu_back = jax.vjp(exact_gelu, upper)[1]
    upper_low = gelu_back(act_grad)[0].astype(jnp.bfloat16)
    up_grad_flipped = contract_rows(upper_low, first_low)
    bias_up_grad = jnp.sum(upper_low.astype(jnp.float32), 0)
    first_grad = second_grad + matmul(upper_low, up_w)
    gain_one_grad = jnp.sum(first_grad * scaled_one, 0)
    shift_one_grad = jnp.sum(first_grad, 0)
    resid_grad = norm_back(first_grad, scaled_one, inverse_one, parts[3])
    after_low = resid_grad.astype(jnp.bfloat16)
    out_weight_grad = contract_rows(attended, after_low)
    bias_out_grad = jnp.sum(after_low.astype(jnp.float32), 0)
    attended_grad = contract_cols(after_low, attention_w[3 * width :]).astype(jnp.bfloat16)
    tail = (
        bias_out_grad,
        gain_one_grad,
        shift_one_grad,
        bias_down_grad,
        gain_two_grad,
        shift_two_grad,
        bias_up_grad,
    )
    return (resid_grad, attended_grad, out_weight_grad, tail, up_grad_flipped, down_grad)


def open_back(
    inputs,
    resid_grad,
    query_grad,
    keys_grad,
    values_grad,
    out_weight_grad,
    tail,
    attention_w,
    width,
):
    stacked_grad = jnp.stack([query_grad, keys_grad, values_grad])
    weight_grad = jnp.einsum(
        "nd,jne->jde", inputs, stacked_grad, preferred_element_type=jnp.float32
    ).reshape(3 * width, width)
    input_grad = resid_grad + jnp.einsum(
        "jne,jde->nd",
        stacked_grad,
        attention_w[: 3 * width].reshape(3, width, width),
        preferred_element_type=jnp.float32,
    )
    bias_query_grad = jnp.sum(query_grad.astype(jnp.float32), 0)
    bias_value_grad = jnp.sum(values_grad.astype(jnp.float32), 0)
    (
        bias_out_grad,
        gain_one_grad,
        shift_one_grad,
        bias_down_grad,
        gain_two_grad,
        shift_two_grad,
        bias_up_grad,
    ) = tail
    vector_grad = jnp.concatenate(
        [
            bias_query_grad,
            bias_value_grad,
            bias_out_grad,
            gain_one_grad,
            shift_one_grad,
            bias_down_grad,
            gain_two_grad,
            shift_two_grad,
            bias_up_grad,
        ]
    )
    attention_grad = jnp.concatenate([weight_grad, out_weight_grad], 0)
    return (input_grad, attention_grad, vector_grad)


def by_stretch(array, stretches):
    return array.reshape((stretches, array.shape[0] // stretches) + array.shape[1:])


def shards(
    shape,
    text_in,
    layout_in,
    lengths,
    dup_rows,
    text_attention,
    text_up,
    text_down,
    text_vector,
    layout_attention,
    layout_up,
    layout_down,
    layout_vector,
    text_cotangent,
    layout_cotangent,
):
    count = shape["gx"] * shape["gy"]
    me = flat_index(shape["gy"])
    text_rows, layout_rows = text_attention.shape[0], layout_attention.shape[0]
    text_vec, layout_vec = text_vector.shape[0], layout_vector.shape[0]
    packed = pack_rows(
        text_attention,
        [layout_attention, layout_up.T, layout_down],
        jnp.concatenate([text_vector, layout_vector]),
    ).astype(jnp.bfloat16)
    gathered = gather_rows(packed, shape, me)
    up_all = gather_rows(text_up.T.astype(jnp.bfloat16), shape, me).reshape(-1, D)
    down_all = gather_rows(text_down.astype(jnp.bfloat16), shape, me).reshape(-1, D)
    text_all, layouts_all, text_vec_all, layout_vec_all = unpack_rows(
        gathered, text_rows, layout_rows, text_vec, layout_vec
    )
    text_weights = (text_all.reshape(-1, D), up_all, down_all, text_vec_all.reshape(-1))
    layout_weights = tuple(rows.reshape(-1, DL) for rows in layouts_all) + (
        layout_vec_all.reshape(-1),
    )
    stretches = lengths.shape[0]
    text_query, text_keys, text_values = open_stream(text_in, text_weights, D)
    layout_query, layout_keys, layout_values = open_stream(layout_in, layout_weights, DL)
    opened = (text_query, text_keys, text_values, layout_query, layout_keys, layout_values)
    opened_stretches = tuple((by_stretch(array, stretches) for array in opened))
    text_att, layout_att, log_total = lax.map(attend_forward, opened_stretches + (lengths,))
    text_att = text_att.reshape(-1, D)
    layout_att = layout_att.reshape(-1, DL)
    text_final, text_saved = close_stream(text_in, text_att, text_weights, D)
    layout_final, layout_saved = close_stream(layout_in, layout_att, layout_weights, DL)
    text_back, layout_back = text_weights, layout_weights
    span = text_in.shape[0] // stretches
    position = jnp.arange(span)
    keep = (position[None, :] < lengths[:, None]) & (dup_rows.reshape(stretches, span) == 0)
    keep = keep.reshape(-1, 1).astype(jnp.float32)
    text_cot = text_cotangent.astype(jnp.float32) * keep
    layout_cot = layout_cotangent.astype(jnp.float32) * keep
    text_resid, text_att_grad, text_out_w, text_tail, text_up_flipped, text_down_grad = close_back(
        text_cot, text_att, text_saved, text_back, D
    )
    (
        layout_resid,
        layout_att_grad,
        layout_out_w,
        layout_tail,
        layout_up_flipped,
        layout_down_grad,
    ) = close_back(layout_cot, layout_att, layout_saved, layout_back, DL)
    back_pieces = opened_stretches + (
        lengths,
        log_total,
        by_stretch(text_att_grad, stretches),
        by_stretch(layout_att_grad, stretches),
    )
    grads = lax.map(attend_backward, back_pieces)
    (
        text_query_grad,
        text_keys_grad,
        text_values_grad,
        layout_query_grad,
        layout_keys_grad,
        layout_values_grad,
    ) = tuple((array.reshape(-1, array.shape[-1]) for array in grads))
    text_input_grad, text_attention_grad, text_vector_grad = open_back(
        text_in,
        text_resid,
        text_query_grad,
        text_keys_grad,
        text_values_grad,
        text_out_w,
        text_tail,
        text_back[0],
        D,
    )
    layout_input_grad, layout_attention_grad, layout_vector_grad = open_back(
        layout_in,
        layout_resid,
        layout_query_grad,
        layout_keys_grad,
        layout_values_grad,
        layout_out_w,
        layout_tail,
        layout_back[0],
        DL,
    )

    def by_owner(array):
        return array.reshape((count, array.shape[0] // count) + array.shape[1:])

    attention_sum = scatter_rows(
        pack_rows(
            by_owner(text_attention_grad),
            [by_owner(g) for g in (layout_attention_grad, layout_up_flipped, layout_down_grad)],
            jnp.concatenate([by_owner(text_vector_grad), by_owner(layout_vector_grad)], -1),
        ).astype(jnp.bfloat16),
        shape,
        me,
    )
    up_sum = scatter_rows(by_owner(text_up_flipped).astype(jnp.bfloat16), shape, me)
    down_sum = scatter_rows(by_owner(text_down_grad).astype(jnp.bfloat16), shape, me)
    text_attention_sum, layout_sums, text_vec_sum, layout_vec_sum = unpack_rows(
        attention_sum, text_rows, layout_rows, text_vec, layout_vec
    )
    return (
        text_final.astype(jnp.bfloat16),
        layout_final.astype(jnp.bfloat16),
        text_input_grad.astype(jnp.bfloat16),
        layout_input_grad.astype(jnp.bfloat16),
        text_attention_sum,
        up_sum.T,
        down_sum,
        text_vec_sum,
        layout_sums[0],
        layout_sums[1].T,
        layout_sums[2],
        layout_vec_sum,
    )


BF = jnp.bfloat16
F32 = jnp.float32
CAT = 128
TEXT_LANES = D // HEADS
LAYOUT_LANES = DL // HEADS
MASK_LANE = TEXT_LANES + LAYOUT_LANES
VMEM_SPEC = pl.BlockSpec(memory_space=pltpu.VMEM)
SMEM_SPEC = pl.BlockSpec(memory_space=pltpu.SMEM)
ANY_SPEC = pl.BlockSpec(memory_space=pl.ANY)
STAGED = "staged"


def nn(left, right):
    return lax.dot_general(left, right, (((1,), (0,)), ((), ())), preferred_element_type=F32)


def nt(left, right):
    return lax.dot_general(left, right, (((1,), (1,)), ((), ())), preferred_element_type=F32)


def tn(left, right):
    return lax.dot_general(left, right, (((0,), (0,)), ((), ())), preferred_element_type=F32)


def row_mean(array):
    return jnp.sum(array, -1, keepdims=True) * (1.0 / array.shape[-1])


def col_sum(array):
    return jnp.sum(array, 0, keepdims=True)


def norm(resid):
    center = resid - row_mean(resid)
    inverse = lax.rsqrt(row_mean(center * center) + EPS)
    return center * inverse, inverse


def norm_grad(grad, scaled, inverse, gain):
    weighted = grad * gain
    return inverse * (weighted - row_mean(weighted) - scaled * row_mean(weighted * scaled))


def kernel_call(body, outs, ins, scratch=(), room=60):
    staged = [index for index, (_, spec) in enumerate(ins) if spec == STAGED]

    def with_copies(*refs):
        rooms, sems = refs[len(refs) - len(staged) - 1 : -1], refs[-1]
        given = list(refs[: len(refs) - len(staged) - 1])
        copies = []
        for order, (index, target) in enumerate(zip(staged, rooms)):
            copies.append(pltpu.make_async_copy(given[index], target, sems.at[order]))
            given[index] = target
        for copy in copies:
            copy.start()
        for copy in copies:
            copy.wait()
        body(*given)

    scratch = list(scratch)
    if staged:
        scratch += [pltpu.VMEM(ins[index][0].shape, ins[index][0].dtype) for index in staged]
        scratch.append(pltpu.SemaphoreType.DMA((len(staged),)))
    return pl.pallas_call(
        with_copies if staged else body,
        out_shape=[jax.ShapeDtypeStruct(shape, kind) for shape, kind, _ in outs],
        in_specs=[ANY_SPEC if spec == STAGED else spec for _, spec in ins],
        out_specs=[spec for _, _, spec in outs],
        scratch_shapes=scratch,
        compiler_params=pltpu.CompilerParams(vmem_limit_bytes=room * 2**20),
    )(*[array for array, _ in ins])


def stack_blocks(blocks):
    count, (_, rows, width) = len(blocks), blocks[0].shape

    def body(*refs):
        out, sems = refs[count], refs[count + 1]
        copies = [
            pltpu.make_async_copy(refs[index].at[0], out.at[index], sems.at[index])
            for index in range(count)
        ]
        for copy in copies:
            copy.start()
        for copy in copies:
            copy.wait()

    return kernel_call(
        body,
        [((count, rows, width), BF, ANY_SPEC)],
        [(block, VMEM_SPEC) for block in blocks],
        [pltpu.SemaphoreType.DMA((count,))],
        room=8,
    )[0]


def turn(dims, core_bit):
    (x, _), _, _, (y, _) = dims
    return (x, y) if core_bit else (y, x)


def swap_turn(array, dims, which, count):
    core = dims[1][0]
    return lax.ppermute(
        array,
        AXES,
        [(device, device ^ turn(dims, device // core % 2)[which]) for device in range(count)],
    )


def spread(held, dims, count):
    pieces = [held]
    for source, which in ((0, 0), (0, 1), (1, 1)):
        pieces.append(swap_turn(pieces[source], dims, which, count))
    return pieces


def gather_own(shard, shape):
    count = shape["gx"] * shape["gy"]
    dims = exchange_dims(shape)
    near = stack_blocks(spread(shard[None], dims, count))
    return [near, swap(near, dims[1][0], count)]


def gather_pieces(shard, shape):
    count = shape["gx"] * shape["gy"]
    dims = exchange_dims(shape)
    _, (core, _), (z, nz), _ = dims
    blocks = []
    for step in range(1, nz):
        blocks.append(swap(shard[None], z * step, count))
    pieces = spread(stack_blocks(blocks), dims, count)
    for index in range(4):
        pieces.append(swap(pieces[index], core, count))
    return pieces


def fetch_blocks(me, dims, refs, place, sems):
    (x, _), (core, _), (z, nz), (y, _) = dims
    odd = me // core % 2
    first = jnp.where(odd == 1, x, y)
    second = jnp.where(odd == 1, y, x)
    mine, partner = [0, first, second, x ^ y], [core, core ^ second, core ^ first, core ^ x ^ y]
    blocks = []
    for ref, offsets in zip(refs[:2], (mine, partner)):
        blocks += [(ref.at[index], offset, True) for index, offset in enumerate(offsets)]
    for ref, offset in zip(refs[2:], mine + partner):
        blocks += [(ref.at[step - 1], offset ^ (z * step), False) for step in range(1, nz)]
    copies = []
    for block, offset, own in blocks:
        for source, target in place(block, me ^ offset, own):
            copies.append(pltpu.make_async_copy(source, target, sems.at[len(copies)]))
    return copies


def send_block(me, dims, device, source, keep, send, sems):
    (x, _), (core, _), (z, nz), (y, _) = dims
    odd = device // core % 2
    away = me ^ device
    across = [away // stride % 2 for stride in (x, y)]
    top = odd * across[0] + (1 - odd) * across[1]
    low = odd * across[1] + (1 - odd) * across[0]
    slot = top * 2 * nz + low * nz + away // z % nz
    far = away // core % 2
    sem = sems.at[device]

    @pl.when(far == 0)
    def _():
        pltpu.make_async_copy(source, keep.at[slot], sem).start()

    @pl.when(far == 1)
    def _():
        pltpu.make_async_copy(source, send.at[slot], sem).start()


def added(terms, start, stop):
    total = terms[0][start:stop].astype(F32)
    for term in terms[1:]:
        total = total + term[start:stop].astype(F32)
    return total


def reduce_part(keep, send, dims, count):
    _, (core, _), (z, nz), _ = dims

    terms = [keep, swap(send, core, count)]
    for which in range(2):
        half = terms[0].shape[0] // 2 if which == 0 else nz
        got = swap_turn(added(terms, half, 2 * half).astype(BF), dims, which, count)
        terms.append(got)
        terms = [term[:half] for term in terms]
    result = added(terms, 0, 1)[0]
    for step in range(1, nz):
        got = swap(added(terms, step, step + 1)[0].astype(BF), z * step, count)
        result = result + got.astype(F32)
    return result


def vector_rows(read, width, segment, count):
    rows = []
    for row in range(segment * count // width):
        at, stop, parts = row * width, (row + 1) * width, []
        while at < stop:
            device, start = at // segment, at % segment
            take = min(segment - start, stop - at)
            parts.append(read(device, start, start + take))
            at += take
        rows.append(parts[0] if len(parts) == 1 else jnp.concatenate(parts, 1))
    return rows


def head_forward(q, k, v):
    scores = nt(k, q)
    top = jnp.max(scores, 0, keepdims=True)
    expo = jnp.exp(scores - top)
    total = col_sum(expo)
    probs = (expo * (1.0 / total)).astype(BF)
    return tn(v, probs).T.astype(BF), top + jnp.log(total)


def project(me, length, text_in, layout_in, pieces, sizes, dims, middle):
    count, text_rows, layout_rows, text_vec, layout_vec = sizes
    rows = text_in.shape[0]
    packed = pieces[2].shape[1]

    def body(*refs):
        me_ref, length_ref, x_ref, xl_ref = refs[:4]
        piece_refs = refs[4 : 4 + len(pieces)]
        (
            q_out,
            k_out,
            v_out,
            weight_out,
            layout_ref,
            up_ref,
            down_ref,
            text_vec_ref,
            layout_vec_ref,
            mixed,
            lse_ref,
            q_ref,
            k_ref,
            v_ref,
            weight,
            tail,
            sems,
            out_sems,
        ) = refs[4 + len(pieces) :]

        def place(source, device, own):
            base = pl.multiple_of(device * text_rows, 16)
            return [
                (source.at[0:text_rows], weight.at[pl.ds(base, text_rows)]),
                (source.at[text_rows:packed], tail.at[device]),
            ]

        copies = fetch_blocks(me_ref[0], dims, piece_refs, place, sems)
        for copy in copies:
            copy.start()
        for copy in copies:
            copy.wait()
        outs = [pltpu.make_async_copy(weight, weight_out, out_sems.at[3])]
        outs[0].start()
        side = D // 3
        for device in range(count):
            block = pl.ds(device * layout_rows, layout_rows)
            for index, ref in enumerate((layout_ref, up_ref, down_ref)):
                ref[block, :] = tail[device, 0:layout_rows, side * index : side * index + DL]

        def read_text(device, start, stop):
            return tail[device, layout_rows : layout_rows + 1, start:stop].astype(F32)

        def read_layout(device, start, stop):
            return read_text(device, text_vec + start, text_vec + stop)

        for index, row in enumerate(vector_rows(read_text, D, text_vec, count)):
            text_vec_ref[index] = row
        for index, row in enumerate(vector_rows(read_layout, DL, layout_vec, count)):
            layout_vec_ref[index] = row
        x, xl = x_ref[...], xl_ref[...]
        seen = lax.broadcasted_iota(jnp.int32, (rows, CAT - MASK_LANE), 0) < length_ref[0]
        lane = lax.broadcasted_iota(jnp.int32, (rows, CAT - MASK_LANE), 1)
        ones = jnp.where(lane == 0, 1.0, 0.0).astype(BF)
        hidden = jnp.where((lane == 0) & jnp.logical_not(seen), NEG, 0.0).astype(BF)
        nothing = jnp.zeros((rows, CAT - MASK_LANE), BF)
        for index, (ref, out, extra) in enumerate(
            ((q_ref, q_out, ones), (k_ref, k_out, hidden), (v_ref, v_out, nothing))
        ):
            text = nn(x, weight[index * D : (index + 1) * D, :])
            layout = nn(xl, layout_ref[index * DL : (index + 1) * DL, :])
            if index != 1:
                text = text + text_vec_ref[index // 2]
                layout = layout + layout_vec_ref[index // 2]
            text, layout = text.astype(BF), layout.astype(BF)
            if index == 0:
                text = text * (1.0 / math.sqrt(TEXT_LANES))
                layout = layout * (1.0 / math.sqrt(LAYOUT_LANES))
            for head in range(HEADS):
                ref[head] = jnp.concatenate(
                    [
                        text[:, TEXT_LANES * head : TEXT_LANES * (head + 1)],
                        layout[:, LAYOUT_LANES * head : LAYOUT_LANES * (head + 1)],
                        extra,
                    ],
                    1,
                )
            outs.append(pltpu.make_async_copy(ref, out, out_sems.at[index]))
            outs[-1].start()

        def head_step(head, carry):
            mixed[head], lse_ref[head] = head_forward(q_ref[head], k_ref[head], v_ref[head])
            return carry

        lax.fori_loop(0, middle, head_step, 0)
        for copy in outs:
            copy.wait()

    cat = ((HEADS, rows, CAT), BF, ANY_SPEC)
    room = pltpu.VMEM((HEADS, rows, CAT), BF)
    return kernel_call(
        body,
        [
            cat,
            cat,
            cat,
            ((4 * D, D), BF, ANY_SPEC),
            ((4 * DL, DL), BF, VMEM_SPEC),
            ((FFL, DL), BF, VMEM_SPEC),
            ((FFL, DL), BF, VMEM_SPEC),
            ((12, 1, D), F32, VMEM_SPEC),
            ((12, 1, DL), F32, VMEM_SPEC),
            ((middle, rows, CAT), BF, VMEM_SPEC),
            ((middle, 1, rows), F32, VMEM_SPEC),
        ],
        [(me, SMEM_SPEC), (length, SMEM_SPEC), (text_in, STAGED), (layout_in, STAGED)]
        + [(array, ANY_SPEC) for array in pieces],
        [
            room,
            room,
            room,
            pltpu.VMEM((4 * D, D), BF),
            pltpu.VMEM((count, packed - text_rows, D), BF),
            pltpu.SemaphoreType.DMA((2 * count,)),
            pltpu.SemaphoreType.DMA((4,)),
        ],
    )


def heads_out(ref, start, stop):
    heads = range(start, stop)
    text = jnp.concatenate([ref[head, :, 0:TEXT_LANES] for head in heads], 1)
    layout = jnp.concatenate([ref[head, :, TEXT_LANES:MASK_LANE] for head in heads], 1)
    return text, layout


def attend(text_in, layout_in, query, keys, values, first, weight, layout_w, text_vec, layout_vec):
    rows = text_in.shape[0]
    middle = first.shape[0]
    late = HEADS - middle

    def body(
        x_ref,
        xl_ref,
        q_any,
        k_any,
        v_any,
        first_ref,
        weight_any,
        layout_ref,
        tv_ref,
        lv_ref,
        out_t,
        out_l,
        lse_ref,
        norm_t,
        inv_t,
        norm_l,
        inv_l,
        q_ref,
        k_ref,
        v_ref,
        mixed,
        weight,
        sems,
    ):
        fetches = [
            pltpu.make_async_copy(source.at[middle:HEADS], target, sems.at[index])
            for index, (source, target) in enumerate(
                ((q_any, q_ref), (k_any, k_ref), (v_any, v_ref))
            )
        ]
        fetches.append(pltpu.make_async_copy(weight_any.at[3 * D : 4 * D], weight, sems.at[3]))
        for fetch in fetches:
            fetch.start()
        for fetch in fetches[:3]:
            fetch.wait()

        def head_step(head, carry):
            mixed[head], lse_ref[head] = head_forward(q_ref[head], k_ref[head], v_ref[head])
            return carry

        lax.fori_loop(0, late, head_step, 0)
        parts = [heads_out(first_ref, 0, middle), heads_out(mixed, 0, late)]
        text = jnp.concatenate([part[0] for part in parts], 1)
        layout = jnp.concatenate([part[1] for part in parts], 1)
        out_t[...] = text
        out_l[...] = layout
        fetches[3].wait()
        after = nn(text, weight[...]) + tv_ref[2]
        norm_t[...], inv_t[...] = norm(x_ref[...].astype(F32) + after)
        after = nn(layout, layout_ref[3 * DL : 4 * DL, :]) + lv_ref[2]
        norm_l[...], inv_l[...] = norm(xl_ref[...].astype(F32) + after)

    room = pltpu.VMEM((late, rows, CAT), BF)
    return kernel_call(
        body,
        [
            ((rows, D), BF, VMEM_SPEC),
            ((rows, DL), BF, VMEM_SPEC),
            ((late, 1, rows), F32, VMEM_SPEC),
            ((rows, D), F32, VMEM_SPEC),
            ((rows, 1), F32, VMEM_SPEC),
            ((rows, DL), F32, VMEM_SPEC),
            ((rows, 1), F32, VMEM_SPEC),
        ],
        [
            (text_in, STAGED),
            (layout_in, STAGED),
            (query, ANY_SPEC),
            (keys, ANY_SPEC),
            (values, ANY_SPEC),
            (first, VMEM_SPEC),
            (weight, ANY_SPEC),
            (layout_w, VMEM_SPEC),
            (text_vec, VMEM_SPEC),
            (layout_vec, VMEM_SPEC),
        ],
        [room, room, room, room, pltpu.VMEM((D, D), BF), pltpu.SemaphoreType.DMA((4,))],
    )


def gelu_both(value):
    bell = jnp.exp2(value * value * (-0.5 / math.log(2.0)))
    near = 1.0 / (1.0 + jnp.abs(value) * (0.3275911 * math.sqrt(0.5)))
    tail = jnp.full_like(value, 0.5 * 1.061405429)
    for factor in (-1.453152027, 1.421413741, -0.284496736, 0.254829592):
        tail = tail * near + 0.5 * factor
    tail = tail * near * bell
    below = jnp.where(value < 0.0, tail, 1.0 - tail)
    return value * below, below + value * bell * (1.0 / math.sqrt(2.0 * math.pi))


def feed_stream(norm_ref, vec_ref, cot_ref, keep, up, down, bias, hidden, slope, blocks, write, outs):
    out_ref, grad_ref, vec_out = outs
    first = norm_ref[...] * vec_ref[3] + vec_ref[4]
    low = first.astype(BF)

    def forward(block, total):
        act, rise = gelu_both(nt(low, up(block)) + bias(block))
        act = act.astype(BF)
        hidden[block] = act
        slope[block] = rise
        return total + nn(act, down(block))

    def loop(body, start):
        return body(0, start) if blocks == 1 else lax.fori_loop(0, blocks, body, start)

    branch = loop(forward, jnp.zeros_like(first))
    scaled, inverse = norm(first + branch + vec_ref[5])
    out_ref[...] = (scaled * vec_ref[6] + vec_ref[7]).astype(BF)
    cotan = cot_ref[...].astype(F32) * keep
    vec_out[1] = col_sum(cotan * scaled)
    vec_out[2] = col_sum(cotan)
    second = norm_grad(cotan, scaled, inverse, vec_ref[6])
    branch_low = second.astype(BF)
    vec_out[0] = col_sum(branch_low.astype(F32))

    def backward(block, total):
        act_grad = nt(branch_low, down(block))
        upper_low = (act_grad * slope[block]).astype(BF)
        write(
            block,
            tn(upper_low, low),
            tn(hidden[block], branch_low),
            col_sum(upper_low.astype(F32)),
        )
        return total + nn(upper_low, up(block))

    grad_ref[...] = loop(backward, second)


def feed(me, keep_rows, norm_t, norm_l, tv, lv, cot_t, cot_l, pieces, lu, ld, dims, text_rows):
    rows = norm_t.shape[0]
    count = 8 * dims[2][1]
    skip = pieces[0].shape[1] - 2 * text_rows
    blocks = FF // D

    def body(*refs):
        me_ref, keep_ref, nt_ref, nl_ref, tv_ref, lv_ref, ct_ref, cl_ref, lu_ref, ld_ref = refs[:10]
        piece_refs = refs[10 : 10 + len(pieces)]
        (
            out_t,
            out_l,
            grad_t,
            grad_l,
            vec_t,
            vec_l,
            lu_grad,
            ld_grad,
            both_keep,
            both_send,
            up,
            down,
            hidden,
            slope,
            hidden_l,
            slope_l,
            grads,
            sems,
        ) = refs[10 + len(pieces) :]
        mine = me_ref[0]

        def place(source, device, own):
            at = pl.ds(pl.multiple_of(device * text_rows, 16), text_rows)
            base = skip if own else 0
            return [
                (source.at[base : base + text_rows], up.at[at]),
                (source.at[base + text_rows : base + 2 * text_rows], down.at[at]),
            ]

        copies = fetch_blocks(mine, dims, piece_refs, place, sems)
        for copy in copies:
            copy.start()
        keep = keep_ref[...]

        def whole(ref):
            return lambda block: ref[...]

        parts = FFL // DL
        bias_l = jnp.concatenate([lv_ref[8 + part] for part in range(parts)], 1)

        def write_l(block, one, two, bias):
            lu_grad[...] = one.astype(BF)
            ld_grad[...] = two.astype(BF)
            for part in range(parts):
                vec_l[3 + part] = bias[:, part * DL : (part + 1) * DL]

        feed_stream(
            nl_ref,
            lv_ref,
            cl_ref,
            keep,
            whole(lu_ref),
            whole(ld_ref),
            lambda block: bias_l,
            hidden_l,
            slope_l,
            1,
            write_l,
            (out_l, grad_l, vec_l),
        )
        for copy in copies:
            copy.wait()
        per_block = D // text_rows

        def rows_of(ref):
            return lambda block: ref[pl.ds(pl.multiple_of(block * D, 16), D), :]

        def write_t(block, one, two, bias):
            vec_t[3 + block] = bias
            for part in range(per_block):
                at = slice(part * text_rows, (part + 1) * text_rows)
                device = block * per_block + part
                grads[device, 0:text_rows] = one[at].astype(BF)
                grads[device, text_rows:] = two[at].astype(BF)
                send_block(mine, dims, device, grads.at[device], both_keep, both_send, sems)

        feed_stream(
            nt_ref,
            tv_ref,
            ct_ref,
            keep,
            rows_of(up),
            rows_of(down),
            lambda block: tv_ref[8 + block],
            hidden,
            slope,
            blocks,
            write_t,
            (out_t, grad_t, vec_t),
        )
        for device in range(count):
            pltpu.make_async_copy(grads.at[device], both_keep.at[0], sems.at[device]).wait()

    part = ((count // 2, 2 * text_rows, D), BF, ANY_SPEC)
    return kernel_call(
        body,
        [
            ((rows, D), BF, VMEM_SPEC),
            ((rows, DL), BF, VMEM_SPEC),
            ((rows, D), F32, VMEM_SPEC),
            ((rows, DL), F32, VMEM_SPEC),
            ((3 + blocks, 1, D), F32, VMEM_SPEC),
            ((3 + blocks, 1, DL), F32, VMEM_SPEC),
            ((FFL, DL), BF, VMEM_SPEC),
            ((FFL, DL), BF, VMEM_SPEC),
            part,
            part,
        ],
        [
            (me, SMEM_SPEC),
            (keep_rows, STAGED),
            (norm_t, STAGED),
            (norm_l, STAGED),
            (tv, VMEM_SPEC),
            (lv, VMEM_SPEC),
            (cot_t, STAGED),
            (cot_l, STAGED),
            (lu, STAGED),
            (ld, STAGED),
        ]
        + [(array, ANY_SPEC) for array in pieces],
        [
            pltpu.VMEM((FF, D), BF),
            pltpu.VMEM((FF, D), BF),
            pltpu.VMEM((blocks, rows, D), BF),
            pltpu.VMEM((blocks, rows, D), F32),
            pltpu.VMEM((1, rows, FFL), BF),
            pltpu.VMEM((1, rows, FFL), F32),
            pltpu.VMEM((count, 2 * text_rows, D), BF),
            pltpu.SemaphoreType.DMA((2 * count,)),
        ],
        room=60,
    )


def close_back_pair(grad_t, grad_l, norms, outs, weight, layout_w, tv, lv):
    rows = grad_t.shape[0]
    norm_t, inv_t, norm_l, inv_l = norms
    out_t, out_l = outs

    def body(
        gt_ref,
        gl_ref,
        nt_ref,
        it_ref,
        nl_ref,
        il_ref,
        ot_ref,
        ol_ref,
        weight_any,
        layout_ref,
        tv_ref,
        lv_ref,
        resid_t,
        resid_l,
        out_wt,
        out_wl,
        vec_t,
        vec_l,
        dout,
        weight,
        sem,
    ):
        fetch = pltpu.make_async_copy(weight_any.at[3 * D : 4 * D], weight, sem)
        fetch.start()

        def close(grad, scaled, inverse, vec, mixed, vec_out, resid_ref, wide):
            vec_out[1] = col_sum(grad * scaled)
            vec_out[2] = col_sum(grad)
            resid = norm_grad(grad, scaled, inverse, vec[3])
            resid_ref[...] = resid
            after = resid.astype(BF)
            vec_out[0] = col_sum(after.astype(F32))
            return after, tn(mixed, after).astype(BF), nt(after, wide()).astype(BF)

        def wide_l():
            return layout_ref[3 * DL : 4 * DL, :]

        def wide_t():
            fetch.wait()
            return weight[...]

        _, out_wl[...], att_l = close(
            gl_ref[...], nl_ref[...], il_ref[...], lv_ref, ol_ref[...], vec_l, resid_l, wide_l
        )
        _, out_wt[...], att_t = close(
            gt_ref[...], nt_ref[...], it_ref[...], tv_ref, ot_ref[...], vec_t, resid_t, wide_t
        )
        nothing = jnp.zeros((rows, CAT - MASK_LANE), BF)
        for head in range(HEADS):
            dout[head] = jnp.concatenate(
                [
                    att_t[:, TEXT_LANES * head : TEXT_LANES * (head + 1)],
                    att_l[:, LAYOUT_LANES * head : LAYOUT_LANES * (head + 1)],
                    nothing,
                ],
                1,
            )

    return kernel_call(
        body,
        [
            ((rows, D), F32, VMEM_SPEC),
            ((rows, DL), F32, VMEM_SPEC),
            ((D, D), BF, VMEM_SPEC),
            ((DL, DL), BF, VMEM_SPEC),
            ((3, 1, D), F32, VMEM_SPEC),
            ((3, 1, DL), F32, VMEM_SPEC),
            ((HEADS, rows, CAT), BF, VMEM_SPEC),
        ],
        [
            (grad_t, STAGED),
            (grad_l, STAGED),
            (norm_t, STAGED),
            (inv_t, STAGED),
            (norm_l, STAGED),
            (inv_l, STAGED),
            (out_t, STAGED),
            (out_l, STAGED),
            (weight, ANY_SPEC),
            (layout_w, STAGED),
            (tv, VMEM_SPEC),
            (lv, VMEM_SPEC),
        ],
        [pltpu.VMEM((D, D), BF), pltpu.SemaphoreType.DMA],
        room=60,
    )


def heads_back(query, keys, values, lse, dout, start, stop):
    rows = query.shape[1]
    size = stop - start

    def body(q_any, k_any, v_any, lse_any, do_any, dq, dk, dv, q_ref, k_ref, v_ref, do_ref, lse_ref, sems):
        copies = [
            pltpu.make_async_copy(source.at[start:stop], target, sems.at[index])
            for index, (source, target) in enumerate(
                ((q_any, q_ref), (k_any, k_ref), (v_any, v_ref), (do_any, do_ref))
            )
        ]
        copies.append(pltpu.make_async_copy(lse_any, lse_ref, sems.at[4]))
        for copy in copies:
            copy.start()
        for copy in copies:
            copy.wait()
        is_text = lax.broadcasted_iota(jnp.int32, (rows, CAT), 1) < TEXT_LANES
        text_row = lax.broadcasted_iota(jnp.int32, (CAT, rows), 0) < TEXT_LANES

        def head_step(head, carry):
            q, k, v, do = q_ref[head], k_ref[head], v_ref[head], do_ref[head]
            probs = jnp.exp(nt(k, q) - lse_ref[head])
            dv[head] = nn(probs.astype(BF), do).astype(BF)
            none = jnp.zeros_like(v)
            mixed = nt(jnp.where(is_text, v, none), do)
            score_t = (probs * (mixed - col_sum(probs * mixed))).astype(BF)
            mixed = nt(jnp.where(is_text, none, v), do)
            score_l = (probs * (mixed - col_sum(probs * mixed))).astype(BF)
            dk_t = nn(score_t, q)
            dk_l = nn(score_l, q)
            dk[head] = jnp.where(is_text, dk_t, dk_t + dk_l).astype(BF)
            dq_t = tn(k, score_t)
            dq_l = tn(k, score_l)
            scaled = jnp.where(
                text_row,
                dq_t * (1.0 / math.sqrt(TEXT_LANES)),
                (dq_t + dq_l) * (1.0 / math.sqrt(LAYOUT_LANES)),
            )
            dq[head] = scaled.T.astype(BF)
            return carry

        lax.fori_loop(0, size, head_step, 0)

    cat = pltpu.VMEM((size, rows, CAT), BF)
    part = ((size, rows, CAT), BF, VMEM_SPEC)
    return kernel_call(
        body,
        [part, part, part],
        [(array, ANY_SPEC) for array in (query, keys, values, lse)] + [(dout, ANY_SPEC)],
        [cat, cat, cat, cat, pltpu.VMEM((size, 1, rows), F32), pltpu.SemaphoreType.DMA((5,))],
        room=16,
    )


def weight_grads(me, text_in, layout_in, backs, out_w, ffn_l, vecs, dims, sizes):
    count, text_rows, layout_rows, text_vec, layout_vec = sizes
    rows = text_in.shape[0]
    packed = text_rows + layout_rows + 8
    groups = len(backs)

    def body(*refs):
        me_ref, x_ref, xl_ref = refs[:3]
        back_refs = refs[3 : 3 + 3 * groups]
        (
            out_wt,
            out_wl,
            lu_grad,
            ld_grad,
            close_t,
            close_l,
            feed_t,
            feed_l,
            joined_t,
            joined_l,
            keep,
            send,
            pack,
            att_l,
            sems,
        ) = refs[3 + 3 * groups :]
        mine = me_ref[0]
        x, xl = x_ref[...], xl_ref[...]
        side = D // 3
        for device in range(count):
            pack[device, text_rows : text_rows + layout_rows, :] = jnp.zeros((layout_rows, D), BF)
        per_block = D // text_rows
        for index in range(3):
            pieces = [heads_out(back_refs[3 * group + index], 0, back_refs[3 * group + index].shape[0]) for group in range(groups)]
            joined_t[index] = jnp.concatenate([text for text, _ in pieces], 1)
            joined_l[index] = jnp.concatenate([layout for _, layout in pieces], 1)
            grad = tn(x, joined_t[index]).astype(BF)
            for part in range(per_block):
                pack[index * per_block + part, 0:text_rows, :] = grad[
                    part * text_rows : (part + 1) * text_rows
                ]
            att_l[index * DL : (index + 1) * DL, :] = tn(xl, joined_l[index]).astype(BF)
        for part in range(per_block):
            pack[3 * per_block + part, 0:text_rows, :] = out_wt[
                part * text_rows : (part + 1) * text_rows, :
            ]
        att_l[3 * DL : 4 * DL, :] = out_wl[...]
        for device in range(count):
            block = pl.ds(device * layout_rows, layout_rows)
            for index, ref in enumerate((att_l, lu_grad, ld_grad)):
                pack[
                    device,
                    text_rows : text_rows + layout_rows,
                    side * index : side * index + DL,
                ] = ref[block, :]

        def vector(joined, close, feeds):
            rows_of = [col_sum(joined[0].astype(F32)), col_sum(joined[2].astype(F32))]
            rows_of += [close[0], close[1], close[2], feeds[0], feeds[1], feeds[2]]
            return rows_of + [feeds[3 + block] for block in range(FF // D)]

        text_rows_of = vector(joined_t, close_t, feed_t)
        layout_rows_of = vector(joined_l, close_l, feed_l)

        def segment(all_rows, width, start, size):
            parts, stop = [], start + size
            while start < stop:
                row, at = start // width, start % width
                take = min(width - at, stop - start)
                parts.append(all_rows[row][:, at : at + take])
                start += take
            return parts

        row = lax.broadcasted_iota(jnp.int32, (8, D), 0)
        for device in range(count):
            parts = segment(text_rows_of, D, device * text_vec, text_vec)
            parts += segment(layout_rows_of, DL, device * layout_vec, layout_vec)
            parts.append(jnp.zeros((1, D - text_vec - layout_vec), F32))
            line = jnp.concatenate(parts, 1)
            pack[device, text_rows + layout_rows :, :] = jnp.where(
                row == 0, jnp.broadcast_to(line, (8, D)), 0.0
            ).astype(BF)
        for device in range(count):
            send_block(mine, dims, device, pack.at[device], keep, send, sems)
        for device in range(count):
            pltpu.make_async_copy(pack.at[device], keep.at[0], sems.at[device]).wait()

    part = ((count // 2, packed, D), BF, ANY_SPEC)
    arrays = []
    for back in backs:
        arrays += list(back)
    arrays += [*out_w, *ffn_l, *vecs]
    return kernel_call(
        body,
        [((3, rows, D), BF, VMEM_SPEC), ((3, rows, DL), BF, VMEM_SPEC), part, part],
        [(me, SMEM_SPEC), (text_in, STAGED), (layout_in, STAGED)]
        + [(array, VMEM_SPEC) for array in arrays],
        [
            pltpu.VMEM((count, packed, D), BF),
            pltpu.VMEM((4 * DL, DL), BF),
            pltpu.SemaphoreType.DMA((count,)),
        ],
        room=60,
    )


def input_grads(joined_t, joined_l, resid_t, resid_l, weight, layout_w):
    rows = resid_t.shape[0]

    def body(jt, jl, rt, rl, weight_any, layout_ref, grad_t, grad_l, weight, sem):
        fetch = pltpu.make_async_copy(weight_any.at[0 : 3 * D], weight, sem)
        fetch.start()
        total = rl[...]
        for index in range(3):
            total = total + nt(jl[index], layout_ref[index * DL : (index + 1) * DL, :])
        grad_l[...] = total.astype(BF)
        fetch.wait()
        total = rt[...]
        for index in range(3):
            total = total + nt(jt[index], weight[index * D : (index + 1) * D, :])
        grad_t[...] = total.astype(BF)

    return kernel_call(
        body,
        [((rows, D), BF, VMEM_SPEC), ((rows, DL), BF, VMEM_SPEC)],
        [(array, VMEM_SPEC) for array in (joined_t, joined_l, resid_t, resid_l)]
        + [(weight, ANY_SPEC), (layout_w, STAGED)],
        [pltpu.VMEM((3 * D, D), BF), pltpu.SemaphoreType.DMA],
        room=20,
    )


def shards_fast(
    shape,
    text_in,
    layout_in,
    lengths,
    dup_rows,
    text_attention,
    text_up,
    text_down,
    text_vector,
    layout_attention,
    layout_up,
    layout_down,
    layout_vector,
    text_cotangent,
    layout_cotangent,
):
    count = shape["gx"] * shape["gy"]
    dims = exchange_dims(shape)
    me = flat_index(shape["gy"]).reshape(1).astype(jnp.int32)
    text_rows, layout_rows = text_attention.shape[0], layout_attention.shape[0]
    text_vec, layout_vec = text_vector.shape[0], layout_vector.shape[0]
    packed = pack_rows(
        text_attention,
        [layout_attention, layout_up.T, layout_down],
        jnp.concatenate([text_vector, layout_vector]),
    ).astype(BF)
    sizes = (count, text_rows, layout_rows, text_vec, layout_vec)
    feed_shard = jnp.concatenate([text_up.T, text_down], 0).astype(BF)
    own = gather_own(jnp.concatenate([packed, feed_shard], 0), shape)
    parts = own + gather_pieces(packed, shape)
    feed_parts = own + gather_pieces(feed_shard, shape)
    middle = HEADS // 2
    q, k, v, weight, layout_w, lu, ld, tv, lv, first, lse_a = project(
        me, lengths, text_in, layout_in, parts, sizes, dims, middle
    )
    out_t, out_l, lse_b, norm_t, inv_t, norm_l, inv_l = attend(
        text_in, layout_in, q, k, v, first, weight, layout_w, tv, lv
    )
    span = text_in.shape[0]
    keep = (jnp.arange(span) < lengths[0]) & (dup_rows == 0)
    keep = keep.astype(F32)[:, None]
    (
        text_final,
        layout_final,
        grad_t,
        grad_l,
        feed_vt,
        feed_vl,
        lu_grad,
        ld_grad,
        both_keep,
        both_send,
    ) = feed(
        me,
        keep,
        norm_t,
        norm_l,
        tv,
        lv,
        text_cotangent,
        layout_cotangent,
        feed_parts,
        lu,
        ld,
        dims,
        text_rows,
    )
    resid_t, resid_l, out_wt, out_wl, close_t, close_l, dout = close_back_pair(
        grad_t, grad_l, (norm_t, inv_t, norm_l, inv_l), (out_t, out_l), weight, layout_w, tv, lv
    )
    backs = [
        heads_back(q, k, v, lse_a, dout, 0, middle), heads_back(q, k, v, lse_b, dout, middle, HEADS)
    ]
    joined_t, joined_l, keep_packed, send_packed = weight_grads(
        me,
        text_in,
        layout_in,
        backs,
        (out_wt, out_wl),
        (lu_grad, ld_grad),
        (close_t, close_l, feed_vt, feed_vl),
        dims,
        sizes,
    )
    text_input_grad, layout_input_grad = input_grads(
        joined_t, joined_l, resid_t, resid_l, weight, layout_w
    )
    both_sum = reduce_part(both_keep, both_send, dims, count)
    up_sum, down_sum = both_sum[:text_rows], both_sum[text_rows:]
    packed_sum = reduce_part(keep_packed, send_packed, dims, count)
    text_sum, layout_sums, text_vec_sum, layout_vec_sum = unpack_rows(
        packed_sum, text_rows, layout_rows, text_vec, layout_vec
    )
    return (
        text_final,
        layout_final,
        text_input_grad,
        layout_input_grad,
        text_sum,
        up_sum.T,
        down_sum,
        text_vec_sum,
        layout_sums[0],
        layout_sums[1].T,
        layout_sums[2],
        layout_vec_sum,
    )


def fits(shape):
    (_, nx), (_, ncore), (_, nz), (_, ny) = exchange_dims(shape)
    count = shape["gx"] * shape["gy"]
    return (
        (nx, ncore, ny) == (2, 2, 2)
        and (4 * D) % (16 * count) == 0
        and (4 * DL) % (8 * count) == 0
        and D % (4 * D // count) == 0
    )


def layer(fast, shape, *arrays):
    if not fast or arrays[2].shape[0] != 1:
        return shards(shape, *arrays)
    return shards_fast(shape, *arrays)


def solution(mesh):
    placed = (
        P(("gx", "gy"), None),
        P(("gx", "gy"), None),
        P(("gx", "gy")),
        P(("gx", "gy")),
        P(("gx", "gy"), None),
        P(None, ("gx", "gy")),
        P(("gx", "gy"), None),
        P(("gx", "gy")),
        P(("gx", "gy"), None),
        P(None, ("gx", "gy")),
        P(("gx", "gy"), None),
        P(("gx", "gy")),
        P(("gx", "gy"), None),
        P(("gx", "gy"), None),
    )
    shape = dict(mesh.shape)
    fast = fits(shape)
    return jax.shard_map(
        functools.partial(layer, fast, shape),
        mesh=mesh,
        in_specs=placed,
        out_specs=(
            P(("gx", "gy"), None),
            P(("gx", "gy"), None),
            P(("gx", "gy"), None),
            P(("gx", "gy"), None),
            P(("gx", "gy"), None),
            P(None, ("gx", "gy")),
            P(("gx", "gy"), None),
            P(("gx", "gy")),
            P(("gx", "gy"), None),
            P(None, ("gx", "gy")),
            P(("gx", "gy"), None),
            P(("gx", "gy")),
        ),
        check_vma=False,
    )
```

```python
import functools
import math

import jax
import jax.numpy as jnp
from jax import lax
from jax.experimental import pallas as pl
from jax.experimental.pallas import tpu as pltpu
from jax.sharding import PartitionSpec as P


AXES = ("gx", "gy")


def exchange_dims(shape):
    gx, gy = shape["gx"], shape["gy"]
    outer = {8: 4, 32: 4}.get(gy, gy)
    inner = gy // outer
    core = 2 if gx % 2 == 0 else 1
    core_dim = (gy, core)
    x_dim = (gy * core, gx // core)
    if inner <= outer:
        z_dim, y_dim = (inner, outer), (1, inner)
    else:
        z_dim, y_dim = (1, inner), (inner, outer)
    return x_dim, core_dim, z_dim, y_dim


def orders(shape):
    x_dim, core_dim, z_dim, y_dim = exchange_dims(shape)
    return ((z_dim, y_dim, x_dim, core_dim), (z_dim, x_dim, y_dim, core_dim))


def offsets(order):
    table = [0]
    for stride, size in order:
        table = [offset ^ (stride * step) for step in range(size) for offset in table]
    return table


def swap(array, offset, count):
    return lax.ppermute(array, AXES, [(device, device ^ offset) for device in range(count)])


def gather_part(part, order, count):
    held = part[None]
    for stride, size in order:
        pieces = [held] + [swap(held, stride * step, count) for step in range(1, size)]
        held = jnp.concatenate(pieces, 0)
    return held


def scatter_part(parts, order, count):
    held = parts
    for stride, size in reversed(order):
        held = held.reshape((size, held.shape[0] // size) + held.shape[1:])
        total = held[0].astype(jnp.float32)
        for step in range(1, size):
            total = total + swap(held[step], stride * step, count).astype(jnp.float32)
        last = (stride, size) == order[0]
        held = total if last else total.astype(jnp.bfloat16)
    return held[0]


def flat_index(gy):
    return lax.axis_index("gx") * gy + lax.axis_index("gy")


def positions(order, count):
    table = offsets(order)
    inverse = [0] * count
    for position, offset in enumerate(table):
        inverse[offset] = position
    return jnp.array(table, jnp.int32), jnp.array(inverse, jnp.int32)


def gather_rows(shard, shape, me):
    count = shape["gx"] * shape["gy"]
    half = shard.shape[0] // 2
    pieces = []
    for index, order in enumerate(orders(shape)):
        held = gather_part(shard[index * half : (index + 1) * half], order, count)
        inverse = positions(order, count)[1]
        pieces.append(jnp.take(held, inverse[jnp.arange(count) ^ me], axis=0))
    return jnp.concatenate(pieces, 1)


def scatter_rows(grads, shape, me):
    count = shape["gx"] * shape["gy"]
    half = grads.shape[1] // 2
    pieces = []
    for index, order in enumerate(orders(shape)):
        table = positions(order, count)[0]
        parts = jnp.take(grads[:, index * half : (index + 1) * half], me ^ table, axis=0)
        pieces.append(scatter_part(parts, order, count))
    return jnp.concatenate(pieces, 0)


def pad_cols(array, width):
    return jnp.pad(array, ((0, 0),) * (array.ndim - 1) + ((0, width - array.shape[-1]),))


def pack_rows(text_rows, layout_rows, vectors):
    side = D // 3
    layouts = jnp.concatenate([pad_cols(rows, side) for rows in layout_rows], -1)
    packed = jnp.concatenate([text_rows, layouts, pad_cols(vectors, D)[..., None, :]], -2)
    rows = packed.shape[-2]
    extra = -rows % 16
    return jnp.pad(packed, ((0, 0),) * (packed.ndim - 2) + ((0, extra), (0, 0)))


def unpack_rows(packed, text_rows, layout_rows, text_vec, layout_vec):
    side = D // 3
    text = packed[..., :text_rows, :]
    block = packed[..., text_rows : text_rows + layout_rows, :]
    layouts = [block[..., side * index : side * index + DL] for index in range(3)]
    vectors = packed[..., text_rows + layout_rows, :]
    return text, layouts, vectors[..., :text_vec], vectors[..., text_vec : text_vec + layout_vec]


D = 768
DL = 192
HEADS = 12
FF = 4 * D
FFL = 4 * DL


EPS = 1e-05
NEG = -1e30


def matmul(left, right):
    return jnp.dot(left, right, preferred_element_type=jnp.float32)


def contract_rows(left, right):
    return lax.dot_general(
        left, right, (((0,), (0,)), ((), ())), preferred_element_type=jnp.float32
    )


def contract_cols(left, right):
    return lax.dot_general(
        left, right, (((1,), (1,)), ((), ())), preferred_element_type=jnp.float32
    )


def vector_parts(vector, width):
    values = vector.astype(jnp.float32)
    return [values[index * width : (index + 1) * width] for index in range(8)] + [
        values[8 * width :]
    ]


def normalize(resid, gain, shift):
    center = resid - jnp.mean(resid, -1, keepdims=True)
    varian = jnp.mean(center * center, -1, keepdims=True)
    inverse = lax.rsqrt(varian + EPS)
    scaled = center * inverse
    return (scaled * gain + shift, scaled, inverse)


def norm_back(grad, scaled, inverse, gain):
    weighted = grad * gain
    inner = jnp.mean(weighted, -1, keepdims=True)
    across = jnp.mean(weighted * scaled, -1, keepdims=True)
    return inverse * (weighted - inner - scaled * across)


def exact_gelu(value):
    return jax.nn.gelu(value, approximate=False)


def open_stream(inputs, weights, width):
    parts = vector_parts(weights[3], width)
    stacked = weights[0][: 3 * width].reshape(3, width, width)
    projected = jnp.einsum("nd,jde->jne", inputs, stacked, preferred_element_type=jnp.float32)
    query = (projected[0] + parts[0]).astype(jnp.bfloat16)
    keys = projected[1].astype(jnp.bfloat16)
    values = (projected[2] + parts[1]).astype(jnp.bfloat16)
    return (query, keys, values)


def heads_view(array):
    return array.reshape(array.shape[0], HEADS, array.shape[1] // HEADS)


def head_scale(array):
    return 1.0 / math.sqrt(array.shape[1] // HEADS)


def joint_scores(text_query, text_keys, layout_query, layout_keys, length):
    rows = text_query.shape[0]
    text_part = jnp.einsum(
        "qhd,khd->hqk",
        heads_view(text_query),
        heads_view(text_keys),
        preferred_element_type=jnp.float32,
    )
    layout_part = jnp.einsum(
        "qhd,khd->hqk",
        heads_view(layout_query),
        heads_view(layout_keys),
        preferred_element_type=jnp.float32,
    )
    scores = text_part * head_scale(text_query) + layout_part * head_scale(layout_query)
    visible = jnp.arange(rows) < length
    return jnp.where(visible[None, None, :], scores, NEG)


def weigh_values(probs, values):
    mixed = jnp.einsum(
        "hqk,khd->qhd", probs, heads_view(values), preferred_element_type=jnp.float32
    )
    return mixed.reshape(values.shape[0], values.shape[1])


def attend_forward(pieces):
    text_query, text_keys, text_values, layout_query, layout_keys, layout_values, length = pieces
    scores = joint_scores(text_query, text_keys, layout_query, layout_keys, length)
    top = jnp.max(scores, -1, keepdims=True)
    expo = jnp.exp(scores - top)
    total = jnp.sum(expo, -1, keepdims=True)
    probs = (expo / total).astype(jnp.bfloat16)
    text_att = weigh_values(probs, text_values).astype(jnp.bfloat16)
    layout_att = weigh_values(probs, layout_values).astype(jnp.bfloat16)
    return (text_att, layout_att, (top + jnp.log(total))[:, :, 0])


def values_grad(probs_low, grad_out):
    moved = jnp.einsum(
        "hqk,qhd->khd", probs_low, heads_view(grad_out), preferred_element_type=jnp.float32
    )
    return moved.reshape(grad_out.shape[0], grad_out.shape[1]).astype(jnp.bfloat16)


def query_keys_grad(score_grads, query, keys):
    scale = head_scale(query)
    rows, width = query.shape
    query_grad = jnp.zeros((rows, HEADS, width // HEADS), jnp.float32)
    keys_grad = jnp.zeros((rows, HEADS, width // HEADS), jnp.float32)
    for score_grad in score_grads:
        query_grad = query_grad + jnp.einsum(
            "hqk,khd->qhd", score_grad, heads_view(keys), preferred_element_type=jnp.float32
        )
        keys_grad = keys_grad + jnp.einsum(
            "hqk,qhd->khd", score_grad, heads_view(query), preferred_element_type=jnp.float32
        )
    query_grad = query_grad * scale
    keys_grad = keys_grad * scale
    return (
        query_grad.reshape(rows, width).astype(jnp.bfloat16),
        keys_grad.reshape(rows, width).astype(jnp.bfloat16),
    )


def softmax_back(probs, mixed):
    return (probs * (mixed - jnp.sum(probs * mixed, -1, keepdims=True))).astype(jnp.bfloat16)


def attend_backward(pieces):
    (
        text_query,
        text_keys,
        text_values,
        layout_query,
        layout_keys,
        layout_values,
        length,
        log_total,
        text_grad,
        layout_grad,
    ) = pieces
    scores = joint_scores(text_query, text_keys, layout_query, layout_keys, length)
    probs = jnp.exp(scores - log_total[:, :, None])
    probs_low = probs.astype(jnp.bfloat16)
    text_values_grad = values_grad(probs_low, text_grad)
    layout_values_grad = values_grad(probs_low, layout_grad)
    text_mixed = jnp.einsum(
        "qhd,khd->hqk",
        heads_view(text_grad),
        heads_view(text_values),
        preferred_element_type=jnp.float32,
    )
    layout_mixed = jnp.einsum(
        "qhd,khd->hqk",
        heads_view(layout_grad),
        heads_view(layout_values),
        preferred_element_type=jnp.float32,
    )
    text_score_grad = softmax_back(probs, text_mixed)
    layout_score_grad = softmax_back(probs, layout_mixed)
    text_query_grad, text_keys_grad = query_keys_grad((text_score_grad,), text_query, text_keys)
    layout_query_grad, layout_keys_grad = query_keys_grad(
        (text_score_grad, layout_score_grad), layout_query, layout_keys
    )
    return (
        text_query_grad,
        text_keys_grad,
        text_values_grad,
        layout_query_grad,
        layout_keys_grad,
        layout_values_grad,
    )


def close_stream(inputs, attended, weights, width):
    attention_w, up_w, down_w, vector = weights
    parts = vector_parts(vector, width)
    after = matmul(attended, attention_w[3 * width :]) + parts[2]
    first, scaled_one, inverse_one = normalize(
        inputs.astype(jnp.float32) + after, parts[3], parts[4]
    )
    first_low = first.astype(jnp.bfloat16)
    upper = contract_cols(first_low, up_w) + parts[8]
    hidden_act = exact_gelu(upper).astype(jnp.bfloat16)
    final, scaled_two, inverse_two = normalize(
        first + matmul(hidden_act, down_w) + parts[5], parts[6], parts[7]
    )
    return (final, (scaled_one, inverse_one, first_low, upper, hidden_act, scaled_two, inverse_two))


def close_back(cotan, attended, saved, weights, width):
    scaled_one, inverse_one, first_low, upper, hidden_act, scaled_two, inverse_two = saved
    attention_w, up_w, down_w, vector = weights
    parts = vector_parts(vector, width)
    gain_two_grad = jnp.sum(cotan * scaled_two, 0)
    shift_two_grad = jnp.sum(cotan, 0)
    second_grad = norm_back(cotan, scaled_two, inverse_two, parts[6])
    branch_low = second_grad.astype(jnp.bfloat16)
    down_grad = contract_rows(hidden_act, branch_low)
    bias_down_grad = jnp.sum(branch_low.astype(jnp.float32), 0)
    act_grad = contract_cols(branch_low, down_w)
    gelu_back = jax.vjp(exact_gelu, upper)[1]
    upper_low = gelu_back(act_grad)[0].astype(jnp.bfloat16)
    up_grad_flipped = contract_rows(upper_low, first_low)
    bias_up_grad = jnp.sum(upper_low.astype(jnp.float32), 0)
    first_grad = second_grad + matmul(upper_low, up_w)
    gain_one_grad = jnp.sum(first_grad * scaled_one, 0)
    shift_one_grad = jnp.sum(first_grad, 0)
    resid_grad = norm_back(first_grad, scaled_one, inverse_one, parts[3])
    after_low = resid_grad.astype(jnp.bfloat16)
    out_weight_grad = contract_rows(attended, after_low)
    bias_out_grad = jnp.sum(after_low.astype(jnp.float32), 0)
    attended_grad = contract_cols(after_low, attention_w[3 * width :]).astype(jnp.bfloat16)
    tail = (
        bias_out_grad,
        gain_one_grad,
        shift_one_grad,
        bias_down_grad,
        gain_two_grad,
        shift_two_grad,
        bias_up_grad,
    )
    return (resid_grad, attended_grad, out_weight_grad, tail, up_grad_flipped, down_grad)


def open_back(
    inputs,
    resid_grad,
    query_grad,
    keys_grad,
    values_grad,
    out_weight_grad,
    tail,
    attention_w,
    width,
):
    stacked_grad = jnp.stack([query_grad, keys_grad, values_grad])
    weight_grad = jnp.einsum(
        "nd,jne->jde", inputs, stacked_grad, preferred_element_type=jnp.float32
    ).reshape(3 * width, width)
    input_grad = resid_grad + jnp.einsum(
        "jne,jde->nd",
        stacked_grad,
        attention_w[: 3 * width].reshape(3, width, width),
        preferred_element_type=jnp.float32,
    )
    bias_query_grad = jnp.sum(query_grad.astype(jnp.float32), 0)
    bias_value_grad = jnp.sum(values_grad.astype(jnp.float32), 0)
    (
        bias_out_grad,
        gain_one_grad,
        shift_one_grad,
        bias_down_grad,
        gain_two_grad,
        shift_two_grad,
        bias_up_grad,
    ) = tail
    vector_grad = jnp.concatenate(
        [
            bias_query_grad,
            bias_value_grad,
            bias_out_grad,
            gain_one_grad,
            shift_one_grad,
            bias_down_grad,
            gain_two_grad,
            shift_two_grad,
            bias_up_grad,
        ]
    )
    attention_grad = jnp.concatenate([weight_grad, out_weight_grad], 0)
    return (input_grad, attention_grad, vector_grad)


def by_stretch(array, stretches):
    return array.reshape((stretches, array.shape[0] // stretches) + array.shape[1:])


def shards(
    shape,
    text_in,
    layout_in,
    lengths,
    dup_rows,
    text_attention,
    text_up,
    text_down,
    text_vector,
    layout_attention,
    layout_up,
    layout_down,
    layout_vector,
    text_cotangent,
    layout_cotangent,
):
    count = shape["gx"] * shape["gy"]
    me = flat_index(shape["gy"])
    text_rows, layout_rows = text_attention.shape[0], layout_attention.shape[0]
    text_vec, layout_vec = text_vector.shape[0], layout_vector.shape[0]
    packed = pack_rows(
        text_attention,
        [layout_attention, layout_up.T, layout_down],
        jnp.concatenate([text_vector, layout_vector]),
    ).astype(jnp.bfloat16)
    gathered = gather_rows(packed, shape, me)
    up_all = gather_rows(text_up.T.astype(jnp.bfloat16), shape, me).reshape(-1, D)
    down_all = gather_rows(text_down.astype(jnp.bfloat16), shape, me).reshape(-1, D)
    text_all, layouts_all, text_vec_all, layout_vec_all = unpack_rows(
        gathered, text_rows, layout_rows, text_vec, layout_vec
    )
    text_weights = (text_all.reshape(-1, D), up_all, down_all, text_vec_all.reshape(-1))
    layout_weights = tuple(rows.reshape(-1, DL) for rows in layouts_all) + (
        layout_vec_all.reshape(-1),
    )
    stretches = lengths.shape[0]
    text_query, text_keys, text_values = open_stream(text_in, text_weights, D)
    layout_query, layout_keys, layout_values = open_stream(layout_in, layout_weights, DL)
    opened = (text_query, text_keys, text_values, layout_query, layout_keys, layout_values)
    opened_stretches = tuple((by_stretch(array, stretches) for array in opened))
    text_att, layout_att, log_total = lax.map(attend_forward, opened_stretches + (lengths,))
    text_att = text_att.reshape(-1, D)
    layout_att = layout_att.reshape(-1, DL)
    text_final, text_saved = close_stream(text_in, text_att, text_weights, D)
    layout_final, layout_saved = close_stream(layout_in, layout_att, layout_weights, DL)
    text_back, layout_back = text_weights, layout_weights
    span = text_in.shape[0] // stretches
    position = jnp.arange(span)
    keep = (position[None, :] < lengths[:, None]) & (dup_rows.reshape(stretches, span) == 0)
    keep = keep.reshape(-1, 1).astype(jnp.float32)
    text_cot = text_cotangent.astype(jnp.float32) * keep
    layout_cot = layout_cotangent.astype(jnp.float32) * keep
    text_resid, text_att_grad, text_out_w, text_tail, text_up_flipped, text_down_grad = close_back(
        text_cot, text_att, text_saved, text_back, D
    )
    (
        layout_resid,
        layout_att_grad,
        layout_out_w,
        layout_tail,
        layout_up_flipped,
        layout_down_grad,
    ) = close_back(layout_cot, layout_att, layout_saved, layout_back, DL)
    back_pieces = opened_stretches + (
        lengths,
        log_total,
        by_stretch(text_att_grad, stretches),
        by_stretch(layout_att_grad, stretches),
    )
    grads = lax.map(attend_backward, back_pieces)
    (
        text_query_grad,
        text_keys_grad,
        text_values_grad,
        layout_query_grad,
        layout_keys_grad,
        layout_values_grad,
    ) = tuple((array.reshape(-1, array.shape[-1]) for array in grads))
    text_input_grad, text_attention_grad, text_vector_grad = open_back(
        text_in,
        text_resid,
        text_query_grad,
        text_keys_grad,
        text_values_grad,
        text_out_w,
        text_tail,
        text_back[0],
        D,
    )
    layout_input_grad, layout_attention_grad, layout_vector_grad = open_back(
        layout_in,
        layout_resid,
        layout_query_grad,
        layout_keys_grad,
        layout_values_grad,
        layout_out_w,
        layout_tail,
        layout_back[0],
        DL,
    )

    def by_owner(array):
        return array.reshape((count, array.shape[0] // count) + array.shape[1:])

    attention_sum = scatter_rows(
        pack_rows(
            by_owner(text_attention_grad),
            [by_owner(g) for g in (layout_attention_grad, layout_up_flipped, layout_down_grad)],
            jnp.concatenate([by_owner(text_vector_grad), by_owner(layout_vector_grad)], -1),
        ).astype(jnp.bfloat16),
        shape,
        me,
    )
    up_sum = scatter_rows(by_owner(text_up_flipped).astype(jnp.bfloat16), shape, me)
    down_sum = scatter_rows(by_owner(text_down_grad).astype(jnp.bfloat16), shape, me)
    text_attention_sum, layout_sums, text_vec_sum, layout_vec_sum = unpack_rows(
        attention_sum, text_rows, layout_rows, text_vec, layout_vec
    )
    return (
        text_final.astype(jnp.bfloat16),
        layout_final.astype(jnp.bfloat16),
        text_input_grad.astype(jnp.bfloat16),
        layout_input_grad.astype(jnp.bfloat16),
        text_attention_sum,
        up_sum.T,
        down_sum,
        text_vec_sum,
        layout_sums[0],
        layout_sums[1].T,
        layout_sums[2],
        layout_vec_sum,
    )


BF = jnp.bfloat16
F32 = jnp.float32
CAT = 128
TEXT_LANES = D // HEADS
LAYOUT_LANES = DL // HEADS
MASK_LANE = TEXT_LANES + LAYOUT_LANES
VMEM_SPEC = pl.BlockSpec(memory_space=pltpu.VMEM)
SMEM_SPEC = pl.BlockSpec(memory_space=pltpu.SMEM)
ANY_SPEC = pl.BlockSpec(memory_space=pl.ANY)
STAGED = "staged"
LATE = "late"


def nn(left, right):
    return lax.dot_general(left, right, (((1,), (0,)), ((), ())), preferred_element_type=F32)


def nt(left, right):
    return lax.dot_general(left, right, (((1,), (1,)), ((), ())), preferred_element_type=F32)


def tn(left, right):
    return lax.dot_general(left, right, (((0,), (0,)), ((), ())), preferred_element_type=F32)


def row_mean(array):
    return jnp.sum(array, -1, keepdims=True) * (1.0 / array.shape[-1])


def col_sum(array):
    return jnp.sum(array, 0, keepdims=True)


def norm(resid):
    center = resid - row_mean(resid)
    inverse = lax.rsqrt(row_mean(center * center) + EPS)
    return center * inverse, inverse


def norm_grad(grad, scaled, inverse, gain):
    weighted = grad * gain
    return inverse * (weighted - row_mean(weighted) - scaled * row_mean(weighted * scaled))


def kernel_call(body, outs, ins, scratch=(), room=60):
    copied = [index for index, (_, spec) in enumerate(ins) if spec in (STAGED, LATE)]
    late = [index for index, (_, spec) in enumerate(ins) if spec == LATE]

    def with_copies(*refs):
        rooms, sems = refs[len(refs) - len(copied) - 1 : -1], refs[-1]
        given = list(refs[: len(refs) - len(copied) - 1])
        copies = {}
        for index, target in zip(copied, rooms):
            copies[index] = pltpu.make_async_copy(given[index], target, sems.at[len(copies)])
            given[index] = target
        for copy in copies.values():
            copy.start()
        for index in copied:
            if index not in late:
                copies[index].wait()

        def settle():
            for index in late:
                copies[index].wait()

        body(*([settle] if late else []), *given)

    scratch = list(scratch)
    if copied:
        scratch += [pltpu.VMEM(ins[index][0].shape, ins[index][0].dtype) for index in copied]
        scratch.append(pltpu.SemaphoreType.DMA((len(copied),)))
    return pl.pallas_call(
        with_copies if copied else body,
        out_shape=[jax.ShapeDtypeStruct(shape, kind) for shape, kind, _ in outs],
        in_specs=[ANY_SPEC if spec in (STAGED, LATE) else spec for _, spec in ins],
        out_specs=[spec for _, _, spec in outs],
        scratch_shapes=scratch,
        compiler_params=pltpu.CompilerParams(vmem_limit_bytes=room * 2**20),
    )(*[array for array, _ in ins])


def stack_rows(parts):
    rows = [part.shape[0] for part in parts]
    width = parts[0].shape[1]

    def body(*refs):
        out, sems = refs[len(parts)], refs[len(parts) + 1]
        copies, base = [], 0
        for index, size in enumerate(rows):
            copies.append(
                pltpu.make_async_copy(refs[index], out.at[base : base + size], sems.at[index])
            )
            base += size
        for copy in copies:
            copy.start()
        for copy in copies:
            copy.wait()

    return kernel_call(
        body,
        [((sum(rows), width), BF, ANY_SPEC)],
        [(part, VMEM_SPEC) for part in parts],
        [pltpu.SemaphoreType.DMA((len(parts),))],
        room=8,
    )[0]


def turn(dims, core_bit):
    (x, _), _, _, (y, _) = dims
    return (x, y) if core_bit else (y, x)


def swap_turn(array, dims, which, count):
    core = dims[1][0]
    return lax.ppermute(
        array,
        AXES,
        [(device, device ^ turn(dims, device // core % 2)[which]) for device in range(count)],
    )


def spread(held, dims, count):
    pieces = [held]
    for source, which in ((0, 0), (0, 1), (1, 1)):
        pieces.append(swap_turn(pieces[source], dims, which, count))
    return pieces


def gather_parts(attention, feed, shape):
    count = shape["gx"] * shape["gy"]
    dims = exchange_dims(shape)
    _, (core, _), (z, nz), _ = dims
    both = jnp.concatenate([attention, feed], 0)

    def shifted(shard, step):
        return swap(shard, z * step, count)

    def exchanged(held):
        pieces = spread(held, dims, count)
        for index in range(4):
            pieces.append(swap(pieces[index], core, count))
        return pieces

    firsts = [shifted(attention, step) for step in range(1, nz)]
    own = stack_rows(spread(both, dims, count))
    own = [own, swap(own, core, count)]
    first = exchanged(stack_rows(firsts))
    seconds = [shifted(feed, step) for step in range(1, nz)]
    return own, first, exchanged(stack_rows(seconds))


def part_blocks(me, dims, own, others, skip, rows, both):
    (x, _), (core, _), (z, nz), (y, _) = dims
    odd = me // core % 2
    low = jnp.where(odd == 1, x, y)
    top = jnp.where(odd == 1, y, x)
    mine, partner = [0, low, top, x ^ y], [core, core ^ top, core ^ low, core ^ x ^ y]
    blocks = []
    for ref, offsets in zip(own, (mine, partner)):
        for index, offset in enumerate(offsets):
            base = both * index + skip
            blocks.append((ref.at[base : base + rows], me ^ offset))
    for ref, offset in zip(others, mine + partner):
        for step in range(1, nz):
            blocks.append((ref.at[(step - 1) * rows : step * rows], me ^ (offset ^ (z * step))))
    return blocks


def fetch_blocks(blocks, place, sems):
    copies = []
    for block, device in blocks:
        for source, target in place(block, device):
            copies.append(pltpu.make_async_copy(source, target, sems.at[len(copies)]))
    return copies


def exchange_slot(me, dims, device):
    (x, _), (core, _), (z, nz), (y, _) = dims
    odd = device // core % 2
    away = me ^ device
    across = [away // stride % 2 for stride in (x, y)]
    top = odd * across[0] + (1 - odd) * across[1]
    low = odd * across[1] + (1 - odd) * across[0]
    return away // z % nz * 4 + top * 2 + low, away // core % 2


def send_block(me, dims, device, source, keep, send, sems):
    slot, far = exchange_slot(me, dims, device)
    sem = sems.at[device]

    @pl.when(far == 0)
    def _():
        pltpu.make_async_copy(source, keep.at[slot], sem).start()

    @pl.when(far == 1)
    def _():
        pltpu.make_async_copy(source, send.at[slot], sem).start()


def store_block(me, dims, device, block, keep, send):
    slot, far = exchange_slot(me, dims, device)

    @pl.when(far == 0)
    def _():
        keep[slot] = block[...]

    @pl.when(far == 1)
    def _():
        send[slot] = block[...]


def added(*terms):
    total = terms[0].astype(F32)
    for term in terms[1:]:
        total = total + term.astype(F32)
    return total


def reduce_part(keep, send, dims, count):
    _, (core, _), (z, nz), _ = dims
    rows, width = keep.shape[1:]

    def sent(how, array, *offsets):
        return how(array.astype(BF), *offsets, count)

    def turned(which):
        return lambda array, total: swap_turn(array, dims, which, total)

    def gated(*tokens):
        held = lax.optimization_barrier((keep, got, *tokens))[:2]
        return [array.reshape(nz, 2, 2, rows, width) for array in held]

    got = swap(send, core, count)
    kept = gated()
    far = sent(turned(0), added(*[a[1:, 1] for a in kept]).reshape(-1, rows, width))
    own = sent(turned(0), added(*[a[0, 1] for a in kept]))
    kept = gated(far)
    far = far.reshape(nz - 1, 2, rows, width)
    far_next = sent(turned(1), added(*[a[1:, 0, 1] for a in kept], far[:, 1]))
    kept = gated(own, far_next)
    own_next = sent(turned(1), added(*[a[0, 0, 1] for a in kept], own[1]))
    kept = gated(far_next)
    result = 0.0
    for step in range(1, nz):
        part = added(*[a[step, 0, 0] for a in kept], far[step - 1, 0], far_next[step - 1])
        result = result + sent(swap, part, z * step).astype(F32)
    return result + added(*[a[0, 0, 0] for a in kept], own[0], own_next)


def vector_rows(read, width, segment, count):
    rows = []
    for row in range(segment * count // width):
        at, stop, parts = row * width, (row + 1) * width, []
        while at < stop:
            device, start = at // segment, at % segment
            take = min(segment - start, stop - at)
            parts.append(read(device, start, start + take))
            at += take
        rows.append(parts[0] if len(parts) == 1 else jnp.concatenate(parts, 1))
    return rows


def head_forward(q, k, v):
    scores = nt(k, q)
    top = jnp.max(scores, 0, keepdims=True)
    expo = jnp.exp(scores - top)
    total = col_sum(expo)
    probs = (expo * (1.0 / total)).astype(BF)
    return tn(v, probs).T.astype(BF), top + jnp.log(total)


def project(me, length, text_in, layout_in, pieces, sizes, dims, middle):
    count, text_rows, layout_rows, text_vec, layout_vec = sizes
    rows = text_in.shape[0]
    packed = pieces[0].shape[0] // 4 - 2 * text_rows

    def body(*refs):
        me_ref, length_ref, x_ref, xl_ref = refs[:4]
        piece_refs = refs[4 : 4 + len(pieces)]
        (
            q_out,
            k_out,
            v_out,
            weight_out,
            layout_ref,
            up_ref,
            down_ref,
            text_vec_ref,
            layout_vec_ref,
            mixed,
            lse_ref,
            q_ref,
            k_ref,
            v_ref,
            weight,
            tail,
            sems,
            out_sems,
        ) = refs[4 + len(pieces) :]

        def place(source, device):
            base = pl.multiple_of(device * text_rows, 16)
            return [
                (source.at[0:text_rows], weight.at[pl.ds(base, text_rows)]),
                (source.at[text_rows:packed], tail.at[device]),
            ]

        blocks = part_blocks(
            me_ref[0], dims, piece_refs[:2], piece_refs[2:], 0, packed, packed + 2 * text_rows
        )
        copies = fetch_blocks(blocks, place, sems)
        for copy in copies:
            copy.start()
        for copy in copies:
            copy.wait()
        outs = [pltpu.make_async_copy(weight, weight_out, out_sems.at[3])]
        outs[0].start()
        side = D // 3
        for device in range(count):
            block = pl.ds(device * layout_rows, layout_rows)
            for index, ref in enumerate((layout_ref, up_ref, down_ref)):
                ref[block, :] = tail[device, 0:layout_rows, side * index : side * index + DL]

        def read_text(device, start, stop):
            return tail[device, layout_rows : layout_rows + 1, start:stop].astype(F32)

        def read_layout(device, start, stop):
            return read_text(device, text_vec + start, text_vec + stop)

        for index, row in enumerate(vector_rows(read_text, D, text_vec, count)):
            text_vec_ref[index] = row
        for index, row in enumerate(vector_rows(read_layout, DL, layout_vec, count)):
            layout_vec_ref[index] = row
        x, xl = x_ref[...], xl_ref[...]
        seen = lax.broadcasted_iota(jnp.int32, (rows, CAT - MASK_LANE), 0) < length_ref[0]
        lane = lax.broadcasted_iota(jnp.int32, (rows, CAT - MASK_LANE), 1)
        ones = jnp.where(lane == 0, 1.0, 0.0).astype(BF)
        hidden = jnp.where((lane == 0) & jnp.logical_not(seen), NEG, 0.0).astype(BF)
        nothing = jnp.zeros((rows, CAT - MASK_LANE), BF)
        for index, (ref, out, extra) in enumerate(
            ((q_ref, q_out, ones), (k_ref, k_out, hidden), (v_ref, v_out, nothing))
        ):
            text = nn(x, weight[index * D : (index + 1) * D, :])
            layout = nn(xl, layout_ref[index * DL : (index + 1) * DL, :])
            if index != 1:
                text = text + text_vec_ref[index // 2]
                layout = layout + layout_vec_ref[index // 2]
            text, layout = text.astype(BF), layout.astype(BF)
            if index == 0:
                text = text * (1.0 / math.sqrt(TEXT_LANES))
                layout = layout * (1.0 / math.sqrt(LAYOUT_LANES))
            for head in range(HEADS):
                ref[head] = jnp.concatenate(
                    [
                        text[:, TEXT_LANES * head : TEXT_LANES * (head + 1)],
                        layout[:, LAYOUT_LANES * head : LAYOUT_LANES * (head + 1)],
                        extra,
                    ],
                    1,
                )
            outs.append(pltpu.make_async_copy(ref, out, out_sems.at[index]))
            outs[-1].start()

        def head_step(head, carry):
            mixed[head], lse_ref[head] = head_forward(q_ref[head], k_ref[head], v_ref[head])
            return carry

        lax.fori_loop(0, middle, head_step, 0)
        for copy in outs:
            copy.wait()

    cat = ((HEADS, rows, CAT), BF, ANY_SPEC)
    room = pltpu.VMEM((HEADS, rows, CAT), BF)
    return kernel_call(
        body,
        [
            cat,
            cat,
            cat,
            ((4 * D, D), BF, ANY_SPEC),
            ((4 * DL, DL), BF, VMEM_SPEC),
            ((FFL, DL), BF, VMEM_SPEC),
            ((FFL, DL), BF, VMEM_SPEC),
            ((12, 1, D), F32, VMEM_SPEC),
            ((12, 1, DL), F32, VMEM_SPEC),
            ((middle, rows, CAT), BF, VMEM_SPEC),
            ((middle, 1, rows), F32, VMEM_SPEC),
        ],
        [(me, SMEM_SPEC), (length, SMEM_SPEC), (text_in, STAGED), (layout_in, STAGED)]
        + [(array, ANY_SPEC) for array in pieces],
        [
            room,
            room,
            room,
            pltpu.VMEM((4 * D, D), BF),
            pltpu.VMEM((count, packed - text_rows, D), BF),
            pltpu.SemaphoreType.DMA((2 * count,)),
            pltpu.SemaphoreType.DMA((4,)),
        ],
    )


def heads_out(ref, start, stop):
    heads = range(start, stop)
    text = jnp.concatenate([ref[head, :, 0:TEXT_LANES] for head in heads], 1)
    layout = jnp.concatenate([ref[head, :, TEXT_LANES:MASK_LANE] for head in heads], 1)
    return text, layout


def attend(text_in, layout_in, query, keys, values, first, weight, layout_w, text_vec, layout_vec):
    rows = text_in.shape[0]
    middle = first.shape[0]
    late = HEADS - middle

    def body(
        x_ref,
        xl_ref,
        q_any,
        k_any,
        v_any,
        first_ref,
        weight_any,
        layout_ref,
        tv_ref,
        lv_ref,
        out_t,
        out_l,
        lse_ref,
        norm_t,
        inv_t,
        norm_l,
        inv_l,
        q_ref,
        k_ref,
        v_ref,
        mixed,
        weight,
        sems,
    ):
        fetches = [
            pltpu.make_async_copy(source.at[middle:HEADS], target, sems.at[index])
            for index, (source, target) in enumerate(
                ((q_any, q_ref), (k_any, k_ref), (v_any, v_ref))
            )
        ]
        fetches.append(pltpu.make_async_copy(weight_any.at[3 * D : 4 * D], weight, sems.at[3]))
        for fetch in fetches:
            fetch.start()
        for fetch in fetches[:3]:
            fetch.wait()

        def head_step(head, carry):
            mixed[head], lse_ref[head] = head_forward(q_ref[head], k_ref[head], v_ref[head])
            return carry

        lax.fori_loop(0, late, head_step, 0)
        parts = [heads_out(first_ref, 0, middle), heads_out(mixed, 0, late)]
        text = jnp.concatenate([part[0] for part in parts], 1)
        layout = jnp.concatenate([part[1] for part in parts], 1)
        out_t[...] = text
        out_l[...] = layout
        fetches[3].wait()
        after = nn(text, weight[...]) + tv_ref[2]
        norm_t[...], inv_t[...] = norm(x_ref[...].astype(F32) + after)
        after = nn(layout, layout_ref[3 * DL : 4 * DL, :]) + lv_ref[2]
        norm_l[...], inv_l[...] = norm(xl_ref[...].astype(F32) + after)

    room = pltpu.VMEM((late, rows, CAT), BF)
    return kernel_call(
        body,
        [
            ((rows, D), BF, VMEM_SPEC),
            ((rows, DL), BF, VMEM_SPEC),
            ((late, 1, rows), F32, VMEM_SPEC),
            ((rows, D), F32, VMEM_SPEC),
            ((rows, 1), F32, VMEM_SPEC),
            ((rows, DL), F32, VMEM_SPEC),
            ((rows, 1), F32, VMEM_SPEC),
        ],
        [
            (text_in, STAGED),
            (layout_in, STAGED),
            (query, ANY_SPEC),
            (keys, ANY_SPEC),
            (values, ANY_SPEC),
            (first, VMEM_SPEC),
            (weight, ANY_SPEC),
            (layout_w, VMEM_SPEC),
            (text_vec, VMEM_SPEC),
            (layout_vec, VMEM_SPEC),
        ],
        [room, room, room, room, pltpu.VMEM((D, D), BF), pltpu.SemaphoreType.DMA((4,))],
    )


def gelu_both(value):
    bell = jnp.exp2(value * value * (-0.5 / math.log(2.0)))
    near = 1.0 / (1.0 + jnp.abs(value) * (0.3275911 * math.sqrt(0.5)))
    tail = jnp.full_like(value, 0.5 * 1.061405429)
    for factor in (-1.453152027, 1.421413741, -0.284496736, 0.254829592):
        tail = tail * near + 0.5 * factor
    tail = tail * near * bell
    below = jnp.where(value < 0.0, tail, 1.0 - tail)
    return value * below, below + value * bell * (1.0 / math.sqrt(2.0 * math.pi))


def feed_stream(
    norm_ref, vec_ref, cot_ref, keep, up, down, bias, arrived, hidden, slope, blocks, write, outs
):
    out_ref, grad_ref, vec_out = outs
    first = norm_ref[...] * vec_ref[3] + vec_ref[4]
    low = first.astype(BF)

    def forward(block, total):
        arrived(block)
        act, rise = gelu_both(nt(low, up(block)) + bias(block))
        act = act.astype(BF)
        hidden[block] = act
        slope[block] = rise
        return total + nn(act, down(block))

    def loop(body, start):
        return body(0, start) if blocks == 1 else lax.fori_loop(0, blocks, body, start)

    branch = loop(forward, jnp.zeros_like(first))
    scaled, inverse = norm(first + branch + vec_ref[5])
    out_ref[...] = (scaled * vec_ref[6] + vec_ref[7]).astype(BF)
    cotan = cot_ref[...].astype(F32) * keep
    vec_out[1] = col_sum(cotan * scaled)
    vec_out[2] = col_sum(cotan)
    second = norm_grad(cotan, scaled, inverse, vec_ref[6])
    branch_low = second.astype(BF)
    vec_out[0] = col_sum(branch_low.astype(F32))

    def backward(block, total):
        act_grad = nt(branch_low, down(block))
        upper_low = (act_grad * slope[block]).astype(BF)
        write(
            block,
            tn(upper_low, low),
            tn(hidden[block], branch_low),
            col_sum(upper_low.astype(F32)),
        )
        return total + nn(upper_low, up(block))

    grad_ref[...] = loop(backward, second)


def feed(me, keep_rows, norm_t, tv, cot_t, pieces, dims, text_rows):
    rows = norm_t.shape[0]
    count = 8 * dims[2][1]
    blocks = FF // D
    per_block = D // text_rows
    both = pieces[0].shape[0] // 4
    skip = both - 2 * text_rows

    def body(*refs):
        me_ref, keep_ref, nt_ref, tv_ref, ct_ref = refs[:5]
        piece_refs = refs[5 : 5 + len(pieces)]
        (
            out_t,
            grad_t,
            vec_t,
            both_keep,
            both_send,
            up,
            down,
            hidden,
            slope,
            grads,
            weight_sems,
            sems,
        ) = refs[5 + len(pieces) :]
        mine = me_ref[0]
        listed = part_blocks(
            mine, dims, piece_refs[:2], piece_refs[2:], skip, 2 * text_rows, both
        )
        for source, device in listed:
            at = pl.ds(pl.multiple_of(device * text_rows, 16), text_rows)
            sem = weight_sems.at[device]
            pltpu.make_async_copy(source.at[0:text_rows], up.at[at], sem).start()
            pltpu.make_async_copy(source.at[text_rows:], down.at[at], sem).start()

        def arrived(block):
            for part in range(per_block):
                sem = weight_sems.at[block * per_block + part]
                for ref in (up, down):
                    pltpu.make_async_copy(ref.at[0:text_rows], ref.at[0:text_rows], sem).wait()

        def rows_of(ref):
            return lambda block: ref[pl.ds(pl.multiple_of(block * D, 16), D), :]

        def write_t(block, one, two, bias):
            vec_t[3 + block] = bias
            for part in range(per_block):
                at = slice(part * text_rows, (part + 1) * text_rows)
                device = block * per_block + part
                grads[device, 0:text_rows] = one[at].astype(BF)
                grads[device, text_rows:] = two[at].astype(BF)
                send_block(mine, dims, device, grads.at[device], both_keep, both_send, sems)

        feed_stream(
            nt_ref,
            tv_ref,
            ct_ref,
            keep_ref[...],
            rows_of(up),
            rows_of(down),
            lambda block: tv_ref[8 + block],
            arrived,
            hidden,
            slope,
            blocks,
            write_t,
            (out_t, grad_t, vec_t),
        )
        for device in range(count):
            pltpu.make_async_copy(grads.at[device], both_keep.at[0], sems.at[device]).wait()

    part = ((count // 2, 2 * text_rows, D), BF, ANY_SPEC)
    return kernel_call(
        body,
        [
            ((rows, D), BF, VMEM_SPEC),
            ((rows, D), F32, VMEM_SPEC),
            ((3 + blocks, 1, D), F32, VMEM_SPEC),
            part,
            part,
        ],
        [
            (me, SMEM_SPEC),
            (keep_rows, STAGED),
            (norm_t, STAGED),
            (tv, VMEM_SPEC),
            (cot_t, STAGED),
        ]
        + [(array, ANY_SPEC) for array in pieces],
        [
            pltpu.VMEM((FF, D), BF),
            pltpu.VMEM((FF, D), BF),
            pltpu.VMEM((blocks, rows, D), BF),
            pltpu.VMEM((blocks, rows, D), F32),
            pltpu.VMEM((count, 2 * text_rows, D), BF),
            pltpu.SemaphoreType.DMA((count,)),
            pltpu.SemaphoreType.DMA((count,)),
        ],
    )


def close_back_pair(keep_rows, layout_feed, text_side, layout_side, weight, layout_w, tv, lv):
    norm_l, cot_l, lu, ld = layout_feed
    rows = norm_l.shape[0]
    parts = FFL // DL

    def body(
        settle,
        keep_ref,
        nl_ref,
        cl_ref,
        lu_ref,
        ld_ref,
        il_ref,
        ol_ref,
        gt_ref,
        nt_ref,
        it_ref,
        ot_ref,
        layout_ref,
        weight_any,
        tv_ref,
        lv_ref,
        out_l,
        feed_l,
        lu_grad,
        ld_grad,
        resid_t,
        resid_l,
        out_wt,
        out_wl,
        vec_t,
        vec_l,
        dout,
        gl_ref,
        hidden_l,
        slope_l,
        weight,
        sem,
    ):
        fetch = pltpu.make_async_copy(weight_any.at[3 * D : 4 * D], weight, sem)
        fetch.start()
        bias_l = jnp.concatenate([lv_ref[8 + part] for part in range(parts)], 1)

        def write_l(block, one, two, bias):
            lu_grad[...] = one.astype(BF)
            ld_grad[...] = two.astype(BF)
            for part in range(parts):
                feed_l[3 + part] = bias[:, part * DL : (part + 1) * DL]

        feed_stream(
            nl_ref,
            lv_ref,
            cl_ref,
            keep_ref[...],
            lambda block: lu_ref[...],
            lambda block: ld_ref[...],
            lambda block: bias_l,
            lambda block: None,
            hidden_l,
            slope_l,
            1,
            write_l,
            (out_l, gl_ref, feed_l),
        )
        settle()

        def close(grad, scaled, inverse, vec, mixed, vec_out, resid_ref, wide):
            vec_out[1] = col_sum(grad * scaled)
            vec_out[2] = col_sum(grad)
            resid = norm_grad(grad, scaled, inverse, vec[3])
            resid_ref[...] = resid
            after = resid.astype(BF)
            vec_out[0] = col_sum(after.astype(F32))
            return after, tn(mixed, after).astype(BF), nt(after, wide()).astype(BF)

        def wide_l():
            return layout_ref[3 * DL : 4 * DL, :]

        def wide_t():
            fetch.wait()
            return weight[...]

        _, out_wl[...], att_l = close(
            gl_ref[...], nl_ref[...], il_ref[...], lv_ref, ol_ref[...], vec_l, resid_l, wide_l
        )
        _, out_wt[...], att_t = close(
            gt_ref[...], nt_ref[...], it_ref[...], tv_ref, ot_ref[...], vec_t, resid_t, wide_t
        )
        nothing = jnp.zeros((rows, CAT - MASK_LANE), BF)
        for head in range(HEADS):
            dout[head] = jnp.concatenate(
                [
                    att_t[:, TEXT_LANES * head : TEXT_LANES * (head + 1)],
                    att_l[:, LAYOUT_LANES * head : LAYOUT_LANES * (head + 1)],
                    nothing,
                ],
                1,
            )

    return kernel_call(
        body,
        [
            ((rows, DL), BF, VMEM_SPEC),
            ((3 + parts, 1, DL), F32, VMEM_SPEC),
            ((FFL, DL), BF, VMEM_SPEC),
            ((FFL, DL), BF, VMEM_SPEC),
            ((rows, D), F32, VMEM_SPEC),
            ((rows, DL), F32, VMEM_SPEC),
            ((D, D), BF, VMEM_SPEC),
            ((DL, DL), BF, VMEM_SPEC),
            ((3, 1, D), F32, VMEM_SPEC),
            ((3, 1, DL), F32, VMEM_SPEC),
            ((HEADS, rows, CAT), BF, VMEM_SPEC),
        ],
        [(array, STAGED) for array in (keep_rows, norm_l, cot_l, lu, ld)]
        + [(array, LATE) for array in (*layout_side, *text_side, layout_w)]
        + [(weight, ANY_SPEC), (tv, VMEM_SPEC), (lv, VMEM_SPEC)],
        [
            pltpu.VMEM((rows, DL), F32),
            pltpu.VMEM((1, rows, FFL), BF),
            pltpu.VMEM((1, rows, FFL), F32),
            pltpu.VMEM((D, D), BF),
            pltpu.SemaphoreType.DMA,
        ],
    )


def heads_back(query, keys, values, lse, dout, start, stop):
    rows = query.shape[1]
    size = stop - start

    def body(q_any, k_any, v_any, lse_any, do_any, dq, dk, dv, q_ref, k_ref, v_ref, do_ref, lse_ref, sems):
        copies = [
            pltpu.make_async_copy(source.at[start:stop], target, sems.at[index])
            for index, (source, target) in enumerate(
                ((q_any, q_ref), (k_any, k_ref), (v_any, v_ref), (do_any, do_ref))
            )
        ]
        copies.append(pltpu.make_async_copy(lse_any, lse_ref, sems.at[4]))
        for copy in copies:
            copy.start()
        for copy in copies:
            copy.wait()
        is_text = lax.broadcasted_iota(jnp.int32, (rows, CAT), 1) < TEXT_LANES
        text_row = lax.broadcasted_iota(jnp.int32, (CAT, rows), 0) < TEXT_LANES

        def head_step(head, carry):
            q, k, v, do = q_ref[head], k_ref[head], v_ref[head], do_ref[head]
            probs = jnp.exp(nt(k, q) - lse_ref[head])
            dv[head] = nn(probs.astype(BF), do).astype(BF)
            none = jnp.zeros_like(v)
            mixed = nt(jnp.where(is_text, v, none), do)
            score_t = (probs * (mixed - col_sum(probs * mixed))).astype(BF)
            mixed = nt(jnp.where(is_text, none, v), do)
            score_l = (probs * (mixed - col_sum(probs * mixed))).astype(BF)
            dk_t = nn(score_t, q)
            dk_l = nn(score_l, q)
            dk[head] = jnp.where(is_text, dk_t, dk_t + dk_l).astype(BF)
            dq_t = tn(k, score_t)
            dq_l = tn(k, score_l)
            scaled = jnp.where(
                text_row,
                dq_t * (1.0 / math.sqrt(TEXT_LANES)),
                (dq_t + dq_l) * (1.0 / math.sqrt(LAYOUT_LANES)),
            )
            dq[head] = scaled.T.astype(BF)
            return carry

        lax.fori_loop(0, size, head_step, 0)

    cat = pltpu.VMEM((size, rows, CAT), BF)
    part = ((size, rows, CAT), BF, VMEM_SPEC)
    return kernel_call(
        body,
        [part, part, part],
        [(array, ANY_SPEC) for array in (query, keys, values, lse)] + [(dout, ANY_SPEC)],
        [cat, cat, cat, cat, pltpu.VMEM((size, 1, rows), F32), pltpu.SemaphoreType.DMA((5,))],
        room=16,
    )


def weight_grads(me, text_in, layout_in, backs, out_w, ffn_l, vecs, dims, sizes):
    count, text_rows, layout_rows, text_vec, layout_vec = sizes
    rows = text_in.shape[0]
    packed = text_rows + layout_rows + 8
    groups = len(backs)

    def body(*refs):
        me_ref, x_ref, xl_ref = refs[:3]
        back_refs = refs[3 : 3 + 3 * groups]
        (
            out_wt,
            out_wl,
            lu_grad,
            ld_grad,
            close_t,
            close_l,
            feed_t,
            feed_l,
            joined_t,
            joined_l,
            keep,
            send,
            pack,
            att_l,
        ) = refs[3 + 3 * groups :]
        mine = me_ref[0]
        x, xl = x_ref[...], xl_ref[...]
        side = D // 3
        for device in range(count):
            pack[device, text_rows : text_rows + layout_rows, :] = jnp.zeros((layout_rows, D), BF)
        per_block = D // text_rows
        for index in range(3):
            refs_of = [back_refs[3 * group + index] for group in range(groups)]
            pieces = [heads_out(ref, 0, ref.shape[0]) for ref in refs_of]
            joined_t[index] = jnp.concatenate([text for text, _ in pieces], 1)
            joined_l[index] = jnp.concatenate([layout for _, layout in pieces], 1)
            att_l[index * DL : (index + 1) * DL, :] = tn(xl, joined_l[index]).astype(BF)
        att_l[3 * DL : 4 * DL, :] = out_wl[...]
        for device in range(count):
            block = pl.ds(device * layout_rows, layout_rows)
            for index, ref in enumerate((att_l, lu_grad, ld_grad)):
                pack[
                    device,
                    text_rows : text_rows + layout_rows,
                    side * index : side * index + DL,
                ] = ref[block, :]

        def vector(joined, close, feeds):
            rows_of = [col_sum(joined[0].astype(F32)), col_sum(joined[2].astype(F32))]
            rows_of += [close[0], close[1], close[2], feeds[0], feeds[1], feeds[2]]
            return rows_of + [feeds[3 + block] for block in range(FF // D)]

        text_rows_of = vector(joined_t, close_t, feed_t)
        layout_rows_of = vector(joined_l, close_l, feed_l)

        def segment(all_rows, width, start, size):
            parts, stop = [], start + size
            while start < stop:
                row, at = start // width, start % width
                take = min(width - at, stop - start)
                parts.append(all_rows[row][:, at : at + take])
                start += take
            return parts

        row = lax.broadcasted_iota(jnp.int32, (8, D), 0)
        for device in range(count):
            parts = segment(text_rows_of, D, device * text_vec, text_vec)
            parts += segment(layout_rows_of, DL, device * layout_vec, layout_vec)
            parts.append(jnp.zeros((1, D - text_vec - layout_vec), F32))
            line = jnp.concatenate(parts, 1)
            pack[device, text_rows + layout_rows :, :] = jnp.where(
                row == 0, jnp.broadcast_to(line, (8, D)), 0.0
            ).astype(BF)
        for index in (3, 0, 1, 2):
            grad = out_wt[...] if index == 3 else tn(x, joined_t[index]).astype(BF)
            for part in range(per_block):
                device = index * per_block + part
                pack[device, 0:text_rows, :] = grad[part * text_rows : (part + 1) * text_rows]

        def place(device, carry):
            store_block(mine, dims, device, pack.at[device], keep, send)
            return carry

        lax.fori_loop(0, count, place, 0)

    part = ((count // 2, packed, D), BF, VMEM_SPEC)
    arrays = []
    for back in backs:
        arrays += list(back)
    arrays += [*out_w, *ffn_l, *vecs]
    return kernel_call(
        body,
        [((3, rows, D), BF, VMEM_SPEC), ((3, rows, DL), BF, VMEM_SPEC), part, part],
        [(me, SMEM_SPEC), (text_in, STAGED), (layout_in, STAGED)]
        + [(array, VMEM_SPEC) for array in arrays],
        [
            pltpu.VMEM((count, packed, D), BF),
            pltpu.VMEM((4 * DL, DL), BF),
        ],
        room=22,
    )


def input_grads(joined_t, joined_l, resid_t, resid_l, weight, layout_w):
    rows = resid_t.shape[0]

    def body(jt, jl, rt, rl, weight_any, layout_ref, grad_t, grad_l, weight, sem):
        fetch = pltpu.make_async_copy(weight_any.at[0 : 3 * D], weight, sem)
        fetch.start()
        total = rl[...]
        for index in range(3):
            total = total + nt(jl[index], layout_ref[index * DL : (index + 1) * DL, :])
        grad_l[...] = total.astype(BF)
        fetch.wait()
        total = rt[...]
        for index in range(3):
            total = total + nt(jt[index], weight[index * D : (index + 1) * D, :])
        grad_t[...] = total.astype(BF)

    return kernel_call(
        body,
        [((rows, D), BF, VMEM_SPEC), ((rows, DL), BF, VMEM_SPEC)],
        [(array, VMEM_SPEC) for array in (joined_t, joined_l, resid_t, resid_l)]
        + [(weight, ANY_SPEC), (layout_w, STAGED)],
        [pltpu.VMEM((3 * D, D), BF), pltpu.SemaphoreType.DMA],
        room=20,
    )


def shards_fast(
    shape,
    text_in,
    layout_in,
    lengths,
    dup_rows,
    text_attention,
    text_up,
    text_down,
    text_vector,
    layout_attention,
    layout_up,
    layout_down,
    layout_vector,
    text_cotangent,
    layout_cotangent,
):
    count = shape["gx"] * shape["gy"]
    dims = exchange_dims(shape)
    me = flat_index(shape["gy"]).reshape(1).astype(jnp.int32)
    text_rows, layout_rows = text_attention.shape[0], layout_attention.shape[0]
    text_vec, layout_vec = text_vector.shape[0], layout_vector.shape[0]
    packed = pack_rows(
        text_attention,
        [layout_attention, layout_up.T, layout_down],
        jnp.concatenate([text_vector, layout_vector]),
    ).astype(BF)
    sizes = (count, text_rows, layout_rows, text_vec, layout_vec)
    feed_shard = jnp.concatenate([text_up.T, text_down], 0).astype(BF)
    own, first_parts, second_parts = gather_parts(packed, feed_shard, shape)
    middle = HEADS // 2
    q, k, v, weight, layout_w, lu, ld, tv, lv, first, lse_a = project(
        me, lengths, text_in, layout_in, own + first_parts, sizes, dims, middle
    )
    out_t, out_l, lse_b, norm_t, inv_t, norm_l, inv_l = attend(
        text_in, layout_in, q, k, v, first, weight, layout_w, tv, lv
    )
    span = text_in.shape[0]
    keep = (jnp.arange(span) < lengths[0]) & (dup_rows == 0)
    keep = keep.astype(F32)[:, None]
    text_final, grad_t, feed_vt, both_keep, both_send = feed(
        me,
        keep,
        norm_t,
        tv,
        text_cotangent,
        own + second_parts,
        dims,
        text_rows,
    )
    (
        layout_final,
        feed_vl,
        lu_grad,
        ld_grad,
        resid_t,
        resid_l,
        out_wt,
        out_wl,
        close_t,
        close_l,
        dout,
    ) = close_back_pair(
        keep,
        (norm_l, layout_cotangent, lu, ld),
        (grad_t, norm_t, inv_t, out_t),
        (inv_l, out_l),
        weight,
        layout_w,
        tv,
        lv,
    )
    backs = [
        heads_back(q, k, v, lse_a, dout, 0, middle), heads_back(q, k, v, lse_b, dout, middle, HEADS)
    ]
    joined_t, joined_l, keep_packed, send_packed = weight_grads(
        me,
        text_in,
        layout_in,
        backs,
        (out_wt, out_wl),
        (lu_grad, ld_grad),
        (close_t, close_l, feed_vt, feed_vl),
        dims,
        sizes,
    )
    text_input_grad, layout_input_grad = input_grads(
        joined_t, joined_l, resid_t, resid_l, weight, layout_w
    )
    both_sum = reduce_part(both_keep, both_send, dims, count)
    up_sum, down_sum = both_sum[:text_rows], both_sum[text_rows:]
    packed_sum = reduce_part(keep_packed, send_packed, dims, count)
    text_sum, layout_sums, text_vec_sum, layout_vec_sum = unpack_rows(
        packed_sum, text_rows, layout_rows, text_vec, layout_vec
    )
    return (
        text_final,
        layout_final,
        text_input_grad,
        layout_input_grad,
        text_sum,
        up_sum.T,
        down_sum,
        text_vec_sum,
        layout_sums[0],
        layout_sums[1].T,
        layout_sums[2],
        layout_vec_sum,
    )


def fits(shape):
    (_, nx), (_, ncore), (_, nz), (_, ny) = exchange_dims(shape)
    count = shape["gx"] * shape["gy"]
    return (
        (nx, ncore, ny, nz) == (2, 2, 2, 4)
        and (4 * D) % (16 * count) == 0
        and (4 * DL) % (8 * count) == 0
        and D % (4 * D // count) == 0
    )


def layer(fast, shape, *arrays):
    if not fast or arrays[2].shape[0] != 1:
        return shards(shape, *arrays)
    return shards_fast(shape, *arrays)


def solution(mesh):
    placed = (
        P(("gx", "gy"), None),
        P(("gx", "gy"), None),
        P(("gx", "gy")),
        P(("gx", "gy")),
        P(("gx", "gy"), None),
        P(None, ("gx", "gy")),
        P(("gx", "gy"), None),
        P(("gx", "gy")),
        P(("gx", "gy"), None),
        P(None, ("gx", "gy")),
        P(("gx", "gy"), None),
        P(("gx", "gy")),
        P(("gx", "gy"), None),
        P(("gx", "gy"), None),
    )
    shape = dict(mesh.shape)
    fast = fits(shape)
    return jax.shard_map(
        functools.partial(layer, fast, shape),
        mesh=mesh,
        in_specs=placed,
        out_specs=(
            P(("gx", "gy"), None),
            P(("gx", "gy"), None),
            P(("gx", "gy"), None),
            P(("gx", "gy"), None),
            P(("gx", "gy"), None),
            P(None, ("gx", "gy")),
            P(("gx", "gy"), None),
            P(("gx", "gy")),
            P(("gx", "gy"), None),
            P(None, ("gx", "gy")),
            P(("gx", "gy"), None),
            P(("gx", "gy")),
        ),
        check_vma=False,
    )
```
